32 devices in a mesh: dp: 16 (over z, y, x), tensor: 2 (over core).
Axes of the slice: x: 2, y: 2, z: 4, core: 2. Of those that a mesh axis runs over, the one named last changes fastest.
Arguments:
- tokens: bfloat16 [32768, 768], P(('dp', 'tensor')), may hold values from -6 to 6
- w_query: bfloat16 [768, 768], P('dp', 'tensor'), may hold values from -0.21875 to 0.21875
- w_key: bfloat16 [768, 768], P('dp', 'tensor'), may hold values from -0.21875 to 0.21875
- w_value: bfloat16 [768, 768], P('dp', 'tensor'), may hold values from -0.21875 to 0.21875
- w_out: bfloat16 [768, 768], P('tensor', 'dp'), may hold values from -3.5 to 3.5
- w_gate: bfloat16 [768, 2048], P('dp', 'tensor'), may hold values from -0.21875 to 0.21875
- w_up: bfloat16 [768, 2048], P('dp', 'tensor'), may hold values from -0.21875 to 0.21875
- w_down: bfloat16 [2048, 768], P('tensor', 'dp'), may hold values from -0.125 to 0.125
- gain_attn: float32 [768], replicated, may hold values from 0.5 to 1.5
- gain_ffn: float32 [768], replicated, may hold values from 0.5 to 1.5
- lengths: int32 [16, 3], P('dp'), may hold values from 0 to 2048, as said below
- cotangent: bfloat16 [32768, 768], P(('dp', 'tensor')), may hold values from -6 to 6
Outputs:
- output: bfloat16 [32768, 768], P(('dp', 'tensor'))
- input_grad: bfloat16 [32768, 768], P(('dp', 'tensor'))
- grad_query: float32 [768, 768], P('dp', 'tensor')
- grad_key: float32 [768, 768], P('dp', 'tensor')
- grad_value: float32 [768, 768], P('dp', 'tensor')
- grad_out: float32 [768, 768], P('tensor', 'dp')
- grad_gate: float32 [768, 2048], P('dp', 'tensor')
- grad_up: float32 [768, 2048], P('dp', 'tensor')
- grad_down: float32 [2048, 768], P('tensor', 'dp')
- grad_gain_attn: float32 [768], replicated
- grad_gain_ffn: float32 [768], replicated
The draws below stay inside these ranges and needn't reach their ends.
Inputs may be any that keep to these rules, and one draw needn't show every extreme that they name: `lengths`: each row holds one to 3 documents packed from the group's first slot, then zeros; a nonzero length is at least 512; a row sums to 2048 at most; some row holds one document of 2048 slots.
All inputs are finite; a program needn't handle non-finite values.
Results may differ from the reference program's by a relative error of at most 0.019.
Values may be sent and summed in bfloat16 or wider, within the bound.
No kernel may reach another device: no remote copies, remote signals or barrier semaphores. Data moves between devices by JAX's collectives and lax.ppermute only.
A program may use at most 256 MiB of HBM per device.

```python
from functools import partial
import jax
import jax.numpy as jnp
from jax import lax

D = 768
HEADS = 12
HEAD = 64
FF = 2048
DOCS = 3
GSLOT = 2048
GROUPS = 16
TOKENS = 32768


def draw_lengths(key, part):
    key_count, key_len, key_pick = jax.random.split(key, 3)
    count = jax.random.randint(key_count, (GROUPS,), 1, DOCS + 1).astype(jnp.int32)
    chosen = jax.random.randint(key_pick, (), 0, GROUPS).astype(jnp.int32)
    rows = jnp.arange(GROUPS, dtype=jnp.int32)
    count = jnp.where(rows == chosen, 1, count)
    upper = jnp.where(count == 1, GSLOT, jnp.where(count == 2, GSLOT // 2, GSLOT // 3)).astype(jnp.int32)
    lower = jnp.where(count == 1, GSLOT // 2, GSLOT // 4).astype(jnp.int32)
    raw = jax.random.randint(key_len, (GROUPS, DOCS), 0, 1 << 20).astype(jnp.int32)
    length = lower[:, None] + raw % (upper - lower + 1)[:, None]
    columns = jnp.arange(DOCS, dtype=jnp.int32)
    length = jnp.where((rows[:, None] == chosen) & (columns[None, :] == 0), GSLOT, length)
    length = jnp.where(columns[None, :] < count[:, None], length, 0)
    return length.astype(jnp.int32)


def block_levels(own_key, shape, pieces, low, largest):
    loudness = 1.0
    for axis_at, shards_of in pieces:
        heights = jax.random.uniform(jax.random.fold_in(jax.random.fold_in(own_key, 6), axis_at), (shards_of,), jnp.float32, low / len(pieces), largest / len(pieces))
        loudness = loudness * jnp.repeat(jnp.exp(heights), shape[axis_at] // shards_of).reshape((-1,) + (1,) * (len(shape) - 1 - axis_at))
    return loudness


def scatter_about(stream_key, shape, spread, limit, pieces=(), kind=jnp.bfloat16):
    drawn = jax.random.normal(stream_key, shape, jnp.float32) * spread
    if len(pieces) > 0:
        drawn = block_levels(stream_key, shape, pieces, -0.22, 0.18) * drawn
    return jnp.clip(drawn, min=-limit, max=limit).astype(kind)


def setup_inputs(seed: int = 0) -> dict:
    seeds = jax.random.split(jax.random.key(seed), 13)
    tokens = scatter_about(seeds[0], (TOKENS, D), 1.0, 6.0, ((0, 32),))
    w_query = scatter_about(seeds[1], (D, D), D ** -0.5, 0.21875, ((0, 16), (1, 2)))
    w_key = scatter_about(seeds[2], (D, D), D ** -0.5, 0.21875, ((0, 16), (1, 2)))
    w_value = scatter_about(seeds[3], (D, D), D ** -0.5, 0.21875, ((0, 16), (1, 2)))
    w_out = scatter_about(seeds[4], (D, D), (D * 8 // GSLOT) ** -0.5, 3.5, ((0, 2), (1, 16)))
    w_gate = scatter_about(seeds[5], (D, FF), D ** -0.5, 0.21875, ((0, 16), (1, 2)))
    w_up = scatter_about(seeds[6], (D, FF), D ** -0.5, 0.21875, ((0, 16), (1, 2)))
    w_down = scatter_about(seeds[7], (FF, D), FF ** -0.5, 0.125, ((0, 2), (1, 16)))
    gain_attn = jnp.clip(1.0 + 0.1 * jax.random.normal(seeds[8], (D,), jnp.float32), 0.5, 1.5)
    gain_ffn = jnp.clip(1.0 + 0.1 * jax.random.normal(seeds[9], (D,), jnp.float32), 0.5, 1.5)
    lengths = draw_lengths(jax.random.fold_in(seeds[12], 71), 0)
    cotangent = scatter_about(seeds[11], (TOKENS, D), 1.0, 6.0, ((0, 32),))
    return dict(tokens=tokens, w_query=w_query, w_key=w_key, w_value=w_value, w_out=w_out, w_gate=w_gate, w_up=w_up, w_down=w_down, gain_attn=gain_attn, gain_ffn=gain_ffn, lengths=lengths, cotangent=cotangent)


EPS = 1e-05
ROPE_BASE = 10000.0
NEGATIVE = -1e+30
HIGHEST = lax.Precision.HIGHEST

@jax.custom_vjp
def low(v):
    return lax.optimization_barrier(v.astype(jnp.bfloat16)).astype(jnp.float32)

@jax.custom_vjp
def low_back(v):
    return v

def low_keep(v):
    return (low(v), None)

def low_pass(kept, grad):
    return (grad,)

def back_keep(v):
    return (v, None)

def back_low(kept, grad):
    return (low(grad),)
low.defvjp(low_keep, low_pass)
low_back.defvjp(back_keep, back_low)

def layout(lengths_row, slots):
    index = jnp.arange(slots, dtype=jnp.int32)
    ends = jnp.cumsum(lengths_row.astype(jnp.int32)).astype(jnp.int32)
    passed = index[:, None] >= ends[None, :]
    segment_ids = lax.optimization_barrier(jnp.sum(passed.astype(jnp.int32), axis=1)).astype(jnp.int32)
    begins = lax.optimization_barrier(jnp.sum(jnp.where(passed, lengths_row.astype(jnp.int32)[None, :], 0), axis=1)).astype(jnp.int32)
    valid = index < ends[-1]
    return (jnp.where(valid, segment_ids, -1).astype(jnp.int32), (index - begins).astype(jnp.int32), valid, index)

def tables(position, head_size):
    half = head_size // 2
    inverse = ROPE_BASE ** (-(jnp.arange(half, dtype=jnp.float32) * 2.0 / head_size))
    angle = position.astype(jnp.float32)[:, None] * inverse[None, :]
    angle = jnp.concatenate([angle, angle], axis=1)
    return (jnp.cos(angle), jnp.sin(angle))

def rotate(values, cosine, sine):
    half = values.shape[-1] // 2
    turned = jnp.concatenate([-values[..., half:], values[..., :half]], axis=-1)
    return values * cosine[:, None, :] + turned * sine[:, None, :]

def norm_rows(values):
    return values * lax.rsqrt(lax.optimization_barrier(jnp.mean(values * values, axis=-1, keepdims=True)) + EPS)

def attend(item, keys, values, segment_ids, index):
    queries, seg_rows, valid_rows, index_rows = item
    raw = low_back(jnp.einsum('qhd,khd->hqk', queries, keys, precision=HIGHEST))
    scores = raw * HEAD ** (-0.5)
    allowed = (seg_rows[:, None] == segment_ids[None, :]) & (index[None, :] <= index_rows[:, None]) & valid_rows[:, None] | (index[None, :] == index_rows[:, None])
    scores = jnp.where(allowed[None], scores, NEGATIVE)
    peak = lax.optimization_barrier(jnp.max(scores, axis=-1, keepdims=True))
    expo = jnp.exp(scores - peak)
    probs = expo / lax.optimization_barrier(jnp.sum(expo, axis=-1, keepdims=True))
    return jnp.einsum('hqk,khd->qhd', low(probs), values, precision=HIGHEST)

def forward_group(tokens, w_query, w_key, w_value, w_out, w_gate, w_up, w_down, gain_attn, gain_ffn, segment_ids, position, valid, index):

    def matmul(left, right):
        return jnp.dot(left, right, precision=HIGHEST)
    slots = tokens.shape[0]
    cosine, sine = tables(position, HEAD)
    queries = low(rotate(low_back(matmul(tokens, w_query)).reshape(slots, HEADS, HEAD), cosine, sine))
    keys = low(rotate(low_back(matmul(tokens, w_key)).reshape(slots, HEADS, HEAD), cosine, sine))
    values = low(low_back(matmul(tokens, w_value))).reshape(slots, HEADS, HEAD)
    block = min(512, slots)
    blocks = slots // block
    items = (queries.reshape(blocks, block, HEADS, HEAD), segment_ids.reshape(blocks, block), valid.reshape(blocks, block), index.reshape(blocks, block))
    runner = jax.checkpoint(partial(attend, keys=keys, values=values, segment_ids=segment_ids, index=index))
    mixed = lax.map(runner, items).reshape(slots, D)
    mixed = low(low_back(mixed))
    attn = low_back(matmul(mixed, w_out))
    first = tokens + attn
    normed = norm_rows(first) * gain_attn
    normed_low = low(normed)
    gate = low_back(matmul(normed_low, w_gate))
    upper = low_back(matmul(normed_low, w_up))
    hidden = low(jax.nn.silu(gate) * upper)
    ffn = low_back(matmul(hidden, w_down))
    second = normed + ffn
    return jnp.where(valid[:, None], norm_rows(second) * gain_ffn, 0.0)

def reference(tokens, w_query, w_key, w_value, w_out, w_gate, w_up, w_down, gain_attn, gain_ffn, lengths, cotangent):
    params = tuple((weight.astype(jnp.float32) for weight in (w_query, w_key, w_value, w_out, w_gate, w_up, w_down, gain_attn, gain_ffn)))
    groups_x = tokens.astype(jnp.float32).reshape(GROUPS, GSLOT, D)
    groups_dy = cotangent.astype(jnp.float32).reshape(GROUPS, GSLOT, D)

    def step(carry, item):
        group_x, group_dy, lengths_row = item
        segment_ids, position, valid, index = layout(lengths_row, GSLOT)

        def run(x_in, *weights):
            return forward_group(x_in, *weights, segment_ids, position, valid, index)
        result, pull = jax.vjp(run, group_x, *params)
        grads = pull(group_dy)
        carry = tuple((total + grad for total, grad in zip(carry, grads[1:])))
        return (carry, (result.astype(jnp.bfloat16), grads[0].astype(jnp.bfloat16)))
    start = tuple((jnp.zeros_like(weight) for weight in params))
    totals, stacked = lax.scan(step, start, (groups_x, groups_dy, lengths))
    outputs, input_grads = stacked
    return (outputs.reshape(TOKENS, D), input_grads.reshape(TOKENS, D), totals[0], totals[1], totals[2], totals[3], totals[4], totals[5], totals[6], totals[7], totals[8])
```

```python
from functools import partial

import jax
import jax.numpy as jnp
from jax import lax
from jax.experimental import pallas as pl
from jax.experimental.pallas import tpu as pltpu
from jax.sharding import PartitionSpec as P

HEAD = 64
PAIR = 2 * HEAD
EPS = 1e-05
ROPE_BASE = 10000.0
NEGATIVE = -1e30
F32 = jnp.float32
BF16 = jnp.bfloat16
VMEM_LIMIT = 56 * 1024 * 1024


def mm(left, right):
    return jnp.dot(left, right, preferred_element_type=F32)


def rdot(left, right):
    return lax.dot_general(left, right, (((1,), (1,)), ((), ())), preferred_element_type=F32)


def tdot(left, right):
    return lax.dot_general(left, right, (((0,), (0,)), ((), ())), preferred_element_type=F32)


def params(limit=VMEM_LIMIT, dims=1):
    return pltpu.CompilerParams(
        vmem_limit_bytes=limit, dimension_semantics=("arbitrary",) * dims
    )


def cost(flops, nbytes, trans=0):
    return pl.CostEstimate(flops=int(flops), bytes_accessed=int(nbytes), transcendentals=int(trans))


def swap_halves(values):
    lane = lax.broadcasted_iota(jnp.int32, values.shape, 1) % HEAD
    half = HEAD // 2
    width = values.shape[1]
    return jnp.where(
        lane < half, pltpu.roll(values, width - half, 1), pltpu.roll(values, half, 1)
    )


def project_kernel(sched, own_ref, oth_ref, wq_ref, wk_ref, wv_ref, cos_ref, sin_ref,
                   q_ref, k_ref, v_ref, vt_ref, *, half):
    step = pl.program_id(0)
    x = jnp.where(step < half, own_ref[...], oth_ref[...])
    cosine, sine = cos_ref[...], sin_ref[...]
    width = wq_ref.shape[1]
    for w_ref, out_ref, scale in ((wq_ref, q_ref, HEAD ** -0.5), (wk_ref, k_ref, 1.0)):
        u = mm(x, w_ref[...])
        for at in range(0, width, PAIR):
            piece = u[:, at:at + PAIR]
            turned = piece * cosine + swap_halves(piece) * sine
            out_ref[:, at:at + PAIR] = (turned * scale).astype(BF16)
    v = mm(x, wv_ref[...])
    v_ref[...] = v.astype(BF16)
    vt_ref[...] = v.T.astype(BF16)


def project(sched, own, oth, wq, wk, wv, cosine, sine, block):
    rows, width = own.shape[0], own.shape[1]
    slots = 2 * rows
    half = rows // block
    cols = wq.shape[1]

    def place(step, sched):
        return lax.rem(step + sched[0] * half, 2 * half)

    weight = pl.BlockSpec((width, cols), lambda s, sched: (0, 0))
    table = pl.BlockSpec((block, PAIR), lambda s, sched: (place(s, sched), 0))
    out = pl.BlockSpec((block, cols), lambda s, sched: (place(s, sched), 0))
    return pl.pallas_call(
        partial(project_kernel, half=half),
        grid_spec=pltpu.PrefetchScalarGridSpec(
            num_scalar_prefetch=1,
            grid=(2 * half,),
            in_specs=[
                pl.BlockSpec((block, width), lambda s, sched: (jnp.minimum(s, half - 1), 0)),
                pl.BlockSpec((block, width), lambda s, sched: (jnp.maximum(s - half, 0), 0)),
                weight, weight, weight, table, table,
            ],
            out_specs=[out, out, out,
                       pl.BlockSpec((cols, block), lambda s, sched: (0, place(s, sched)))],
        ),
        out_shape=[jax.ShapeDtypeStruct((slots, cols), BF16)] * 3
        + [jax.ShapeDtypeStruct((cols, slots), BF16)],
        compiler_params=params(),
        cost_estimate=cost(6 * slots * width * cols, 14 * slots * cols),
        name="project",
    )(sched, own, oth, wq, wk, wv, cosine, sine)


def head_masks(values):
    lane = lax.broadcasted_iota(jnp.int32, (1, PAIR), 1)
    low = (lane < HEAD).astype(values.dtype)
    return (values * low, values * (1 - low))


def allowed_block(start, key_at, query_at, bk, bq):
    key_index = key_at + lax.broadcasted_iota(jnp.int32, (bk, bq), 0)
    query_index = query_at + lax.broadcasted_iota(jnp.int32, (bk, bq), 1)
    return (key_index >= start) & (key_index <= query_index)


def forward_kernel(sched, q_ref, k_ref, vt_ref, start_ref, oth_ref, own_ref, lse_ref, acc_ref,
                   *, bq, bk, blocks):
    step = pl.program_id(1)
    half = blocks // 2
    i = lax.rem(step + (1 - sched[0]) * half, blocks)
    queries = head_masks(q_ref[...])
    start = start_ref[...]
    ratio = bq // bk
    acc_ref[...] = jnp.zeros_like(acc_ref)

    def visit(j, carry, masked):
        at = pl.multiple_of(j * bk, bk)
        keys = k_ref[pl.ds(at, bk), :]
        if masked:
            allowed = allowed_block(start, at, i * bq, bk, bq)
        out = []
        for h in range(2):
            peak, total = carry[2 * h], carry[2 * h + 1]
            scores = rdot(keys, queries[h])
            if masked:
                scores = jnp.where(allowed, scores, NEGATIVE)
            new_peak = jnp.maximum(peak, jnp.max(scores, axis=0, keepdims=True))
            fade = jnp.exp(peak - new_peak)
            expo = jnp.exp(scores - new_peak)
            total = total * fade + jnp.sum(expo, axis=0, keepdims=True)
            rows = pl.ds(h * HEAD, HEAD)
            acc_ref[rows, :] = acc_ref[rows, :] * fade + mm(
                vt_ref[rows, pl.ds(at, bk)], expo.astype(BF16)
            )
            out += [new_peak, total]
        return tuple(out)

    low = sched[2 + i]
    mid = jnp.minimum(sched[2 + blocks + i], i * ratio)
    carry = (jnp.full((1, bq), NEGATIVE, F32), jnp.zeros((1, bq), F32)) * 2
    carry = lax.fori_loop(low, mid, lambda j, c: visit(j, c, True), carry)
    carry = lax.fori_loop(jnp.maximum(low, mid), i * ratio, lambda j, c: visit(j, c, False), carry)
    for d in range(ratio):
        carry = visit(i * ratio + d, carry, True)
    result = []
    for h in range(2):
        peak, total = carry[2 * h], carry[2 * h + 1]
        result.append(acc_ref[h * HEAD:(h + 1) * HEAD, :] / total)
        lse_ref[h:h + 1, :] = peak + jnp.log(total)
    mixed = jnp.concatenate(result, axis=0).T.astype(BF16)

    @pl.when(step < half)
    def _():
        oth_ref[...] = mixed

    @pl.when(step >= half)
    def _():
        own_ref[...] = mixed


def attend_forward(sched, q, k, vt, start, bq, bk):
    slots, cols = q.shape
    pairs, blocks = cols // PAIR, slots // bq
    half = blocks // 2

    def place(n, sched):
        return lax.rem(n + (1 - sched[0]) * half, blocks)

    return pl.pallas_call(
        partial(forward_kernel, bq=bq, bk=bk, blocks=blocks),
        grid_spec=pltpu.PrefetchScalarGridSpec(
            num_scalar_prefetch=1,
            grid=(pairs, blocks),
            in_specs=[
                pl.BlockSpec((bq, PAIR), lambda p, n, s: (place(n, s), p)),
                pl.BlockSpec((slots, PAIR), lambda p, n, s: (0, p)),
                pl.BlockSpec((PAIR, slots), lambda p, n, s: (p, 0)),
                pl.BlockSpec((1, bq), lambda p, n, s: (0, place(n, s))),
            ],
            out_specs=[
                pl.BlockSpec((bq, PAIR), lambda p, n, s: (jnp.minimum(n, half - 1), p)),
                pl.BlockSpec((bq, PAIR), lambda p, n, s: (jnp.maximum(n - half, 0), p)),
                pl.BlockSpec((None, 2, bq), lambda p, n, s: (p, 0, place(n, s))),
            ],
            scratch_shapes=[pltpu.VMEM((PAIR, bq), F32)],
        ),
        out_shape=[
            jax.ShapeDtypeStruct((slots // 2, cols), BF16),
            jax.ShapeDtypeStruct((slots // 2, cols), BF16),
            jax.ShapeDtypeStruct((pairs, 2, slots), F32),
        ],
        compiler_params=params(dims=2),
        cost_estimate=cost(2 * slots * slots * cols * 2, 8 * slots * cols, slots * slots * 6),
        name="attend_forward",
    )(sched, q, k, vt, start)


def backward_kernel(sched, q_ref, k_ref, v_ref, cos_ref, sin_ref, start_ref, lse_ref,
                    o_oth_ref, o_own_ref, g_oth_ref, g_own_ref,
                    dq_ref, dk_ref, dv_ref, kt_ref, dqt_ref, dk_acc, dv_acc, *, bq, bk, blocks):
    step = pl.program_id(1)
    half = blocks // 2
    i = lax.rem(step + (1 - sched[0]) * half, blocks)
    ratio = bq // bk

    @pl.when(step == 0)
    def _():
        kt_ref[...] = k_ref[...].astype(F32).T.astype(BF16)
        dk_acc[...] = jnp.zeros_like(dk_acc)
        dv_acc[...] = jnp.zeros_like(dv_acc)

    first = step < half
    grads = jnp.where(first, g_oth_ref[...], g_own_ref[...])
    mixed = jnp.where(first, o_oth_ref[...], o_own_ref[...])
    queries = head_masks(q_ref[...])
    couts = head_masks(grads)
    start = start_ref[...]
    product = grads.astype(F32) * mixed.astype(F32)
    big = product.astype(BF16)
    small = (product - big.astype(F32)).astype(BF16)
    row = lax.broadcasted_iota(jnp.int32, (16, PAIR), 0)
    lane = lax.broadcasted_iota(jnp.int32, (16, PAIR), 1)
    pick = jnp.where(lane // HEAD == row, 1.0, 0.0).astype(BF16)
    inner = rdot(pick, big) + rdot(pick, small)
    lse = lse_ref[...]
    dqt_ref[...] = jnp.zeros_like(dqt_ref)

    def visit(j, masked):
        at = pl.multiple_of(j * bk, bk)
        where = pl.ds(at, bk)
        keys, values = k_ref[where, :], v_ref[where, :]
        if masked:
            allowed = allowed_block(start, at, i * bq, bk, bq)
        dk_part, dv_part = [], []
        for h in range(2):
            rows = pl.ds(h * HEAD, HEAD)
            probs = jnp.exp(rdot(keys, queries[h]) - lse[h:h + 1, :])
            if masked:
                probs = jnp.where(allowed, probs, 0.0)
            d_probs = rdot(values, couts[h])
            d_scores = (probs * (d_probs - inner[h:h + 1, :])).astype(BF16)
            dv_part.append(mm(probs.astype(BF16), couts[h]))
            dk_part.append(mm(d_scores, queries[h]))
            dqt_ref[rows, :] += mm(kt_ref[rows, where], d_scores)
        dk_acc[where, :] += dk_part[0] + dk_part[1]
        dv_acc[where, :] += dv_part[0] + dv_part[1]

    low = sched[2 + i]
    mid = jnp.minimum(sched[2 + blocks + i], i * ratio)

    @pl.loop(low, mid)
    def _(j):
        visit(j, True)

    @pl.loop(jnp.maximum(low, mid), i * ratio)
    def _(j):
        visit(j, False)

    for d in range(ratio):
        visit(i * ratio + d, True)

    def unrotate(g, cosine, sine):
        return g * cosine - swap_halves(g) * sine

    here = pl.ds(pl.multiple_of(i * bq, bq), bq)
    dq = dqt_ref[...].T * (HEAD ** -0.5)
    dq_ref[...] = unrotate(dq, cos_ref[here, :], sin_ref[here, :]).astype(BF16)

    @pl.when(step == blocks - 1)
    def _():
        dk_ref[...] = unrotate(dk_acc[...], cos_ref[...], sin_ref[...]).astype(BF16)
        dv_ref[...] = dv_acc[...].astype(BF16)


def attend_backward(sched, q, k, v, cosine, sine, start, lse, o_oth, o_own, g_oth, g_own, bq, bk):
    slots, cols = q.shape
    pairs, blocks = cols // PAIR, slots // bq
    half = blocks // 2

    def place(n, sched):
        return lax.rem(n + (1 - sched[0]) * half, blocks)

    whole = pl.BlockSpec((slots, PAIR), lambda p, n, s: (0, p))
    table = pl.BlockSpec((slots, PAIR), lambda p, n, s: (0, 0))
    oth = pl.BlockSpec((bq, PAIR), lambda p, n, s: (jnp.minimum(n, half - 1), p))
    own = pl.BlockSpec((bq, PAIR), lambda p, n, s: (jnp.maximum(n - half, 0), p))
    query = pl.BlockSpec((bq, PAIR), lambda p, n, s: (place(n, s), p))
    return pl.pallas_call(
        partial(backward_kernel, bq=bq, bk=bk, blocks=blocks),
        grid_spec=pltpu.PrefetchScalarGridSpec(
            num_scalar_prefetch=1,
            grid=(pairs, blocks),
            in_specs=[
                query, whole, whole, table, table,
                pl.BlockSpec((1, bq), lambda p, n, s: (0, place(n, s))),
                pl.BlockSpec((None, 2, bq), lambda p, n, s: (p, 0, place(n, s))),
                oth, own, oth, own,
            ],
            out_specs=[query, whole, whole],
            scratch_shapes=[
                pltpu.VMEM((PAIR, slots), BF16),
                pltpu.VMEM((PAIR, bq), F32),
                pltpu.VMEM((slots, PAIR), F32),
                pltpu.VMEM((slots, PAIR), F32),
            ],
        ),
        out_shape=[jax.ShapeDtypeStruct((slots, cols), BF16)] * 3,
        compiler_params=params(dims=2),
        cost_estimate=cost(5 * slots * slots * cols * 2, 20 * slots * cols, slots * slots * 6),
        name="attend_backward",
    )(sched, q, k, v, cosine, sine, start, lse, o_oth, o_own, g_oth, g_own)


def feed_kernel(sched, x_ref, own_ref, oth_ref, dy_ref, w_ref, ga_ref, gf_ref,
                out_ref, dfirst_ref, gown_ref, goth_ref, normed_ref, dffn_ref, dattn_ref,
                hidden_ref, dgate_ref, dup_ref, gains_ref,
                gate_s, up_s, sig_s, *, block, local, hid, head_cols):
    step = pl.program_id(0)
    me = sched[0]
    out_at = 3 * hid
    outs = slice(out_at, out_at + head_cols)
    x = x_ref[...].astype(F32)
    attn = rdot(own_ref[...], w_ref[me, :, outs]) + rdot(oth_ref[...], w_ref[1 - me, :, outs])
    first = x + attn
    rms1 = lax.rsqrt(jnp.mean(first * first, axis=-1, keepdims=True) + EPS)
    unit1 = first * rms1
    normed = unit1 * ga_ref[...]
    normed_b = normed.astype(BF16)
    normed_ref[...] = normed_b
    ffn = None
    for t in range(2):
        cols = slice(t * hid, (t + 1) * hid)
        gate = mm(normed_b, w_ref[t, :, 0:hid])
        upper = mm(normed_b, w_ref[t, :, hid:2 * hid])
        sigma = 1.0 / (1.0 + jnp.exp(-gate))
        hidden = (gate * sigma * upper).astype(BF16)
        gate_s[:, cols] = gate
        up_s[:, cols] = upper
        sig_s[:, cols] = sigma
        hidden_ref[:, cols] = hidden
        part = rdot(hidden, w_ref[t, :, 2 * hid:3 * hid])
        ffn = part if ffn is None else ffn + part
    second = normed + ffn
    rms2 = lax.rsqrt(jnp.mean(second * second, axis=-1, keepdims=True) + EPS)
    unit2 = second * rms2
    slot = me * local + step * block + lax.broadcasted_iota(jnp.int32, (block, 1), 0)
    valid = slot < sched[1]
    out_ref[...] = jnp.where(valid, unit2 * gf_ref[...], 0.0).astype(BF16)
    dy = jnp.where(valid, dy_ref[...].astype(F32), 0.0)
    gain_ffn = jnp.sum(dy * unit2, axis=0, keepdims=True)
    scaled = dy * gf_ref[...]
    d_second = rms2 * (scaled - unit2 * jnp.mean(scaled * unit2, axis=-1, keepdims=True))
    d_ffn = d_second.astype(BF16)
    dffn_ref[...] = d_ffn
    d_normed = d_second
    for t in range(2):
        cols = slice(t * hid, (t + 1) * hid)
        d_hidden = mm(d_ffn, w_ref[t, :, 2 * hid:3 * hid])
        gate, sigma = gate_s[:, cols], sig_s[:, cols]
        slope = d_hidden * sigma
        d_gate = (slope * up_s[:, cols] * (1.0 + gate * (1.0 - sigma))).astype(BF16)
        d_up = (slope * gate).astype(BF16)
        dgate_ref[:, cols] = d_gate
        dup_ref[:, cols] = d_up
        d_normed = d_normed + rdot(d_gate, w_ref[t, :, 0:hid]) + rdot(d_up, w_ref[t, :, hid:2 * hid])
    gain_attn = jnp.sum(d_normed * unit1, axis=0, keepdims=True)
    scaled = d_normed * ga_ref[...]
    d_first = rms1 * (scaled - unit1 * jnp.mean(scaled * unit1, axis=-1, keepdims=True))
    dfirst_ref[...] = d_first
    d_attn = d_first.astype(BF16)
    dattn_ref[...] = d_attn
    gown_ref[...] = mm(d_attn, w_ref[me, :, outs]).astype(BF16)
    goth_ref[...] = mm(d_attn, w_ref[1 - me, :, outs]).astype(BF16)

    @pl.when(step == 0)
    def _():
        gains_ref[...] = jnp.zeros_like(gains_ref)

    gains_ref[0:1, :] += gain_attn
    gains_ref[1:2, :] += gain_ffn


def feed(sched, x, own, oth, dy, weights, gain_attn, gain_ffn, hid, block):
    local, width = x.shape
    head_cols = own.shape[1]
    rows = pl.BlockSpec((block, width), lambda s, sched: (s, 0))
    heads = pl.BlockSpec((block, head_cols), lambda s, sched: (s, 0))
    wide = pl.BlockSpec((block, 2 * hid), lambda s, sched: (s, 0))
    gain = pl.BlockSpec((1, width), lambda s, sched: (0, 0))
    full = pl.BlockSpec(weights.shape, lambda s, sched: (0, 0, 0), pipeline_mode=pl.Buffered(1))

    def shape(cols, dtype):
        return jax.ShapeDtypeStruct((local, cols), dtype)

    return pl.pallas_call(
        partial(feed_kernel, block=block, local=local, hid=hid, head_cols=head_cols),
        grid_spec=pltpu.PrefetchScalarGridSpec(
            num_scalar_prefetch=1,
            grid=(local // block,),
            in_specs=[rows, heads, heads, rows, full, gain, gain],
            out_specs=[rows, rows, heads, heads, rows, rows, rows, wide, wide, wide,
                       pl.BlockSpec((8, width), lambda s, sched: (0, 0))],
            scratch_shapes=[pltpu.VMEM((block, 2 * hid), F32)] * 3,
        ),
        out_shape=[
            shape(width, BF16), shape(width, F32), shape(head_cols, BF16), shape(head_cols, BF16),
            shape(width, BF16), shape(width, BF16), shape(width, BF16),
            shape(2 * hid, BF16), shape(2 * hid, BF16), shape(2 * hid, BF16),
            jax.ShapeDtypeStruct((8, width), F32),
        ],
        compiler_params=params(),
        cost_estimate=cost(8 * local * width * (3 * hid + head_cols) , 30 * local * width),
        name="feed",
    )(sched, x, own, oth, dy, weights, gain_attn, gain_ffn)


def weight_grad_kernel(sched, normed_ref, dffn_ref, dattn_ref, hidden_ref, dgate_ref, dup_ref,
                       own_ref, oth_ref, out_ref, *, hid):
    t = pl.program_id(0)
    normed, d_ffn = normed_ref[...], dffn_ref[...]
    out_ref[0, :, 0:hid] = tdot(normed, dgate_ref[...]).astype(BF16)
    out_ref[0, :, hid:2 * hid] = tdot(normed, dup_ref[...]).astype(BF16)
    out_ref[0, :, 2 * hid:3 * hid] = tdot(d_ffn, hidden_ref[...]).astype(BF16)
    mixed = jnp.where(t == sched[0], own_ref[...], oth_ref[...])
    out_ref[0, :, 3 * hid:] = tdot(dattn_ref[...], mixed).astype(BF16)


def weight_grads(sched, normed, d_ffn, d_attn, hidden, d_gate, d_up, own, oth, hid):
    local, width = normed.shape
    head_cols = own.shape[1]
    total = 3 * hid + head_cols
    rows = pl.BlockSpec((local, width), lambda t, sched: (0, 0))
    heads = pl.BlockSpec((local, head_cols), lambda t, sched: (0, 0))
    wide = pl.BlockSpec((local, hid), lambda t, sched: (0, t))
    return pl.pallas_call(
        partial(weight_grad_kernel, hid=hid),
        grid_spec=pltpu.PrefetchScalarGridSpec(
            num_scalar_prefetch=1,
            grid=(2,),
            in_specs=[rows, rows, rows, wide, wide, wide, heads, heads],
            out_specs=pl.BlockSpec((1, width, total), lambda t, sched: (t, 0, 0)),
        ),
        out_shape=jax.ShapeDtypeStruct((2, width, total), BF16),
        compiler_params=params(),
        cost_estimate=cost(4 * local * width * total, 8 * local * total),
        name="weight_grads",
    )(sched, normed, d_ffn, d_attn, hidden, d_gate, d_up, own, oth)


def input_weight_kernel(sched, own_ref, oth_ref, dq_ref, dk_ref, dv_ref, out_ref, *, local):
    me = sched[0]
    here = pl.ds(pl.multiple_of(me * local, local), local)
    there = pl.ds(pl.multiple_of((1 - me) * local, local), local)
    cols = dq_ref.shape[1]
    for at, ref in enumerate((dq_ref, dk_ref, dv_ref)):
        part = tdot(own_ref[...], ref[here, :]) + tdot(oth_ref[...], ref[there, :])
        out_ref[:, at * cols:(at + 1) * cols] = part.astype(BF16)


def input_weight_grads(sched, own, oth, dq, dk, dv, block=256):
    local, width = own.shape
    slots, cols = dq.shape
    rows = pl.BlockSpec((local, block), lambda s, sched: (0, s))
    full = pl.BlockSpec((slots, cols), lambda s, sched: (0, 0))
    return pl.pallas_call(
        partial(input_weight_kernel, local=local),
        grid_spec=pltpu.PrefetchScalarGridSpec(
            num_scalar_prefetch=1,
            grid=(width // block,),
            in_specs=[rows, rows, full, full, full],
            out_specs=pl.BlockSpec((block, 3 * cols), lambda s, sched: (s, 0)),
        ),
        out_shape=jax.ShapeDtypeStruct((width, 3 * cols), BF16),
        compiler_params=params(),
        cost_estimate=cost(6 * slots * width * cols, 6 * slots * cols),
        name="input_weight_grads",
    )(sched, own, oth, dq, dk, dv)


def input_grad_kernel(sched, dq_ref, dk_ref, dv_ref, wq_ref, wk_ref, wv_ref, dfirst_ref,
                      oth_ref, own_ref, *, half):
    step = pl.program_id(0)
    part = (rdot(dq_ref[...], wq_ref[...]) + rdot(dk_ref[...], wk_ref[...])
            + rdot(dv_ref[...], wv_ref[...]))

    @pl.when(step < half)
    def _():
        oth_ref[...] = part.astype(BF16)

    @pl.when(step >= half)
    def _():
        own_ref[...] = dfirst_ref[...] + part


def input_grads(sched, dq, dk, dv, wq, wk, wv, d_first, block):
    local, width = d_first.shape
    cols = dq.shape[1]
    half = local // block

    def place(n, sched):
        return lax.rem(n + (1 - sched[0]) * half, 2 * half)

    heads = pl.BlockSpec((block, cols), lambda n, s: (place(n, s), 0))
    weight = pl.BlockSpec((width, cols), lambda n, s: (0, 0))
    own = pl.BlockSpec((block, width), lambda n, s: (jnp.maximum(n - half, 0), 0))
    return pl.pallas_call(
        partial(input_grad_kernel, half=half),
        grid_spec=pltpu.PrefetchScalarGridSpec(
            num_scalar_prefetch=1,
            grid=(2 * half,),
            in_specs=[heads, heads, heads, weight, weight, weight, own],
            out_specs=[pl.BlockSpec((block, width), lambda n, s: (jnp.minimum(n, half - 1), 0)), own],
        ),
        out_shape=[jax.ShapeDtypeStruct((local, width), BF16),
                   jax.ShapeDtypeStruct((local, width), F32)],
        compiler_params=params(),
        cost_estimate=cost(12 * local * width * cols, 12 * local * width),
        name="input_grads",
    )(sched, dq, dk, dv, wq, wk, wv, d_first)


def exchange(value):
    return lax.ppermute(value, "tensor", [(0, 1), (1, 0)])


def flip(value, bit):
    count = lax.axis_size("dp")
    return lax.ppermute(value, "dp", [(at, at ^ (1 << bit)) for at in range(count)])


def bit_orders(count):
    bits = count.bit_length() - 1
    low = list(range(min(2, bits)))
    high = list(range(min(2, bits), bits))
    return high + low, high + low[::-1]


def gather_rows(piece, order):
    me = lax.axis_index("dp")
    rows, cols = piece.shape
    held = piece[None]
    for bit in order:
        other = flip(held, bit)
        mine = ((me >> bit) & 1) == 0
        held = jnp.stack([jnp.where(mine, held, other), jnp.where(mine, other, held)])
    bits = len(order)
    held = held.reshape((2,) * bits + (rows, cols))
    axes = [bits - 1 - order.index(bit) for bit in range(bits - 1, -1, -1)]
    return held.transpose(*axes, bits, bits + 1).reshape(-1, cols)


def scatter_rows(total, order):
    me = lax.axis_index("dp")
    bits = len(order)
    rows, cols = total.shape[0] >> bits, total.shape[1]
    held = total.reshape((2,) * bits + (rows, cols))
    left = list(range(bits - 1, -1, -1))
    for bit in order:
        axis = left.index(bit)
        left.pop(axis)
        low = lax.index_in_dim(held, 0, axis, keepdims=False)
        high = lax.index_in_dim(held, 1, axis, keepdims=False)
        mine = ((me >> bit) & 1) == 0
        got = flip(jnp.where(mine, high, low), bit)
        held = (jnp.where(mine, low, high).astype(F32) + got.astype(F32)).astype(BF16)
    return held.reshape(rows, cols)


def sum_everywhere(value):
    value = value + exchange(value)
    for bit in range(lax.axis_size("dp").bit_length() - 1):
        value = value + flip(value, bit)
    return value


def local(tokens, w_query, w_key, w_value, w_out, w_gate, w_up, w_down, gain_attn, gain_ffn,
          lengths, cotangent):
    rows, width = tokens.shape
    slots = 2 * rows
    me = lax.axis_index("tensor")
    count = lax.axis_size("dp")
    cols, hid = w_query.shape[1], w_gate.shape[1]
    share = width // count
    bq = bk = 512
    blocks = slots // bq

    packed = jnp.concatenate([w_gate, w_up, w_down.T, w_out.T], axis=1)
    feed_w = lax.all_gather(packed, ("tensor", "dp"), axis=0, tiled=True)
    feed_w = feed_w.reshape(2, width, packed.shape[1])
    fore, back = bit_orders(count)
    full_q = gather_rows(w_query, fore)
    full_k = gather_rows(w_key, back)
    full_v = gather_rows(w_value, fore)
    other_x = exchange(tokens)

    index = jnp.arange(slots, dtype=jnp.int32)
    row = lengths[0]
    ends = jnp.cumsum(row)
    begins = jnp.sum(jnp.where(index[:, None] >= ends[None, :], row[None, :], 0), axis=1)
    position = (index - begins).astype(F32)
    lane = jnp.arange(PAIR, dtype=jnp.int32) % HEAD
    inverse = ROPE_BASE ** (-((lane % (HEAD // 2)).astype(F32) * 2.0 / HEAD))
    angle = position[:, None] * inverse[None, :]
    cosine = jnp.cos(angle)
    sine = jnp.where(lane[None, :] < HEAD // 2, -jnp.sin(angle), jnp.sin(angle))
    block_begin = begins.reshape(blocks, bq)
    sched = jnp.concatenate([
        jnp.stack([me.astype(jnp.int32), ends[-1]]),
        block_begin[:, 0] // bk,
        (block_begin[:, -1] + bk - 1) // bk,
    ])
    start = begins.reshape(1, slots)

    q, k, v, vt = project(sched, tokens, other_x, full_q, full_k, full_v, cosine, sine, 512)
    mixed_send, mixed_own, lse = attend_forward(sched, q, k, vt, start, bq, bk)
    mixed_oth = exchange(mixed_send)
    (output, d_first, g_own, g_send, normed, d_ffn, d_attn, hidden, d_gate, d_up,
     gains) = feed(sched, tokens, mixed_own, mixed_oth, cotangent, feed_w,
                   gain_attn.reshape(1, width), gain_ffn.reshape(1, width), hid, 256)
    g_oth = exchange(g_send)
    grads = weight_grads(sched, normed, d_ffn, d_attn, hidden, d_gate, d_up,
                         mixed_own, mixed_oth, hid)
    reduced = lax.psum_scatter(grads.reshape(2 * width, grads.shape[2]), ("tensor", "dp"),
                               scatter_dimension=0, tiled=True).astype(F32)
    gains = sum_everywhere(gains)
    dq, dk, dv = attend_backward(sched, q, k, v, cosine, sine, start, lse,
                                 mixed_send, mixed_own, g_oth, g_own, bq, bk)
    qkv = input_weight_grads(sched, tokens, other_x, dq, dk, dv)
    fore, back = bit_orders(count)
    edge = 3 * cols // 2
    qkv = jnp.concatenate([scatter_rows(qkv[:, :edge], fore[::-1]),
                           scatter_rows(qkv[:, edge:], back[::-1])], axis=1).astype(F32)
    x_send, x_own = input_grads(sched, dq, dk, dv, full_q, full_k, full_v, d_first, 512)
    input_grad = (x_own + exchange(x_send).astype(F32)).astype(BF16)
    return (
        output,
        input_grad,
        qkv[:, :cols],
        qkv[:, cols:2 * cols],
        qkv[:, 2 * cols:],
        reduced[:, 3 * hid:].T,
        reduced[:, :hid],
        reduced[:, hid:2 * hid],
        reduced[:, 2 * hid:3 * hid].T,
        gains[0],
        gains[1],
    )


def solution(mesh):
    split = P("dp", "tensor")
    turned = P("tensor", "dp")
    slots = P(("dp", "tensor"), None)
    return jax.shard_map(
        local,
        mesh=mesh,
        in_specs=(slots, split, split, split, turned, split, split, turned, P(), P(),
                  P("dp", None), slots),
        out_specs=(slots, slots, split, split, split, turned, split, split, turned, P(), P()),
        check_vma=False,
    )
```

```python
from functools import partial

import jax
import jax.numpy as jnp
from jax import lax
from jax.experimental import pallas as pl
from jax.experimental.pallas import tpu as pltpu
from jax.sharding import Mesh
from jax.sharding import PartitionSpec as P

HEAD = 64
PAIR = 2 * HEAD
EPS = 1e-05
ROPE_BASE = 10000.0
NEGATIVE = -1e30
F32 = jnp.float32
BF16 = jnp.bfloat16
VMEM_LIMIT = 56 * 1024 * 1024
DP = ("far", "near")


def mm(left, right):
    return jnp.dot(left, right, preferred_element_type=F32)


def rdot(left, right):
    return lax.dot_general(left, right, (((1,), (1,)), ((), ())), preferred_element_type=F32)


def tdot(left, right):
    return lax.dot_general(left, right, (((0,), (0,)), ((), ())), preferred_element_type=F32)


def params(limit=VMEM_LIMIT, dims=1):
    return pltpu.CompilerParams(
        vmem_limit_bytes=limit, dimension_semantics=("arbitrary",) * dims
    )


def cost(flops, nbytes, trans=0):
    return pl.CostEstimate(flops=int(flops), bytes_accessed=int(nbytes), transcendentals=int(trans))


def swap_halves(values):
    lane = lax.broadcasted_iota(jnp.int32, values.shape, 1) % HEAD
    half = HEAD // 2
    width = values.shape[1]
    return jnp.where(
        lane < half, pltpu.roll(values, width - half, 1), pltpu.roll(values, half, 1)
    )


def head_masks(values):
    lane = lax.broadcasted_iota(jnp.int32, (1, PAIR), 1)
    low = (lane < HEAD).astype(values.dtype)
    return (values * low, values * (1 - low))


def forward_kernel(sched, own_x_ref, oth_x_ref, wq_ref, wk_ref, wv_ref, cos_ref, sin_ref, start_ref,
                   qkv_ref, oth_ref, own_ref, lse_ref, acc_ref, vt_ref, *, bq, bk, sub, chunk, blocks):
    step = pl.program_id(1)
    half = blocks // 2
    i = lax.rem(step + (1 - sched[0]) * half, blocks)

    @pl.when(step == 0)
    def _():
        local = own_x_ref.shape[0]
        weights = jnp.concatenate([wq_ref[...], wk_ref[...], wv_ref[...]], axis=1)
        for x_ref, side in ((own_x_ref, sched[0]), (oth_x_ref, 1 - sched[0])):
            for r in range(0, local, chunk):
                at = pl.multiple_of(side * local + r, chunk)
                here = pl.ds(at, chunk)
                u = mm(x_ref[r:r + chunk, :], weights)
                cosine, sine = cos_ref[here, :], sin_ref[here, :]
                for n, scale in ((0, HEAD ** -0.5), (1, 1.0)):
                    piece = u[:, n * PAIR:(n + 1) * PAIR]
                    turned = piece * cosine + swap_halves(piece) * sine
                    qkv_ref[here, n * PAIR:(n + 1) * PAIR] = (turned * scale).astype(BF16)
                v = u[:, 2 * PAIR:]
                qkv_ref[here, 2 * PAIR:] = v.astype(BF16)
                vt_ref[:, here] = v.T.astype(BF16)

    queries = head_masks(qkv_ref[pl.ds(pl.multiple_of(i * bq, bq), bq), 0:PAIR])
    start = start_ref[...]
    acc_ref[...] = jnp.zeros_like(acc_ref)
    streams = [(h, c) for h in range(2) for c in range(0, bq, sub)]

    def visit(j, carry, masked, last):
        at = pl.multiple_of(i * bq if last else j * bk, bk)
        scores, out = [], []
        for h, c in streams:
            size = c + sub if last else bk
            s = rdot(qkv_ref[pl.ds(at, size), PAIR:2 * PAIR], queries[h][c:c + sub])
            if masked:
                key_index = at + lax.broadcasted_iota(jnp.int32, (size, sub), 0)
                query_index = i * bq + c + lax.broadcasted_iota(jnp.int32, (size, sub), 1)
                allowed = (key_index >= start[:, c:c + sub]) & (key_index <= query_index)
                s = jnp.where(allowed, s, NEGATIVE)
            scores.append(s)
        for n, (h, c) in enumerate(streams):
            size = c + sub if last else bk
            peak, total = carry[2 * n], carry[2 * n + 1]
            new_peak = jnp.maximum(peak, jnp.max(scores[n], axis=0, keepdims=True))
            fade = jnp.exp(peak - new_peak)
            expo = jnp.exp(scores[n] - new_peak)
            total = total * fade + jnp.sum(expo, axis=0, keepdims=True)
            rows, cols = pl.ds(h * HEAD, HEAD), slice(c, c + sub)
            acc_ref[rows, cols] = acc_ref[rows, cols] * fade + mm(
                vt_ref[rows, pl.ds(at, size)], expo.astype(BF16)
            )
            out += [new_peak, total]
        return tuple(out)

    low = sched[2 + i]
    top = i * (bq // bk)
    mid = jnp.minimum(sched[2 + blocks + i], top)
    carry = (jnp.full((1, sub), NEGATIVE, F32), jnp.zeros((1, sub), F32)) * len(streams)
    carry = lax.fori_loop(low, mid, lambda j, c: visit(j, c, True, False), carry)
    carry = lax.fori_loop(jnp.maximum(low, mid), top, lambda j, c: visit(j, c, False, False), carry)
    carry = visit(None, carry, True, True)
    for n, (h, c) in enumerate(streams):
        peak, total = carry[2 * n], carry[2 * n + 1]
        rows, cols = slice(h * HEAD, (h + 1) * HEAD), slice(c, c + sub)
        acc_ref[rows, cols] = acc_ref[rows, cols] / total
        lse_ref[h:h + 1, cols] = peak + jnp.log(total)
    mixed = acc_ref[...].T.astype(BF16)

    @pl.when(step < half)
    def _():
        oth_ref[...] = mixed

    @pl.when(step >= half)
    def _():
        own_ref[...] = mixed


def placing(blocks):
    half = blocks // 2

    def place(n, sched):
        return lax.rem(n + (1 - sched[0]) * half, blocks)

    return place, half


def attend_forward(sched, own_x, oth_x, weights, cosine, sine, start, bq, bk, sub=256, chunk=512):
    local, width = own_x.shape
    slots, cols = 2 * local, weights.shape[1] // 3
    pairs, blocks = cols // PAIR, slots // bq
    place, half = placing(blocks)
    rows = pl.BlockSpec((local, width), lambda p, n, s: (0, 0), pipeline_mode=pl.Buffered(1))
    table = pl.BlockSpec((slots, PAIR), lambda p, n, s: (0, 0), pipeline_mode=pl.Buffered(1))
    return pl.pallas_call(
        partial(forward_kernel, bq=bq, bk=bk, sub=sub, chunk=chunk, blocks=blocks),
        grid_spec=pltpu.PrefetchScalarGridSpec(
            num_scalar_prefetch=1,
            grid=(pairs, blocks),
            in_specs=[
                rows, rows,
                *[pl.BlockSpec((width, PAIR), lambda p, n, s, at=at: (0, at + p))
                  for at in (0, pairs, 2 * pairs)],
                table, table,
                pl.BlockSpec((1, bq), lambda p, n, s: (0, place(n, s))),
            ],
            out_specs=[
                pl.BlockSpec((slots, 3 * PAIR), lambda p, n, s: (0, p)),
                pl.BlockSpec((bq, PAIR), lambda p, n, s: (jnp.minimum(n, half - 1), p)),
                pl.BlockSpec((bq, PAIR), lambda p, n, s: (jnp.maximum(n - half, 0), p)),
                pl.BlockSpec((None, 2, bq), lambda p, n, s: (p, 0, place(n, s))),
            ],
            scratch_shapes=[pltpu.VMEM((PAIR, bq), F32), pltpu.VMEM((PAIR, slots), BF16)],
        ),
        out_shape=[
            jax.ShapeDtypeStruct((slots, 3 * cols), BF16),
            jax.ShapeDtypeStruct((local, cols), BF16),
            jax.ShapeDtypeStruct((local, cols), BF16),
            jax.ShapeDtypeStruct((pairs, 2, slots), F32),
        ],
        compiler_params=params(dims=2),
        cost_estimate=cost(4 * slots * slots * cols + 6 * slots * width * cols,
                           16 * slots * cols, slots * slots * 6),
        name="attend_forward",
    )(sched, own_x, oth_x, weights, weights, weights, cosine, sine, start)


def backward_kernel(sched, q_ref, k_ref, v_ref, cos_ref, sin_ref, start_ref, lse_ref,
                    o_oth_ref, o_own_ref, g_oth_ref, g_own_ref, x_own_ref, x_oth_ref,
                    all_ref, dw_ref, dq_acc, dkt_acc, dvt_acc, *, bq, bk, sub, blocks):
    step = pl.program_id(1)
    half = blocks // 2
    i = lax.rem(step + (1 - sched[0]) * half, blocks)

    @pl.when(step == 0)
    def _():
        dkt_acc[...] = jnp.zeros_like(dkt_acc)
        dvt_acc[...] = jnp.zeros_like(dvt_acc)

    first = step < half
    grads = jnp.where(first, g_oth_ref[...], g_own_ref[...])
    mixed = jnp.where(first, o_oth_ref[...], o_own_ref[...])
    queries = head_masks(q_ref[...])
    couts = head_masks(grads)
    query_t = q_ref[...].astype(F32).T.astype(BF16)
    cout_t = grads.astype(F32).T.astype(BF16)
    start = start_ref[...]
    product = grads.astype(F32) * mixed.astype(F32)
    big = product.astype(BF16)
    small = (product - big.astype(F32)).astype(BF16)
    row = lax.broadcasted_iota(jnp.int32, (PAIR, 2 * PAIR), 0)
    lane = lax.broadcasted_iota(jnp.int32, (PAIR, 2 * PAIR), 1)
    pick = jnp.where(row // HEAD == lane // PAIR, 1.0, 0.0).astype(BF16)
    inner = mm(big, pick) + mm(small, pick)
    lse = [jnp.broadcast_to(lse_ref[h:h + 1, :], (PAIR, bq)).T for h in range(2)]
    dq_acc[...] = jnp.zeros_like(dq_acc)

    def wide(value, size):
        return jnp.concatenate([value] * (size // PAIR), axis=1)

    def visit(j, masked, last):
        at = pl.multiple_of(i * bq if last else j * bk, bk)
        streams = [(c, h) for c in range(0, bq, sub) for h in range(2)]

        def scores(n):
            c, h = streams[n]
            size = c + sub if last else bk
            where = pl.ds(at, size)
            rows = slice(c, c + sub)
            return rdot(queries[h][rows], k_ref[where, :]), rdot(couts[h][rows], v_ref[where, :])

        def absorb(n, pair):
            c, h = streams[n]
            raw, d_probs = pair
            size = c + sub if last else bk
            where = pl.ds(at, size)
            rows = slice(c, c + sub)
            lanes = slice(h * HEAD, (h + 1) * HEAD)
            probs = jnp.exp(raw - wide(lse[h][rows], size))
            if masked:
                begin = jnp.broadcast_to(start[:, rows], (PAIR, sub)).T
                key_index = at + lax.broadcasted_iota(jnp.int32, (sub, size), 1)
                query_index = i * bq + c + lax.broadcasted_iota(jnp.int32, (sub, size), 0)
                allowed = (key_index >= wide(begin, size)) & (key_index <= query_index)
                probs = jnp.where(allowed, probs, 0.0)
            d_scores = (probs * (d_probs - wide(inner[rows, h * PAIR:(h + 1) * PAIR], size))).astype(BF16)
            dvt_acc[lanes, where] += mm(cout_t[lanes, rows], probs.astype(BF16))
            dkt_acc[lanes, where] += mm(query_t[lanes, rows], d_scores)
            dq_acc[rows, :] += mm(d_scores, head_masks(k_ref[where, :])[h])

        ready = scores(0)
        for n in range(len(streams)):
            held = ready
            if n + 1 < len(streams):
                ready = scores(n + 1)
            absorb(n, held)

    low = sched[2 + i]
    mid = jnp.minimum(sched[2 + blocks + i], i * (bq // bk))

    @pl.loop(low, mid)
    def _(j):
        visit(j, True, False)

    @pl.loop(jnp.maximum(low, mid), i * (bq // bk))
    def _(j):
        visit(j, False, False)

    visit(None, True, True)

    def unrotate(g, cosine, sine):
        return g * cosine - swap_halves(g) * sine

    here = pl.ds(pl.multiple_of(i * bq, bq), bq)
    dq = unrotate(dq_acc[...] * (HEAD ** -0.5), cos_ref[here, :], sin_ref[here, :])
    all_ref[here, 0:PAIR] = dq.astype(BF16)

    @pl.when(step == blocks - 1)
    def _():
        dk = unrotate(dkt_acc[...].T, cos_ref[...], sin_ref[...])
        all_ref[:, PAIR:2 * PAIR] = dk.astype(BF16)
        all_ref[:, 2 * PAIR:] = dvt_acc[...].T.astype(BF16)
        local = x_own_ref.shape[0]
        mine = pl.ds(pl.multiple_of(sched[0] * local, local), local)
        rest = pl.ds(pl.multiple_of((1 - sched[0]) * local, local), local)
        dw_ref[...] = (tdot(x_own_ref[...], all_ref[mine, :])
                       + tdot(x_oth_ref[...], all_ref[rest, :])).astype(BF16)


def attend_backward(sched, qkv, cosine, sine, start, lse, o_oth, o_own, g_oth, g_own, x_own, x_oth,
                    bq, bk, sub=256):
    slots, cols = qkv.shape[0], qkv.shape[1] // 3
    pairs, blocks = cols // PAIR, slots // bq
    local, width = x_own.shape
    place, half = placing(blocks)
    table = pl.BlockSpec((slots, PAIR), lambda p, n, s: (0, 0), pipeline_mode=pl.Buffered(1))
    rows = pl.BlockSpec((local, width), lambda p, n, s: (0, 0), pipeline_mode=pl.Buffered(1))
    oth = pl.BlockSpec((bq, PAIR), lambda p, n, s: (jnp.minimum(n, half - 1), p))
    own = pl.BlockSpec((bq, PAIR), lambda p, n, s: (jnp.maximum(n - half, 0), p))
    return pl.pallas_call(
        partial(backward_kernel, bq=bq, bk=bk, sub=sub, blocks=blocks),
        grid_spec=pltpu.PrefetchScalarGridSpec(
            num_scalar_prefetch=1,
            grid=(pairs, blocks),
            in_specs=[
                pl.BlockSpec((bq, PAIR), lambda p, n, s: (place(n, s), 3 * p)),
                pl.BlockSpec((slots, PAIR), lambda p, n, s: (0, 3 * p + 1)),
                pl.BlockSpec((slots, PAIR), lambda p, n, s: (0, 3 * p + 2)),
                table, table,
                pl.BlockSpec((1, bq), lambda p, n, s: (0, place(n, s))),
                pl.BlockSpec((None, 2, bq), lambda p, n, s: (p, 0, place(n, s))),
                oth, own, oth, own, rows, rows,
            ],
            out_specs=[pl.BlockSpec((slots, 3 * PAIR), lambda p, n, s: (0, p)),
                       pl.BlockSpec((width, 3 * PAIR), lambda p, n, s: (0, p))],
            scratch_shapes=[
                pltpu.VMEM((bq, PAIR), F32),
                pltpu.VMEM((PAIR, slots), F32),
                pltpu.VMEM((PAIR, slots), F32),
            ],
        ),
        out_shape=[jax.ShapeDtypeStruct((slots, 3 * cols), BF16),
                   jax.ShapeDtypeStruct((width, 3 * cols), BF16)],
        compiler_params=params(dims=2),
        cost_estimate=cost(10 * slots * slots * cols + 6 * slots * width * cols,
                           20 * slots * cols, slots * slots * 6),
        name="attend_backward",
    )(sched, qkv, qkv, qkv, cosine, sine, start, lse, o_oth, o_own, g_oth, g_own, x_own, x_oth)


def feed_kernel(sched, x_ref, own_ref, oth_ref, dy_ref, w_hbm, ga_ref, gf_ref,
                out_ref, dfirst_ref, gown_ref, goth_ref, grads_ref, gains_ref,
                w_ref, keep_a, keep_b, hidden_s, dgate_s, dup_s, normed_s, dffn_s, dattn_s, mixed_s,
                sems, *, block, sub, chunk, local, hid, head_cols, parts, share):
    step = pl.program_id(0)
    me = sched[0]
    steps = local // block
    outs = slice(3 * hid, 3 * hid + head_cols)
    pieces = [(slice(3 * hid, w_ref.shape[2]), None), (slice(0, 2 * hid), 0), (slice(0, 2 * hid), 1),
              (slice(2 * hid, 3 * hid), None)]

    def piece(n):
        cols, t = pieces[n]
        at = (slice(None), slice(None), cols) if t is None else (t, slice(None), cols)
        return pltpu.make_async_copy(w_hbm.at[at], w_ref.at[at], sems.at[n])

    @pl.when(step == 0)
    def _():
        for n in range(len(pieces)):
            piece(n).start()
        gains_ref[...] = jnp.zeros_like(gains_ref)

    def arrive(n):
        @pl.when(step == 0)
        def _():
            piece(n).wait()

    chunks = [(t, c) for t in range(2) for c in range(0, hid, chunk)]

    @pl.when(step < steps)
    def _():
        subs = list(range(0, block, sub))
        base = pl.multiple_of(step * block, block)
        arrive(0)
        first, rms1, unit1, normed, normed_b, ffn = {}, {}, {}, {}, {}, {}
        attn = {}
        for r in subs:
            rows = slice(r, r + sub)
            attn[r] = rdot(own_ref[rows, :], w_ref[me, :, outs]) + rdot(oth_ref[rows, :], w_ref[1 - me, :, outs])
        for r in subs:
            rows = slice(r, r + sub)
            here = pl.ds(base + r, sub)
            first = x_ref[rows, :].astype(F32) + attn[r]
            rms1[r] = lax.rsqrt(jnp.mean(first * first, axis=-1, keepdims=True) + EPS)
            unit1[r] = first * rms1[r]
            normed[r] = unit1[r] * ga_ref[...]
            normed_b[r] = normed[r].astype(BF16)
            normed_s[here, :] = normed_b[r]
            mixed_s[here, :] = jnp.concatenate([own_ref[rows, :], oth_ref[rows, :]], axis=1)
        for n, (t, c) in enumerate(chunks):
            if n == 0:
                arrive(1)
            if t == 1 and c == 0:
                arrive(2)
            at = t * hid + c
            cols = slice(at, at + chunk)
            hid_b = {}
            for r in subs:
                rows = slice(r, r + sub)
                here = pl.ds(base + r, sub)
                gate = mm(normed_b[r], w_ref[t, :, c:c + chunk])
                upper = mm(normed_b[r], w_ref[t, :, hid + c:hid + c + chunk])
                sigma = 1.0 / (1.0 + jnp.exp(-gate))
                silu = gate * sigma
                hid_b[r] = (silu * upper).astype(BF16)
                keep_a[rows, cols] = silu
                keep_b[rows, cols] = upper * (sigma + silu * (1.0 - sigma))
                hidden_s[here, cols] = hid_b[r]
            if n == 0:
                arrive(3)
            for r in subs:
                part = rdot(hid_b[r], w_ref[t, :, 2 * hid + c:2 * hid + c + chunk])
                ffn[r] = part if n == 0 else ffn[r] + part
        d_second, d_ffn, dn = {}, {}, {}
        for r in subs:
            rows = slice(r, r + sub)
            here = pl.ds(base + r, sub)
            second = normed[r] + ffn[r]
            rms2 = lax.rsqrt(jnp.mean(second * second, axis=-1, keepdims=True) + EPS)
            unit2 = second * rms2
            slot = me * local + base + r + lax.broadcasted_iota(jnp.int32, (sub, 1), 0)
            valid = slot < sched[1]
            out_ref[rows, :] = jnp.where(valid, unit2 * gf_ref[...], 0.0).astype(BF16)
            dy = jnp.where(valid, dy_ref[rows, :].astype(F32), 0.0)
            gains_ref[1:2, :] += jnp.sum(dy * unit2, axis=0, keepdims=True)
            scaled = dy * gf_ref[...]
            d_second[r] = rms2 * (scaled - unit2 * jnp.mean(scaled * unit2, axis=-1, keepdims=True))
            d_ffn[r] = d_second[r].astype(BF16)
            dffn_s[here, :] = d_ffn[r]
            dn[r] = d_second[r]
        for t, c in chunks:
            at = t * hid + c
            cols = slice(at, at + chunk)
            dg, du = {}, {}
            for r in subs:
                rows = slice(r, r + sub)
                here = pl.ds(base + r, sub)
                d_hidden = mm(d_ffn[r], w_ref[t, :, 2 * hid + c:2 * hid + c + chunk])
                dg[r] = (d_hidden * keep_b[rows, cols]).astype(BF16)
                du[r] = (d_hidden * keep_a[rows, cols]).astype(BF16)
                dgate_s[here, cols] = dg[r]
                dup_s[here, cols] = du[r]
            for r in subs:
                dn[r] = dn[r] + rdot(dg[r], w_ref[t, :, c:c + chunk]) + rdot(du[r], w_ref[t, :, hid + c:hid + c + chunk])
        for r in subs:
            rows = slice(r, r + sub)
            here = pl.ds(base + r, sub)
            gains_ref[0:1, :] += jnp.sum(dn[r] * unit1[r], axis=0, keepdims=True)
            scaled = dn[r] * ga_ref[...]
            d_first = rms1[r] * (scaled - unit1[r] * jnp.mean(scaled * unit1[r], axis=-1, keepdims=True))
            dfirst_ref[rows, :] = d_first
            d_attn = d_first.astype(BF16)
            dattn_s[here, :] = d_attn
            gown_ref[rows, :] = mm(d_attn, w_ref[me, :, outs]).astype(BF16)
            goth_ref[rows, :] = mm(d_attn, w_ref[1 - me, :, outs]).astype(BF16)

    @pl.when(step >= steps)
    def _():
        tile = step - steps
        t, part = lax.div(tile, parts), lax.rem(tile, parts)
        size = dattn_s.shape[1] // parts
        rows = pl.ds(pl.multiple_of(part * size, size), size)
        cols = pl.ds(pl.multiple_of(t * hid, hid), hid)
        mixed = jnp.where(t == me, mixed_s[:, :head_cols], mixed_s[:, head_cols:])
        for at, left, right in ((0, normed_s, dgate_s[:, cols]), (hid, normed_s, dup_s[:, cols]),
                                (2 * hid, dffn_s, hidden_s[:, cols]), (3 * hid, dattn_s, mixed)):
            value = tdot(left[:, rows], right).astype(BF16)
            there = slice(at, at + right.shape[1])
            if share is None:
                grads_ref[0, :, there] = value
            else:
                near = grads_ref.shape[1]
                for n in range(size // share):
                    grads_ref[0, n % near, n // near, :, there] = value[n * share:(n + 1) * share]


def feed(sched, x, own, oth, dy, weights, gain_attn, gain_ffn, hid, share, near,
         block=512, sub=256, chunk=512, parts=2):
    local, width = x.shape
    head_cols = own.shape[1]
    total = weights.shape[2]
    steps = local // block
    packed = share % 16 == 0

    def at(s):
        return jnp.minimum(s, steps - 1)

    rows = pl.BlockSpec((block, width), lambda s, sched: (at(s), 0))
    heads = pl.BlockSpec((block, head_cols), lambda s, sched: (at(s), 0))
    gain = pl.BlockSpec((1, width), lambda s, sched: (0, 0))

    def tile(s, sched):
        n = jnp.maximum(s - steps, 0)
        if packed:
            return (lax.div(n, parts), 0, lax.rem(n, parts), 0, 0)
        return (lax.div(n, parts), lax.rem(n, parts), 0)

    if packed:
        grads_shape = (2, near, width // (near * share), share, total)
        grads_block = (1, near, width // (near * share * parts), share, total)
    else:
        grads_shape, grads_block = (2, width, total), (1, width // parts, total)

    def shape(cols, dtype):
        return jax.ShapeDtypeStruct((local, cols), dtype)

    results = pl.pallas_call(
        partial(feed_kernel, block=block, sub=sub, chunk=chunk, local=local, hid=hid,
                head_cols=head_cols, parts=parts, share=share if packed else None),
        grid_spec=pltpu.PrefetchScalarGridSpec(
            num_scalar_prefetch=1,
            grid=(steps + 2 * parts,),
            in_specs=[rows, heads, heads, rows, pl.BlockSpec(memory_space=pl.ANY), gain, gain],
            out_specs=[rows, rows, heads, heads,
                       pl.BlockSpec(grads_block, tile),
                       pl.BlockSpec((16, width), lambda s, sched: (0, 0))],
            scratch_shapes=[pltpu.VMEM(weights.shape, BF16)]
            + [pltpu.VMEM((block, 2 * hid), F32)] * 2
            + [pltpu.VMEM((local, 2 * hid), BF16)] * 3
            + [pltpu.VMEM((local, width), BF16)] * 3
            + [pltpu.VMEM((local, 2 * head_cols), BF16), pltpu.SemaphoreType.DMA((4,))],
        ),
        out_shape=[
            shape(width, BF16), shape(width, F32), shape(head_cols, BF16), shape(head_cols, BF16),
            jax.ShapeDtypeStruct(grads_shape, BF16),
            jax.ShapeDtypeStruct((16, width), F32),
        ],
        compiler_params=params(60 * 1024 * 1024),
        cost_estimate=cost(12 * local * width * total, 30 * local * width),
        name="feed",
    )(sched, x, own, oth, dy, weights, gain_attn, gain_ffn)
    grads = results[4]
    if not packed:
        grads = grads.reshape(2, -1, near, share, total).swapaxes(1, 2)
    return (*results[:4], grads.reshape(-1, total), results[5])


def input_grad_kernel(sched, d_ref, w_ref, dfirst_ref, oth_ref, own_ref, *, half):
    step = pl.program_id(0)
    cols = d_ref.shape[1]
    order = [at + n * PAIR for n in range(3) for at in range(0, cols, 3 * PAIR)]
    part = rdot(jnp.concatenate([d_ref[:, at:at + PAIR] for at in order], axis=1), w_ref[...])

    @pl.when(step < half)
    def _():
        oth_ref[...] = part.astype(BF16)

    @pl.when(step >= half)
    def _():
        own_ref[...] = dfirst_ref[...] + part


def input_grads(sched, d_qkv, weights, d_first, block):
    local, width = d_first.shape
    cols = d_qkv.shape[1]
    half = local // block
    place, _ = placing(2 * half)
    own = pl.BlockSpec((block, width), lambda n, s: (jnp.maximum(n - half, 0), 0))
    return pl.pallas_call(
        partial(input_grad_kernel, half=half),
        grid_spec=pltpu.PrefetchScalarGridSpec(
            num_scalar_prefetch=1,
            grid=(2 * half,),
            in_specs=[pl.BlockSpec((block, cols), lambda n, s: (place(n, s), 0)),
                      pl.BlockSpec((width, cols), lambda n, s: (0, 0)), own],
            out_specs=[pl.BlockSpec((block, width), lambda n, s: (jnp.minimum(n, half - 1), 0)), own],
        ),
        out_shape=[jax.ShapeDtypeStruct((local, width), BF16),
                   jax.ShapeDtypeStruct((local, width), F32)],
        compiler_params=params(),
        cost_estimate=cost(4 * local * width * cols, 4 * local * (width + cols)),
        name="input_grads",
    )(sched, d_qkv, weights, d_first)


def finish_kernel(total_ref, gate_ref, up_ref, down_ref, out_ref):
    hid = gate_ref.shape[1]
    gate_ref[...] = total_ref[:, 0:hid].astype(F32)
    up_ref[...] = total_ref[:, hid:2 * hid].astype(F32)
    down_ref[...] = total_ref[:, 2 * hid:3 * hid].astype(F32)
    out_ref[...] = total_ref[:, 3 * hid:].astype(F32)


def finish(total, hid):
    share, cols = total.shape
    gate, up, down, out = pl.pallas_call(
        finish_kernel,
        out_shape=[jax.ShapeDtypeStruct((share, width), F32)
                   for width in (hid, hid, hid, cols - 3 * hid)],
        cost_estimate=cost(0, 6 * share * cols),
        name="finish",
    )(total)
    return gate, up, down.T, out.T


def exchange(value):
    return lax.ppermute(value, "tensor", [(0, 1), (1, 0)])


def flip(value, bit):
    count = lax.axis_size(DP)
    return lax.ppermute(value, DP, [(at, at ^ (1 << bit)) for at in range(count)])


def bit_orders(count):
    bits = count.bit_length() - 1
    low = list(range(min(2, bits)))
    high = list(range(min(2, bits), bits))
    return high[::-1] + low, high[::-1] + low[::-1]


def join(held, bit):
    other = flip(held, bit)
    mine = ((lax.axis_index(DP) >> bit) & 1) == 0
    return jnp.stack([jnp.where(mine, held, other), jnp.where(mine, other, held)])


def in_order(held, order):
    bits = len(order)
    rows, cols = held.shape[-2:]
    held = held.reshape((2,) * bits + (rows, cols))
    axes = [bits - 1 - order.index(bit) for bit in range(bits - 1, -1, -1)]
    return held.transpose(*axes, bits, bits + 1).reshape(-1, cols)


def gather_rows(piece, edge):
    fore, back = bit_orders(lax.axis_size(DP))
    high = len(fore) - min(2, len(fore))
    held = piece[None]
    for bit in fore[:high]:
        held = join(held, bit)
    parts = [held[..., :edge], held[..., edge:]]
    for one, two in zip(fore[high:], back[high:]):
        parts = [join(parts[0], one), join(parts[1], two)]
    return jnp.concatenate([in_order(parts[0], fore), in_order(parts[1], back)], axis=1)


def scatter_rows(total, order):
    me = lax.axis_index(DP)
    bits = len(order)
    rows, cols = total.shape[0] >> bits, total.shape[1]
    held = total.reshape((2,) * bits + (rows, cols))
    left = list(range(bits - 1, -1, -1))
    for bit in order:
        axis = left.index(bit)
        left.pop(axis)
        low = lax.index_in_dim(held, 0, axis, keepdims=False)
        high = lax.index_in_dim(held, 1, axis, keepdims=False)
        mine = ((me >> bit) & 1) == 0
        got = flip(jnp.where(mine, high, low), bit)
        held = (jnp.where(mine, low, high).astype(F32) + got.astype(F32)).astype(BF16)
    return held.reshape(rows, cols)


def local(tokens, w_query, w_key, w_value, w_out, w_gate, w_up, w_down, gain_attn, gain_ffn,
          lengths, cotangent):
    rows, width = tokens.shape
    slots = 2 * rows
    me = lax.axis_index("tensor")
    count = lax.axis_size(DP)
    cols, hid = w_query.shape[1], w_gate.shape[1]
    share = width // count
    edge = 5 * cols // 3
    bq, bk = rows, rows // 2
    blocks = slots // bq

    packed = jnp.concatenate([w_gate, w_up, w_down.T, w_out.T], axis=1)
    feed_w = lax.all_gather(packed, ("tensor",) + DP, axis=0, tiled=True)
    feed_w = feed_w.reshape(2, width, packed.shape[1])
    full_qkv = gather_rows(jnp.concatenate([w_query, w_key, w_value], axis=1), edge)
    other_x = exchange(tokens)

    index = jnp.arange(slots, dtype=jnp.int32)
    row = lengths[0]
    ends = jnp.cumsum(row)
    begins = jnp.sum(jnp.where(index[:, None] >= ends[None, :], row[None, :], 0), axis=1)
    position = (index - begins).astype(F32)
    lane = jnp.arange(PAIR, dtype=jnp.int32) % HEAD
    inverse = ROPE_BASE ** (-((lane % (HEAD // 2)).astype(F32) * 2.0 / HEAD))
    angle = position[:, None] * inverse[None, :]
    cosine = jnp.cos(angle)
    sine = jnp.where(lane[None, :] < HEAD // 2, -jnp.sin(angle), jnp.sin(angle))
    block_begin = begins.reshape(blocks, bq)
    sched = jnp.concatenate([
        jnp.stack([me.astype(jnp.int32), ends[-1]]),
        block_begin[:, 0] // bk,
        (block_begin[:, -1] + bk - 1) // bk,
    ])
    start = begins.reshape(1, slots)

    qkv, mixed_send, mixed_own, lse = attend_forward(
        sched, tokens, other_x, full_qkv, cosine, sine, start, bq, bk)
    mixed_oth = exchange(mixed_send)
    output, d_first, g_own, g_send, grads, gains = feed(
        sched, tokens, mixed_own, mixed_oth, cotangent, feed_w, gain_attn.reshape(1, width),
        gain_ffn.reshape(1, width), hid, share, lax.axis_size("near"))
    g_oth = exchange(g_send)
    reduced = lax.psum_scatter(grads, ("tensor", "near"), scatter_dimension=0, tiled=True)
    reduced = lax.psum_scatter(reduced, "far", scatter_dimension=0, tiled=True)
    gains = gains[:2] + exchange(gains[:2])
    d_qkv, dw = attend_backward(sched, qkv, cosine, sine, start, lse, mixed_send, mixed_own,
                                g_oth, g_own, tokens, other_x, bq, bk)
    dw, gains = lax.optimization_barrier((dw, gains))
    fore, back = bit_orders(count)
    for bit in fore[::-1]:
        gains = gains + flip(gains, bit)
    dw = jnp.concatenate([scatter_rows(dw[:, :edge], fore[::-1]),
                          scatter_rows(dw[:, edge:], back[::-1])], axis=1).astype(F32)
    dw = dw.reshape(share, cols // PAIR, 3, PAIR)
    x_send, x_own = input_grads(sched, d_qkv, full_qkv, d_first, 512)
    input_grad = (x_own + exchange(x_send).astype(F32)).astype(BF16)
    grad_gate, grad_up, grad_down, grad_out = finish(reduced, hid)
    return (
        output,
        input_grad,
        dw[:, :, 0].reshape(share, cols),
        dw[:, :, 1].reshape(share, cols),
        dw[:, :, 2].reshape(share, cols),
        grad_out,
        grad_gate,
        grad_up,
        grad_down,
        gains[0],
        gains[1],
    )


def solution(mesh):
    count, pair = mesh.shape["dp"], mesh.shape["tensor"]
    near = min(4, count)
    mesh = Mesh(mesh.devices.reshape(count // near, near, pair), DP + ("tensor",))
    split = P(DP, "tensor")
    turned = P("tensor", DP)
    slots = P(DP + ("tensor",), None)
    return jax.shard_map(
        local,
        mesh=mesh,
        in_specs=(slots, split, split, split, turned, split, split, turned, P(), P(),
                  P(DP, None), slots),
        out_specs=(slots, slots, split, split, split, turned, split, split, turned, P(), P()),
        check_vma=False,
    )
```

```python
from functools import partial

import jax
import jax.numpy as jnp
from jax import lax
from jax.experimental import pallas as pl
from jax.experimental.pallas import tpu as pltpu
from jax.sharding import Mesh
from jax.sharding import PartitionSpec as P

HEAD = 64
PAIR = 2 * HEAD
EPS = 1e-05
ROPE_BASE = 10000.0
NEGATIVE = -1e30
F32 = jnp.float32
BF16 = jnp.bfloat16
VMEM_LIMIT = 56 * 1024 * 1024
DP = ("far", "near")


def mm(left, right):
    return jnp.dot(left, right, preferred_element_type=F32)


def rdot(left, right):
    return lax.dot_general(left, right, (((1,), (1,)), ((), ())), preferred_element_type=F32)


def tdot(left, right):
    return lax.dot_general(left, right, (((0,), (0,)), ((), ())), preferred_element_type=F32)


def params(limit=VMEM_LIMIT, dims=1):
    return pltpu.CompilerParams(
        vmem_limit_bytes=limit, dimension_semantics=("arbitrary",) * dims
    )


def cost(flops, nbytes, trans=0):
    return pl.CostEstimate(flops=int(flops), bytes_accessed=int(nbytes), transcendentals=int(trans))


def swap_halves(values):
    lane = lax.broadcasted_iota(jnp.int32, values.shape, 1) % HEAD
    half = HEAD // 2
    width = values.shape[1]
    return jnp.where(
        lane < half, pltpu.roll(values, width - half, 1), pltpu.roll(values, half, 1)
    )


def head_masks(values):
    return one_head(values, 0), one_head(values, 1)


def one_head(values, h):
    lane = lax.broadcasted_iota(jnp.int32, (1, PAIR), 1)
    return values * (lane // HEAD == h).astype(values.dtype)


def forward_kernel(sched, own_x_ref, oth_x_ref, wq_ref, wk_ref, wv_ref, cos_ref, sin_ref, start_ref,
                   qkv_ref, oth_ref, own_ref, lse_ref, acc_ref, vt_ref, *, bq, bk, sub, chunk, blocks):
    step = pl.program_id(1)
    half = blocks // 2
    i = lax.rem(step + (1 - sched[0]) * half, blocks)

    @pl.when(step == 0)
    def _():
        local = own_x_ref.shape[0]
        weights = jnp.concatenate([wq_ref[...], wk_ref[...], wv_ref[...]], axis=1)
        for x_ref, side in ((own_x_ref, sched[0]), (oth_x_ref, 1 - sched[0])):
            for r in range(0, local, chunk):
                here = pl.ds(pl.multiple_of(side * local + r, chunk), chunk)
                u = mm(x_ref[r:r + chunk, :], weights)
                cosine, sine = cos_ref[here, :], sin_ref[here, :]
                for n, scale in ((0, HEAD ** -0.5), (1, 1.0)):
                    piece = u[:, n * PAIR:(n + 1) * PAIR]
                    turned = piece * cosine + swap_halves(piece) * sine
                    qkv_ref[here, n * PAIR:(n + 1) * PAIR] = (turned * scale).astype(BF16)
                v = u[:, 2 * PAIR:]
                qkv_ref[here, 2 * PAIR:] = v.astype(BF16)
                vt_ref[:, here] = v.T.astype(BF16)

    start = start_ref[...]
    acc_ref[...] = jnp.zeros_like(acc_ref)
    streams = list(range(0, bq, sub))

    @pl.loop(0, 2)
    def _(h):
        queries = one_head(qkv_ref[pl.ds(pl.multiple_of(i * bq, bq), bq), 0:PAIR], h)
        rows = pl.ds(pl.multiple_of(h * HEAD, HEAD), HEAD)

        def visit(j, carry, last):
            at = pl.multiple_of(i * bq if last else j * bk, bk)
            scores, out = [], []
            for c in streams:
                size = c + sub if last else bk
                s = rdot(qkv_ref[pl.ds(at, size), PAIR:2 * PAIR], queries[c:c + sub])
                key_index = lax.broadcasted_iota(jnp.int32, (size, sub), 0)
                allowed = key_index >= start[:, c:c + sub] - at
                if last:
                    query_index = c + lax.broadcasted_iota(jnp.int32, (size, sub), 1)
                    allowed = allowed & (key_index <= query_index)
                scores.append(jnp.where(allowed, s, NEGATIVE))
            for n, c in enumerate(streams):
                size = c + sub if last else bk
                peak, total = carry[2 * n], carry[2 * n + 1]
                new_peak = jnp.maximum(peak, jnp.max(scores[n], axis=0, keepdims=True))
                fade = jnp.exp(peak - new_peak)
                expo = jnp.exp(scores[n] - new_peak)
                total = total * fade + jnp.sum(expo, axis=0, keepdims=True)
                cols = slice(c, c + sub)
                acc_ref[rows, cols] = acc_ref[rows, cols] * fade + mm(
                    vt_ref[rows, pl.ds(at, size)], expo.astype(BF16)
                )
                out += [new_peak, total]
            return tuple(out)

        carry = (jnp.full((1, sub), NEGATIVE, F32), jnp.zeros((1, sub), F32)) * len(streams)
        carry = lax.fori_loop(sched[2 + i], i * (bq // bk), lambda j, c: visit(j, c, False), carry)
        carry = visit(None, carry, True)
        for n, c in enumerate(streams):
            peak, total = carry[2 * n], carry[2 * n + 1]
            cols = slice(c, c + sub)
            acc_ref[rows, cols] = acc_ref[rows, cols] / total
            lse_ref[pl.ds(h, 1), cols] = peak + jnp.log(total)

    mixed = acc_ref[...].T.astype(BF16)

    @pl.when(step < half)
    def _():
        oth_ref[...] = mixed

    @pl.when(step >= half)
    def _():
        own_ref[...] = mixed


def placing(blocks):
    half = blocks // 2

    def place(n, sched):
        return lax.rem(n + (1 - sched[0]) * half, blocks)

    return place, half


def attend_forward(sched, own_x, oth_x, weights, cosine, sine, start, bq, bk, sub=256, chunk=512):
    local, width = own_x.shape
    slots, cols = 2 * local, weights.shape[1] // 3
    pairs, blocks = cols // PAIR, slots // bq
    place, half = placing(blocks)
    rows = pl.BlockSpec((local, width), lambda p, n, s: (0, 0), pipeline_mode=pl.Buffered(1))
    table = pl.BlockSpec((slots, PAIR), lambda p, n, s: (0, 0), pipeline_mode=pl.Buffered(1))
    return pl.pallas_call(
        partial(forward_kernel, bq=bq, bk=bk, sub=sub, chunk=chunk, blocks=blocks),
        grid_spec=pltpu.PrefetchScalarGridSpec(
            num_scalar_prefetch=1,
            grid=(pairs, blocks),
            in_specs=[
                rows, rows,
                *[pl.BlockSpec((width, PAIR), lambda p, n, s, at=at: (0, at + p))
                  for at in (0, pairs, 2 * pairs)],
                table, table,
                pl.BlockSpec((1, bq), lambda p, n, s: (0, place(n, s))),
            ],
            out_specs=[
                pl.BlockSpec((slots, 3 * PAIR), lambda p, n, s: (0, p)),
                pl.BlockSpec((bq, PAIR), lambda p, n, s: (jnp.minimum(n, half - 1), p)),
                pl.BlockSpec((bq, PAIR), lambda p, n, s: (jnp.maximum(n - half, 0), p)),
                pl.BlockSpec((None, 2, bq), lambda p, n, s: (p, 0, place(n, s))),
            ],
            scratch_shapes=[pltpu.VMEM((PAIR, bq), F32), pltpu.VMEM((PAIR, slots), BF16)],
        ),
        out_shape=[
            jax.ShapeDtypeStruct((slots, 3 * cols), BF16),
            jax.ShapeDtypeStruct((local, cols), BF16),
            jax.ShapeDtypeStruct((local, cols), BF16),
            jax.ShapeDtypeStruct((pairs, 2, slots), F32),
        ],
        compiler_params=params(dims=2),
        cost_estimate=cost(4 * slots * slots * cols + 6 * slots * width * cols,
                           16 * slots * cols, slots * slots * 6),
        name="attend_forward",
    )(sched, own_x, oth_x, weights, weights, weights, cosine, sine, start)


def backward_kernel(sched, q_ref, k_ref, v_ref, cos_ref, sin_ref, start_ref, lse_ref,
                    o_oth_ref, o_own_ref, g_oth_ref, g_own_ref, x_own_ref, x_oth_ref,
                    all_ref, dw_ref, dq_acc, dkt_acc, dvt_acc, *, bq, bk, sub, blocks):
    step = pl.program_id(1)
    half = blocks // 2
    i = lax.rem(step + (1 - sched[0]) * half, blocks)

    @pl.when(step == 0)
    def _():
        dkt_acc[...] = jnp.zeros_like(dkt_acc)
        dvt_acc[...] = jnp.zeros_like(dvt_acc)

    first = step < half
    grads = jnp.where(first, g_oth_ref[...], g_own_ref[...])
    mixed = jnp.where(first, o_oth_ref[...], o_own_ref[...])
    queries = head_masks(q_ref[...])
    couts = head_masks(grads)
    query_t = q_ref[...].astype(F32).T.astype(BF16)
    cout_t = grads.astype(F32).T.astype(BF16)
    begin = jnp.broadcast_to(start_ref[...], (PAIR, bq)).T
    product = grads.astype(F32) * mixed.astype(F32)
    big = product.astype(BF16)
    small = (product - big.astype(F32)).astype(BF16)
    row = lax.broadcasted_iota(jnp.int32, (PAIR, 2 * PAIR), 0)
    lane = lax.broadcasted_iota(jnp.int32, (PAIR, 2 * PAIR), 1)
    pick = jnp.where(row // HEAD == lane // PAIR, 1.0, 0.0).astype(BF16)
    inner = mm(big, pick) + mm(small, pick)
    lse = [jnp.broadcast_to(lse_ref[h:h + 1, :], (PAIR, bq)).T for h in range(2)]
    dq_acc[...] = jnp.zeros_like(dq_acc)

    def wide(value, size):
        return jnp.concatenate([value] * (size // PAIR), axis=1)

    def visit(j, last):
        at = pl.multiple_of(i * bq if last else j * bk, bk)
        streams = [(c, h) for c in range(0, bq, sub) for h in range(2)]

        def scores(n):
            c, h = streams[n]
            size = c + sub if last else bk
            where = pl.ds(at, size)
            rows = slice(c, c + sub)
            return rdot(queries[h][rows], k_ref[where, :]), rdot(couts[h][rows], v_ref[where, :])

        def absorb(n, pair):
            c, h = streams[n]
            raw, d_probs = pair
            size = c + sub if last else bk
            where = pl.ds(at, size)
            rows = slice(c, c + sub)
            lanes = slice(h * HEAD, (h + 1) * HEAD)
            probs = jnp.exp(raw - wide(lse[h][rows], size))
            key_index = lax.broadcasted_iota(jnp.int32, (sub, size), 1)
            allowed = key_index >= wide(begin[rows], size) - at
            if last:
                query_index = c + lax.broadcasted_iota(jnp.int32, (sub, size), 0)
                allowed = allowed & (key_index <= query_index)
            probs = jnp.where(allowed, probs, 0.0)
            d_scores = (probs * (d_probs - wide(inner[rows, h * PAIR:(h + 1) * PAIR], size))).astype(BF16)
            dvt_acc[lanes, where] += mm(cout_t[lanes, rows], probs.astype(BF16))
            dkt_acc[lanes, where] += mm(query_t[lanes, rows], d_scores)
            dq_acc[rows, :] += mm(d_scores, head_masks(k_ref[where, :])[h])

        ready = scores(0)
        for n in range(len(streams)):
            held = ready
            if n + 1 < len(streams):
                ready = scores(n + 1)
            absorb(n, held)

    @pl.loop(sched[2 + blocks + i], i * (bq // bk))
    def _(j):
        visit(j, False)

    visit(None, True)

    def unrotate(g, cosine, sine):
        return g * cosine - swap_halves(g) * sine

    here = pl.ds(pl.multiple_of(i * bq, bq), bq)
    dq = unrotate(dq_acc[...] * (HEAD ** -0.5), cos_ref[here, :], sin_ref[here, :])
    all_ref[here, 0:PAIR] = dq.astype(BF16)

    @pl.when(step == blocks - 1)
    def _():
        dk = unrotate(dkt_acc[...].T, cos_ref[...], sin_ref[...])
        all_ref[:, PAIR:2 * PAIR] = dk.astype(BF16)
        all_ref[:, 2 * PAIR:] = dvt_acc[...].T.astype(BF16)
        local = x_own_ref.shape[0]
        mine = pl.ds(pl.multiple_of(sched[0] * local, local), local)
        rest = pl.ds(pl.multiple_of((1 - sched[0]) * local, local), local)
        dw_ref[...] = (tdot(x_own_ref[...], all_ref[mine, :])
                       + tdot(x_oth_ref[...], all_ref[rest, :])).astype(BF16)


def attend_backward(sched, qkv, cosine, sine, start, lse, o_oth, o_own, g_oth, g_own, x_own, x_oth,
                    bq, bk, sub=256):
    slots, cols = qkv.shape[0], qkv.shape[1] // 3
    pairs, blocks = cols // PAIR, slots // bq
    local, width = x_own.shape
    place, half = placing(blocks)
    table = pl.BlockSpec((slots, PAIR), lambda p, n, s: (0, 0), pipeline_mode=pl.Buffered(1))
    rows = pl.BlockSpec((local, width), lambda p, n, s: (0, 0), pipeline_mode=pl.Buffered(1))
    oth = pl.BlockSpec((bq, PAIR), lambda p, n, s: (jnp.minimum(n, half - 1), p))
    own = pl.BlockSpec((bq, PAIR), lambda p, n, s: (jnp.maximum(n - half, 0), p))
    return pl.pallas_call(
        partial(backward_kernel, bq=bq, bk=bk, sub=sub, blocks=blocks),
        grid_spec=pltpu.PrefetchScalarGridSpec(
            num_scalar_prefetch=1,
            grid=(pairs, blocks),
            in_specs=[
                pl.BlockSpec((bq, PAIR), lambda p, n, s: (place(n, s), 3 * p)),
                pl.BlockSpec((slots, PAIR), lambda p, n, s: (0, 3 * p + 1)),
                pl.BlockSpec((slots, PAIR), lambda p, n, s: (0, 3 * p + 2)),
                table, table,
                pl.BlockSpec((1, bq), lambda p, n, s: (0, place(n, s))),
                pl.BlockSpec((None, 2, bq), lambda p, n, s: (p, 0, place(n, s))),
                oth, own, oth, own, rows, rows,
            ],
            out_specs=[pl.BlockSpec((slots, 3 * PAIR), lambda p, n, s: (0, p)),
                       pl.BlockSpec((width, 3 * PAIR), lambda p, n, s: (0, p))],
            scratch_shapes=[
                pltpu.VMEM((bq, PAIR), F32),
                pltpu.VMEM((PAIR, slots), F32),
                pltpu.VMEM((PAIR, slots), F32),
            ],
        ),
        out_shape=[jax.ShapeDtypeStruct((slots, 3 * cols), BF16),
                   jax.ShapeDtypeStruct((width, 3 * cols), BF16)],
        compiler_params=params(dims=2),
        cost_estimate=cost(10 * slots * slots * cols + 6 * slots * width * cols,
                           20 * slots * cols, slots * slots * 6),
        name="attend_backward",
    )(sched, qkv, qkv, qkv, cosine, sine, start, lse, o_oth, o_own, g_oth, g_own, x_own, x_oth)


def feed_kernel(sched, x_ref, own_ref, oth_ref, dy_ref, w_hbm, ga_ref, gf_ref,
                out_ref, dfirst_ref, gown_ref, goth_ref, grads_ref, gains_ref,
                w_ref, keep_a, keep_b, total_s, right_s, left_s, dattn_s, mixed_s,
                sems, *, block, sub, chunk, local, hid, head_cols, parts, share):
    step = pl.program_id(0)
    me = sched[0]
    steps = local // block
    outs = slice(3 * hid, 3 * hid + head_cols)
    pieces = [(slice(3 * hid, w_ref.shape[2]), None), (slice(0, 2 * hid), 0), (slice(0, 2 * hid), 1),
              (slice(2 * hid, 3 * hid), None)]

    def piece(n):
        cols, t = pieces[n]
        at = (slice(None), slice(None), cols) if t is None else (t, slice(None), cols)
        return pltpu.make_async_copy(w_hbm.at[at], w_ref.at[at], sems.at[n])

    @pl.when(step == 0)
    def _():
        for n in range(len(pieces)):
            piece(n).start()
        gains_ref[...] = jnp.zeros_like(gains_ref)

    def arrive(n):
        @pl.when(step == 0)
        def _():
            piece(n).wait()

    @pl.when(step < steps)
    def _():
        subs = list(range(0, block, sub))
        base = pl.multiple_of(step * block, block)
        arrive(0)
        attn, rms1, unit1, normed, normed_b = {}, {}, {}, {}, {}
        for r in subs:
            rows = slice(r, r + sub)
            attn[r] = rdot(own_ref[rows, :], w_ref[me, :, outs]) + rdot(oth_ref[rows, :], w_ref[1 - me, :, outs])
        for r in subs:
            rows = slice(r, r + sub)
            here = pl.ds(base + r, sub)
            first = x_ref[rows, :].astype(F32) + attn[r]
            rms1[r] = lax.rsqrt(jnp.mean(first * first, axis=-1, keepdims=True) + EPS)
            unit1[r] = first * rms1[r]
            normed[r] = unit1[r] * ga_ref[...]
            normed_b[r] = normed[r].astype(BF16)
            left_s[0, here, :] = normed_b[r]
            mixed_s[here, :] = jnp.concatenate([own_ref[rows, :], oth_ref[rows, :]], axis=1)
        total_s[...] = jnp.zeros_like(total_s)

        @pl.loop(0, 2)
        def _(t):
            for at, count in ((0, 1), (0, 3), (1, 2)):
                @pl.when((step == 0) & (t == at))
                def _():
                    piece(count).wait()

            for c in range(0, hid, chunk):
                cols = pl.ds(pl.multiple_of(t * hid + c, chunk), chunk)
                hid_b = {}
                for r in subs:
                    rows = slice(r, r + sub)
                    gate = mm(normed_b[r], w_ref[t, :, c:c + chunk])
                    upper = mm(normed_b[r], w_ref[t, :, hid + c:hid + c + chunk])
                    sigma = 1.0 / (1.0 + jnp.exp(-gate))
                    silu = gate * sigma
                    hid_b[r] = (silu * upper).astype(BF16)
                    keep_a[rows, cols] = silu
                    keep_b[rows, cols] = upper * (sigma + silu * (1.0 - sigma))
                    right_s[2, pl.ds(base + r, sub), cols] = hid_b[r]
                for r in subs:
                    total_s[r:r + sub, :] += rdot(hid_b[r], w_ref[t, :, 2 * hid + c:2 * hid + c + chunk])

        d_second, d_ffn = {}, {}
        for r in subs:
            rows = slice(r, r + sub)
            here = pl.ds(base + r, sub)
            second = normed[r] + total_s[rows, :]
            rms2 = lax.rsqrt(jnp.mean(second * second, axis=-1, keepdims=True) + EPS)
            unit2 = second * rms2
            slot = me * local + base + r + lax.broadcasted_iota(jnp.int32, (sub, 1), 0)
            valid = slot < sched[1]
            out_ref[rows, :] = jnp.where(valid, unit2 * gf_ref[...], 0.0).astype(BF16)
            dy = jnp.where(valid, dy_ref[rows, :].astype(F32), 0.0)
            gains_ref[1:2, :] += jnp.sum(dy * unit2, axis=0, keepdims=True)
            scaled = dy * gf_ref[...]
            d_second[r] = rms2 * (scaled - unit2 * jnp.mean(scaled * unit2, axis=-1, keepdims=True))
            d_ffn[r] = d_second[r].astype(BF16)
            left_s[1, here, :] = d_ffn[r]
            total_s[rows, :] = d_second[r]

        @pl.loop(0, 2)
        def _(t):
            for c in range(0, hid, chunk):
                cols = pl.ds(pl.multiple_of(t * hid + c, chunk), chunk)
                dg, du = {}, {}
                for r in subs:
                    rows, here = slice(r, r + sub), pl.ds(base + r, sub)
                    d_hidden = mm(d_ffn[r], w_ref[t, :, 2 * hid + c:2 * hid + c + chunk])
                    dg[r] = (d_hidden * keep_b[rows, cols]).astype(BF16)
                    du[r] = (d_hidden * keep_a[rows, cols]).astype(BF16)
                    right_s[0, here, cols] = dg[r]
                    right_s[1, here, cols] = du[r]
                for r in subs:
                    total_s[r:r + sub, :] += rdot(dg[r], w_ref[t, :, c:c + chunk]) + rdot(
                        du[r], w_ref[t, :, hid + c:hid + c + chunk])

        for r in subs:
            rows = slice(r, r + sub)
            here = pl.ds(base + r, sub)
            d_normed = total_s[rows, :]
            gains_ref[0:1, :] += jnp.sum(d_normed * unit1[r], axis=0, keepdims=True)
            scaled = d_normed * ga_ref[...]
            d_first = rms1[r] * (scaled - unit1[r] * jnp.mean(scaled * unit1[r], axis=-1, keepdims=True))
            dfirst_ref[rows, :] = d_first
            d_attn = d_first.astype(BF16)
            dattn_s[here, :] = d_attn
            gown_ref[rows, :] = mm(d_attn, w_ref[me, :, outs]).astype(BF16)
            goth_ref[rows, :] = mm(d_attn, w_ref[1 - me, :, outs]).astype(BF16)

    @pl.when(step >= steps)
    def _():
        tile = step - steps
        t, part = lax.div(tile, parts), lax.rem(tile, parts)
        size = dattn_s.shape[1] // parts
        rows = pl.ds(pl.multiple_of(part * size, size), size)
        cols = pl.ds(pl.multiple_of(t * hid, hid), hid)

        def store(value, there):
            if share is None:
                grads_ref[0, :, there] = value
            else:
                near = grads_ref.shape[1]
                for n in range(size // share):
                    grads_ref[0, n % near, n // near, :, there] = value[n * share:(n + 1) * share]

        for n in range(3):
            left = left_s[n // 2, :, rows]
            store(tdot(left, right_s[n, :, cols]).astype(BF16), slice(n * hid, (n + 1) * hid))

        mixed = jnp.where(t == me, mixed_s[:, :head_cols], mixed_s[:, head_cols:])
        store(tdot(dattn_s[:, rows], mixed).astype(BF16), slice(3 * hid, 3 * hid + head_cols))


def feed(sched, x, own, oth, dy, weights, gain_attn, gain_ffn, hid, share, near,
         block=512, sub=256, chunk=512, parts=2):
    local, width = x.shape
    head_cols = own.shape[1]
    total = weights.shape[2]
    steps = local // block
    packed = share % 16 == 0

    def at(s):
        return jnp.minimum(s, steps - 1)

    rows = pl.BlockSpec((block, width), lambda s, sched: (at(s), 0))
    heads = pl.BlockSpec((block, head_cols), lambda s, sched: (at(s), 0))
    gain = pl.BlockSpec((1, width), lambda s, sched: (0, 0))

    def tile(s, sched):
        n = jnp.maximum(s - steps, 0)
        if packed:
            return (lax.div(n, parts), 0, lax.rem(n, parts), 0, 0)
        return (lax.div(n, parts), lax.rem(n, parts), 0)

    if packed:
        grads_shape = (2, near, width // (near * share), share, total)
        grads_block = (1, near, width // (near * share * parts), share, total)
    else:
        grads_shape, grads_block = (2, width, total), (1, width // parts, total)

    def shape(cols, dtype):
        return jax.ShapeDtypeStruct((local, cols), dtype)

    results = pl.pallas_call(
        partial(feed_kernel, block=block, sub=sub, chunk=chunk, local=local, hid=hid,
                head_cols=head_cols, parts=parts, share=share if packed else None),
        grid_spec=pltpu.PrefetchScalarGridSpec(
            num_scalar_prefetch=1,
            grid=(steps + 2 * parts,),
            in_specs=[rows, heads, heads, rows, pl.BlockSpec(memory_space=pl.ANY), gain, gain],
            out_specs=[rows, rows, heads, heads,
                       pl.BlockSpec(grads_block, tile),
                       pl.BlockSpec((16, width), lambda s, sched: (0, 0))],
            scratch_shapes=[pltpu.VMEM(weights.shape, BF16)]
            + [pltpu.VMEM((block, 2 * hid), F32)] * 2
            + [pltpu.VMEM((block, width), F32)]
            + [pltpu.VMEM((3, local, 2 * hid), BF16), pltpu.VMEM((2, local, width), BF16)]
            + [pltpu.VMEM((local, width), BF16)]
            + [pltpu.VMEM((local, 2 * head_cols), BF16), pltpu.SemaphoreType.DMA((4,))],
        ),
        out_shape=[
            shape(width, BF16), shape(width, F32), shape(head_cols, BF16), shape(head_cols, BF16),
            jax.ShapeDtypeStruct(grads_shape, BF16),
            jax.ShapeDtypeStruct((16, width), F32),
        ],
        compiler_params=params(60 * 1024 * 1024),
        cost_estimate=cost(12 * local * width * total, 30 * local * width),
        name="feed",
    )(sched, x, own, oth, dy, weights, gain_attn, gain_ffn)
    grads = results[4]
    if not packed:
        grads = grads.reshape(2, -1, near, share, total).swapaxes(1, 2)
    return (*results[:4], grads.reshape(-1, total), results[5])


def input_grad_kernel(sched, d_ref, w_ref, dfirst_ref, oth_ref, own_ref, *, half):
    step = pl.program_id(0)
    cols = d_ref.shape[1]
    order = [at + n * PAIR for n in range(3) for at in range(0, cols, 3 * PAIR)]
    part = rdot(jnp.concatenate([d_ref[:, at:at + PAIR] for at in order], axis=1), w_ref[...])

    @pl.when(step < half)
    def _():
        oth_ref[...] = part.astype(BF16)

    @pl.when(step >= half)
    def _():
        own_ref[...] = dfirst_ref[...] + part


def input_grads(sched, d_qkv, weights, d_first, block):
    local, width = d_first.shape
    cols = d_qkv.shape[1]
    half = local // block
    place, _ = placing(2 * half)
    own = pl.BlockSpec((block, width), lambda n, s: (jnp.maximum(n - half, 0), 0))
    return pl.pallas_call(
        partial(input_grad_kernel, half=half),
        grid_spec=pltpu.PrefetchScalarGridSpec(
            num_scalar_prefetch=1,
            grid=(2 * half,),
            in_specs=[pl.BlockSpec((block, cols), lambda n, s: (place(n, s), 0)),
                      pl.BlockSpec((width, cols), lambda n, s: (0, 0)), own],
            out_specs=[pl.BlockSpec((block, width), lambda n, s: (jnp.minimum(n, half - 1), 0)), own],
        ),
        out_shape=[jax.ShapeDtypeStruct((local, width), BF16),
                   jax.ShapeDtypeStruct((local, width), F32)],
        compiler_params=params(),
        cost_estimate=cost(4 * local * width * cols, 4 * local * (width + cols)),
        name="input_grads",
    )(sched, d_qkv, weights, d_first)


def finish_kernel(total_ref, gate_ref, up_ref, down_ref, out_ref):
    hid = gate_ref.shape[1]
    gate_ref[...] = total_ref[:, 0:hid].astype(F32)
    up_ref[...] = total_ref[:, hid:2 * hid].astype(F32)
    down_ref[...] = total_ref[:, 2 * hid:3 * hid].astype(F32)
    out_ref[...] = total_ref[:, 3 * hid:].astype(F32)


def finish(total, hid):
    share, cols = total.shape
    gate, up, down, out = pl.pallas_call(
        finish_kernel,
        out_shape=[jax.ShapeDtypeStruct((share, width), F32)
                   for width in (hid, hid, hid, cols - 3 * hid)],
        cost_estimate=cost(0, 6 * share * cols),
        name="finish",
    )(total)
    return gate, up, down.T, out.T


def exchange(value):
    return lax.ppermute(value, "tensor", [(0, 1), (1, 0)])


def flip(value, bit):
    count = lax.axis_size(DP)
    return lax.ppermute(value, DP, [(at, at ^ (1 << bit)) for at in range(count)])


def bit_orders(count):
    bits = count.bit_length() - 1
    low = list(range(min(2, bits)))
    high = list(range(min(2, bits), bits))
    return high[::-1] + low, high[::-1] + low[::-1]


def join(held, bit):
    other = flip(held, bit)
    mine = ((lax.axis_index(DP) >> bit) & 1) == 0
    return jnp.stack([jnp.where(mine, held, other), jnp.where(mine, other, held)])


def in_order(held, order):
    bits = len(order)
    rows, cols = held.shape[-2:]
    held = held.reshape((2,) * bits + (rows, cols))
    axes = [bits - 1 - order.index(bit) for bit in range(bits - 1, -1, -1)]
    return held.transpose(*axes, bits, bits + 1).reshape(-1, cols)


def gather_rows(piece, edge):
    fore, back = bit_orders(lax.axis_size(DP))
    high = len(fore) - min(2, len(fore))
    held = piece[None]
    for bit in fore[:high]:
        held = join(held, bit)
    parts = [held[..., :edge], held[..., edge:]]
    for one, two in zip(fore[high:], back[high:]):
        parts = [join(parts[0], one), join(parts[1], two)]
    return jnp.concatenate([in_order(parts[0], fore), in_order(parts[1], back)], axis=1)


def scatter_rows(total, order):
    me = lax.axis_index(DP)
    bits = len(order)
    rows, cols = total.shape[0] >> bits, total.shape[1]
    held = total.reshape((2,) * bits + (rows, cols))
    left = list(range(bits - 1, -1, -1))
    for bit in order:
        axis = left.index(bit)
        left.pop(axis)
        low = lax.index_in_dim(held, 0, axis, keepdims=False)
        high = lax.index_in_dim(held, 1, axis, keepdims=False)
        mine = ((me >> bit) & 1) == 0
        got = flip(jnp.where(mine, high, low), bit)
        held = (jnp.where(mine, low, high).astype(F32) + got.astype(F32)).astype(BF16)
    return held.reshape(rows, cols)


def local(tokens, w_query, w_key, w_value, w_out, w_gate, w_up, w_down, gain_attn, gain_ffn,
          lengths, cotangent):
    rows, width = tokens.shape
    slots = 2 * rows
    me = lax.axis_index("tensor")
    count = lax.axis_size(DP)
    cols, hid = w_query.shape[1], w_gate.shape[1]
    share = width // count
    edge = 5 * cols // 3
    bq, bk = rows, rows // 2
    blocks = slots // bq

    packed = jnp.concatenate([w_gate, w_up, w_down.T, w_out.T], axis=1)
    feed_w = lax.all_gather(packed, ("tensor",) + DP, axis=0, tiled=True)
    feed_w = feed_w.reshape(2, width, packed.shape[1])
    full_qkv = gather_rows(jnp.concatenate([w_query, w_key, w_value], axis=1), edge)
    other_x = exchange(tokens)

    index = jnp.arange(slots, dtype=jnp.int32)
    row = lengths[0]
    ends = jnp.cumsum(row)
    begins = jnp.sum(jnp.where(index[:, None] >= ends[None, :], row[None, :], 0), axis=1)
    position = (index - begins).astype(F32)
    lane = jnp.arange(PAIR, dtype=jnp.int32) % HEAD
    inverse = ROPE_BASE ** (-((lane % (HEAD // 2)).astype(F32) * 2.0 / HEAD))
    angle = position[:, None] * inverse[None, :]
    cosine = jnp.cos(angle)
    sine = jnp.where(lane[None, :] < HEAD // 2, -jnp.sin(angle), jnp.sin(angle))
    sched = jnp.concatenate([
        jnp.stack([me.astype(jnp.int32), ends[-1]]),
        begins[::bq] // bk,
        begins[::bq] // (bk // 2),
    ])
    start = begins.reshape(1, slots)

    qkv, mixed_send, mixed_own, lse = attend_forward(
        sched, tokens, other_x, full_qkv, cosine, sine, start, bq, bk)
    mixed_oth = exchange(mixed_send)
    output, d_first, g_own, g_send, grads, gains = feed(
        sched, tokens, mixed_own, mixed_oth, cotangent, feed_w, gain_attn.reshape(1, width),
        gain_ffn.reshape(1, width), hid, share, lax.axis_size("near"))
    g_oth = exchange(g_send)
    reduced = lax.psum_scatter(grads, ("tensor", "near"), scatter_dimension=0, tiled=True)
    reduced = lax.psum_scatter(reduced, "far", scatter_dimension=0, tiled=True)
    gains = gains[:2] + exchange(gains[:2])
    d_qkv, dw = attend_backward(sched, qkv, cosine, sine, start, lse, mixed_send, mixed_own,
                                g_oth, g_own, tokens, other_x, bq, bk // 2)
    dw, gains = lax.optimization_barrier((dw, gains))
    fore, back = bit_orders(count)
    for bit in fore[::-1]:
        gains = gains + flip(gains, bit)
    dw = jnp.concatenate([scatter_rows(dw[:, :edge], fore[::-1]),
                          scatter_rows(dw[:, edge:], back[::-1])], axis=1).astype(F32)
    dw = dw.reshape(share, cols // PAIR, 3, PAIR)
    x_send, x_own = input_grads(sched, d_qkv, full_qkv, d_first, 512)
    input_grad = (x_own + exchange(x_send).astype(F32)).astype(BF16)
    grad_gate, grad_up, grad_down, grad_out = finish(reduced, hid)
    return (
        output,
        input_grad,
        dw[:, :, 0].reshape(share, cols),
        dw[:, :, 1].reshape(share, cols),
        dw[:, :, 2].reshape(share, cols),
        grad_out,
        grad_gate,
        grad_up,
        grad_down,
        gains[0],
        gains[1],
    )


def solution(mesh):
    count, pair = mesh.shape["dp"], mesh.shape["tensor"]
    near = min(4, count)
    mesh = Mesh(mesh.devices.reshape(count // near, near, pair), DP + ("tensor",))
    split = P(DP, "tensor")
    turned = P("tensor", DP)
    slots = P(DP + ("tensor",), None)
    return jax.shard_map(
        local,
        mesh=mesh,
        in_specs=(slots, split, split, split, turned, split, split, turned, P(), P(),
                  P(DP, None), slots),
        out_specs=(slots, slots, split, split, split, turned, split, split, turned, P(), P()),
        check_vma=False,
    )
```

```python
from functools import partial

import jax
import jax.numpy as jnp
from jax import lax
from jax.experimental import pallas as pl
from jax.experimental.pallas import tpu as pltpu
from jax.sharding import Mesh
from jax.sharding import PartitionSpec as P

HEAD = 64
PAIR = 2 * HEAD
EPS = 1e-05
ROPE_BASE = 10000.0
NEGATIVE = -1e30
F32 = jnp.float32
BF16 = jnp.bfloat16
VMEM_LIMIT = 56 * 1024 * 1024
DP = ("far", "near")
EXTRA = 16
SIDE, TOTAL, BIT_X, BIT_Y, FAR, LOWS = range(6)


def mm(left, right):
    return jnp.dot(left, right, preferred_element_type=F32)


def rdot(left, right):
    return lax.dot_general(left, right, (((1,), (1,)), ((), ())), preferred_element_type=F32)


def tdot(left, right):
    return lax.dot_general(left, right, (((0,), (0,)), ((), ())), preferred_element_type=F32)


def params(limit=VMEM_LIMIT, dims=1):
    return pltpu.CompilerParams(
        vmem_limit_bytes=limit, dimension_semantics=("arbitrary",) * dims
    )


def cost(flops, nbytes, trans=0):
    return pl.CostEstimate(flops=int(flops), bytes_accessed=int(nbytes), transcendentals=int(trans))


def swap_halves(values):
    lane = lax.broadcasted_iota(jnp.int32, values.shape, 1) % HEAD
    half = HEAD // 2
    width = values.shape[1]
    return jnp.where(
        lane < half, pltpu.roll(values, width - half, 1), pltpu.roll(values, half, 1)
    )


def head_masks(values):
    return one_head(values, 0), one_head(values, 1)


def one_head(values, h):
    lane = lax.broadcasted_iota(jnp.int32, (1, PAIR), 1)
    return values * (lane // HEAD == h).astype(values.dtype)


def forward_kernel(sched, own_x_ref, oth_x_ref, wq_ref, wk_ref, wv_ref, cos_ref, sin_ref, start_ref,
                   qkv_ref, oth_ref, own_ref, lse_ref, acc_ref, vt_ref, *, bq, bk, sub, chunk, blocks):
    step = pl.program_id(1)
    half = blocks // 2
    i = lax.rem(step + (1 - sched[0]) * half, blocks)

    @pl.when(step == 0)
    def _():
        local = own_x_ref.shape[0]
        weights = jnp.concatenate([wq_ref[...], wk_ref[...], wv_ref[...]], axis=1)
        for x_ref, side in ((own_x_ref, sched[0]), (oth_x_ref, 1 - sched[0])):
            for r in range(0, local, chunk):
                here = pl.ds(pl.multiple_of(side * local + r, chunk), chunk)
                u = mm(x_ref[r:r + chunk, :], weights)
                cosine, sine = cos_ref[here, :], sin_ref[here, :]
                for n, scale in ((0, HEAD ** -0.5), (1, 1.0)):
                    piece = u[:, n * PAIR:(n + 1) * PAIR]
                    turned = piece * cosine + swap_halves(piece) * sine
                    qkv_ref[here, n * PAIR:(n + 1) * PAIR] = (turned * scale).astype(BF16)
                v = u[:, 2 * PAIR:]
                qkv_ref[here, 2 * PAIR:] = v.astype(BF16)
                vt_ref[:, here] = v.T.astype(BF16)

    start = start_ref[...]
    acc_ref[...] = jnp.zeros_like(acc_ref)
    streams = list(range(0, bq, sub))

    @pl.loop(0, 2)
    def _(h):
        queries = one_head(qkv_ref[pl.ds(pl.multiple_of(i * bq, bq), bq), 0:PAIR], h)
        rows = pl.ds(pl.multiple_of(h * HEAD, HEAD), HEAD)

        def visit(j, carry, last):
            at = pl.multiple_of(i * bq if last else j * bk, bk)
            scores, out = [], []
            for c in streams:
                size = c + sub if last else bk
                s = rdot(qkv_ref[pl.ds(at, size), PAIR:2 * PAIR], queries[c:c + sub])
                key_index = lax.broadcasted_iota(jnp.int32, (size, sub), 0)
                allowed = key_index >= start[:, c:c + sub] - at
                if last:
                    query_index = c + lax.broadcasted_iota(jnp.int32, (size, sub), 1)
                    allowed = allowed & (key_index <= query_index)
                scores.append(jnp.where(allowed, s, NEGATIVE))
            for n, c in enumerate(streams):
                size = c + sub if last else bk
                peak, total = carry[2 * n], carry[2 * n + 1]
                new_peak = jnp.maximum(peak, jnp.max(scores[n], axis=0, keepdims=True))
                fade = jnp.exp(peak - new_peak)
                expo = jnp.exp(scores[n] - new_peak)
                total = total * fade + jnp.sum(expo, axis=0, keepdims=True)
                cols = slice(c, c + sub)
                acc_ref[rows, cols] = acc_ref[rows, cols] * fade + mm(
                    vt_ref[rows, pl.ds(at, size)], expo.astype(BF16)
                )
                out += [new_peak, total]
            return tuple(out)

        carry = (jnp.full((1, sub), NEGATIVE, F32), jnp.zeros((1, sub), F32)) * len(streams)
        carry = lax.fori_loop(sched[LOWS + i], i * (bq // bk), lambda j, c: visit(j, c, False), carry)
        carry = visit(None, carry, True)
        for n, c in enumerate(streams):
            peak, total = carry[2 * n], carry[2 * n + 1]
            cols = slice(c, c + sub)
            acc_ref[rows, cols] = acc_ref[rows, cols] / total
            lse_ref[pl.ds(h, 1), cols] = peak + jnp.log(total)

    mixed = acc_ref[...].T.astype(BF16)

    @pl.when(step < half)
    def _():
        oth_ref[...] = mixed

    @pl.when(step >= half)
    def _():
        own_ref[...] = mixed


def placing(blocks):
    half = blocks // 2

    def place(n, sched):
        return lax.rem(n + (1 - sched[0]) * half, blocks)

    return place, half


def attend_forward(sched, own_x, oth_x, weights, cosine, sine, start, bq, bk, sub=256, chunk=512):
    local, width = own_x.shape
    slots, cols = 2 * local, weights.shape[1] // 3
    pairs, blocks = cols // PAIR, slots // bq
    place, half = placing(blocks)
    rows = pl.BlockSpec((local, width), lambda p, n, s: (0, 0), pipeline_mode=pl.Buffered(1))
    table = pl.BlockSpec((slots, PAIR), lambda p, n, s: (0, 0), pipeline_mode=pl.Buffered(1))
    return pl.pallas_call(
        partial(forward_kernel, bq=bq, bk=bk, sub=sub, chunk=chunk, blocks=blocks),
        grid_spec=pltpu.PrefetchScalarGridSpec(
            num_scalar_prefetch=1,
            grid=(pairs, blocks),
            in_specs=[
                rows, rows,
                *[pl.BlockSpec((width, PAIR), lambda p, n, s, at=at: (0, at + p))
                  for at in (0, pairs, 2 * pairs)],
                table, table,
                pl.BlockSpec((1, bq), lambda p, n, s: (0, place(n, s))),
            ],
            out_specs=[
                pl.BlockSpec((slots, 3 * PAIR), lambda p, n, s: (0, p)),
                pl.BlockSpec((bq, PAIR), lambda p, n, s: (jnp.minimum(n, half - 1), p)),
                pl.BlockSpec((bq, PAIR), lambda p, n, s: (jnp.maximum(n - half, 0), p)),
                pl.BlockSpec((None, 2, bq), lambda p, n, s: (p, 0, place(n, s))),
            ],
            scratch_shapes=[pltpu.VMEM((PAIR, bq), F32), pltpu.VMEM((PAIR, slots), BF16)],
        ),
        out_shape=[
            jax.ShapeDtypeStruct((slots, 3 * cols), BF16),
            jax.ShapeDtypeStruct((local, cols), BF16),
            jax.ShapeDtypeStruct((local, cols), BF16),
            jax.ShapeDtypeStruct((pairs, 2, slots), F32),
        ],
        compiler_params=params(dims=2),
        cost_estimate=cost(4 * slots * slots * cols + 6 * slots * width * cols,
                           16 * slots * cols, slots * slots * 6),
        name="attend_forward",
    )(sched, own_x, oth_x, weights, weights, weights, cosine, sine, start)


def backward_kernel(sched, q_ref, k_ref, v_ref, cos_ref, sin_ref, start_ref, lse_ref,
                    o_oth_ref, o_own_ref, g_oth_ref, g_own_ref, x_own_ref, x_oth_ref,
                    gains_ref, all_ref, *rest, bq, bk, sub, blocks, share):
    step = pl.program_id(1)
    half = blocks // 2
    i = lax.rem(step + (1 - sched[0]) * half, blocks)

    dw_refs, (dq_acc, dkt_acc, dvt_acc) = rest[:-3], rest[-3:]

    @pl.when(step == 0)
    def _():
        dkt_acc[...] = jnp.zeros_like(dkt_acc)
        dvt_acc[...] = jnp.zeros_like(dvt_acc)

    first = step < half
    grads = jnp.where(first, g_oth_ref[...], g_own_ref[...])
    mixed = jnp.where(first, o_oth_ref[...], o_own_ref[...])
    queries = head_masks(q_ref[...])
    couts = head_masks(grads)
    query_t = q_ref[...].astype(F32).T.astype(BF16)
    cout_t = grads.astype(F32).T.astype(BF16)
    begin = jnp.broadcast_to(start_ref[...], (PAIR, bq)).T
    product = grads.astype(F32) * mixed.astype(F32)
    big = product.astype(BF16)
    small = (product - big.astype(F32)).astype(BF16)
    row = lax.broadcasted_iota(jnp.int32, (PAIR, 2 * PAIR), 0)
    lane = lax.broadcasted_iota(jnp.int32, (PAIR, 2 * PAIR), 1)
    pick = jnp.where(row // HEAD == lane // PAIR, 1.0, 0.0).astype(BF16)
    inner = mm(big, pick) + mm(small, pick)
    lse = [jnp.broadcast_to(lse_ref[h:h + 1, :], (PAIR, bq)).T for h in range(2)]
    dq_acc[...] = jnp.zeros_like(dq_acc)

    def wide(value, size):
        return jnp.concatenate([value] * (size // PAIR), axis=1)

    def visit(j, last):
        at = pl.multiple_of(i * bq if last else j * bk, bk)
        streams = [(c, h) for c in range(0, bq, sub) for h in range(2)]

        def scores(n):
            c, h = streams[n]
            size = c + sub if last else bk
            where = pl.ds(at, size)
            rows = slice(c, c + sub)
            return rdot(queries[h][rows], k_ref[where, :]), rdot(couts[h][rows], v_ref[where, :])

        def absorb(n, pair):
            c, h = streams[n]
            raw, d_probs = pair
            size = c + sub if last else bk
            where = pl.ds(at, size)
            rows = slice(c, c + sub)
            lanes = slice(h * HEAD, (h + 1) * HEAD)
            probs = jnp.exp(raw - wide(lse[h][rows], size))
            key_index = lax.broadcasted_iota(jnp.int32, (sub, size), 1)
            allowed = key_index >= wide(begin[rows], size) - at
            if last:
                query_index = c + lax.broadcasted_iota(jnp.int32, (sub, size), 0)
                allowed = allowed & (key_index <= query_index)
            probs = jnp.where(allowed, probs, 0.0)
            d_scores = (probs * (d_probs - wide(inner[rows, h * PAIR:(h + 1) * PAIR], size))).astype(BF16)
            dvt_acc[lanes, where] += mm(cout_t[lanes, rows], probs.astype(BF16))
            dkt_acc[lanes, where] += mm(query_t[lanes, rows], d_scores)
            dq_acc[rows, :] += mm(d_scores, head_masks(k_ref[where, :])[h])

        ready = scores(0)
        for n in range(len(streams)):
            held = ready
            if n + 1 < len(streams):
                ready = scores(n + 1)
            absorb(n, held)

    @pl.loop(sched[LOWS + blocks + i], i * (bq // bk))
    def _(j):
        visit(j, False)

    visit(None, True)

    def unrotate(g, cosine, sine):
        return g * cosine - swap_halves(g) * sine

    here = pl.ds(pl.multiple_of(i * bq, bq), bq)
    dq = unrotate(dq_acc[...] * (HEAD ** -0.5), cos_ref[here, :], sin_ref[here, :])
    all_ref[here, 0:PAIR] = dq.astype(BF16)

    @pl.when(step == blocks - 1)
    def _():
        dk = unrotate(dkt_acc[...].T, cos_ref[...], sin_ref[...])
        all_ref[:, PAIR:2 * PAIR] = dk.astype(BF16)
        all_ref[:, 2 * PAIR:] = dvt_acc[...].T.astype(BF16)
        local = x_own_ref.shape[0]
        mine = pl.ds(pl.multiple_of(sched[0] * local, local), local)
        other = pl.ds(pl.multiple_of((1 - sched[0]) * local, local), local)
        total = (tdot(x_own_ref[...], all_ref[mine, :])
                 + tdot(x_oth_ref[...], all_ref[other, :])).astype(BF16)
        if share is None:
            dw_refs[0][...] = total
        else:
            part_rows(total, gains_ref[...], sched[BIT_X], sched[BIT_Y], *dw_refs, share)


def encode(value):
    high = value.astype(BF16)
    rest = value - high.astype(F32)
    middle = rest.astype(BF16)
    low = (rest - middle.astype(F32)).astype(BF16)
    rows, cols = value.shape
    pieces = [piece.astype(F32) for piece in (high, middle, low)]
    return jnp.concatenate(pieces + [jnp.zeros((EXTRA - 3 * rows, cols), F32)], axis=0).astype(BF16)


def decode(rows, count=2):
    wide = rows.astype(F32)
    return wide[0:count] + wide[count:2 * count] + wide[2 * count:3 * count]


def part_rows(total, gains, bit_x, bit_y, keep_a, send_a, keep_b, send_b, share):
    def block(z, y, x):
        at = (4 * z + 2 * y + x) * share
        return total[at:at + share]

    pieces = keep_a.shape[0] // share
    for n in range(pieces):
        z, side, here = 2 * (n // 2), n % 2, slice(n * share, (n + 1) * share)
        zero, one = block(z, side, 0), block(z, side, 1)
        keep_a[here] = jnp.where(bit_x == 0, zero, one)
        send_a[here] = jnp.where(bit_x == 0, one, zero)
        zero, one = block(z + 1, 0, side), block(z + 1, 1, side)
        keep_b[here] = jnp.where(bit_y == 0, zero, one)
        send_b[here] = jnp.where(bit_y == 0, one, zero)
    send_a[pieces * share:] = encode(gains)


def attend_backward(sched, qkv, cosine, sine, start, lse, o_oth, o_own, g_oth, g_own, x_own, x_oth,
                    gains, bq, bk, share, sub=256):
    slots, cols = qkv.shape[0], qkv.shape[1] // 3
    pairs, blocks = cols // PAIR, slots // bq
    local, width = x_own.shape
    place, half = placing(blocks)
    table = pl.BlockSpec((slots, PAIR), lambda p, n, s: (0, 0), pipeline_mode=pl.Buffered(1))
    rows = pl.BlockSpec((local, width), lambda p, n, s: (0, 0), pipeline_mode=pl.Buffered(1))
    oth = pl.BlockSpec((bq, PAIR), lambda p, n, s: (jnp.minimum(n, half - 1), p))
    own = pl.BlockSpec((bq, PAIR), lambda p, n, s: (jnp.maximum(n - half, 0), p))
    if share is None:
        dw_specs = [pl.BlockSpec((width, 3 * PAIR), lambda p, n, s: (0, p))]
        dw_shapes = [(width, 3 * cols)]
    else:
        rows_out = [width // 4, width // 4 + EXTRA, width // 4, width // 4]
        dw_specs = [pl.BlockSpec((size, 3 * PAIR), lambda p, n, s: (0, p)) for size in rows_out]
        dw_shapes = [(size, 3 * cols) for size in rows_out]
    return pl.pallas_call(
        partial(backward_kernel, bq=bq, bk=bk, sub=sub, blocks=blocks, share=share),
        grid_spec=pltpu.PrefetchScalarGridSpec(
            num_scalar_prefetch=1,
            grid=(pairs, blocks),
            in_specs=[
                pl.BlockSpec((bq, PAIR), lambda p, n, s: (place(n, s), 3 * p)),
                pl.BlockSpec((slots, PAIR), lambda p, n, s: (0, 3 * p + 1)),
                pl.BlockSpec((slots, PAIR), lambda p, n, s: (0, 3 * p + 2)),
                table, table,
                pl.BlockSpec((1, bq), lambda p, n, s: (0, place(n, s))),
                pl.BlockSpec((None, 2, bq), lambda p, n, s: (p, 0, place(n, s))),
                oth, own, oth, own, rows, rows,
                pl.BlockSpec((2, 3 * PAIR), lambda p, n, s: (0, p)),
            ],
            out_specs=[pl.BlockSpec((slots, 3 * PAIR), lambda p, n, s: (0, p)), *dw_specs],
            scratch_shapes=[
                pltpu.VMEM((bq, PAIR), F32),
                pltpu.VMEM((PAIR, slots), F32),
                pltpu.VMEM((PAIR, slots), F32),
            ],
        ),
        out_shape=[jax.ShapeDtypeStruct(shape, BF16) for shape in [(slots, 3 * cols), *dw_shapes]],
        compiler_params=params(dims=2),
        cost_estimate=cost(10 * slots * slots * cols + 6 * slots * width * cols,
                           20 * slots * cols, slots * slots * 6),
        name="attend_backward",
    )(sched, qkv, qkv, qkv, cosine, sine, start, lse, o_oth, o_own, g_oth, g_own, x_own, x_oth, gains)


def feed_kernel(sched, x_ref, own_ref, oth_ref, dy_ref, w_hbm, ga_ref, gf_ref,
                out_ref, dfirst_ref, gown_ref, goth_ref, grads_ref, gains_ref,
                w_ref, keep_a, keep_b, total_s, right_s, left_s, dattn_s, mixed_s,
                sems, *, block, sub, chunk, local, hid, head_cols, parts, share):
    step = pl.program_id(0)
    me = sched[0]
    steps = local // block
    outs = slice(3 * hid, 3 * hid + head_cols)
    pieces = [(slice(3 * hid, w_ref.shape[2]), None), (slice(0, 2 * hid), 0), (slice(0, 2 * hid), 1),
              (slice(2 * hid, 3 * hid), None)]

    def piece(n):
        cols, t = pieces[n]
        at = (slice(None), slice(None), cols) if t is None else (t, slice(None), cols)
        return pltpu.make_async_copy(w_hbm.at[at], w_ref.at[at], sems.at[n])

    @pl.when(step == 0)
    def _():
        for n in range(len(pieces)):
            piece(n).start()
        gains_ref[...] = jnp.zeros_like(gains_ref)

    def arrive(n):
        @pl.when(step == 0)
        def _():
            piece(n).wait()

    @pl.when(step < steps)
    def _():
        subs = list(range(0, block, sub))
        base = pl.multiple_of(step * block, block)
        arrive(0)
        attn, rms1, unit1, normed, normed_b = {}, {}, {}, {}, {}
        for r in subs:
            rows = slice(r, r + sub)
            attn[r] = rdot(own_ref[rows, :], w_ref[me, :, outs]) + rdot(oth_ref[rows, :], w_ref[1 - me, :, outs])
        for r in subs:
            rows = slice(r, r + sub)
            here = pl.ds(base + r, sub)
            first = x_ref[rows, :].astype(F32) + attn[r]
            rms1[r] = lax.rsqrt(jnp.mean(first * first, axis=-1, keepdims=True) + EPS)
            unit1[r] = first * rms1[r]
            normed[r] = unit1[r] * ga_ref[...]
            normed_b[r] = normed[r].astype(BF16)
            left_s[0, here, :] = normed_b[r]
            mixed_s[here, :] = jnp.concatenate([own_ref[rows, :], oth_ref[rows, :]], axis=1)
        total_s[...] = jnp.zeros_like(total_s)

        @pl.loop(0, 2)
        def _(t):
            for at, count in ((0, 1), (0, 3), (1, 2)):
                @pl.when((step == 0) & (t == at))
                def _():
                    piece(count).wait()

            for c in range(0, hid, chunk):
                cols = pl.ds(pl.multiple_of(t * hid + c, chunk), chunk)
                hid_b = {}
                for r in subs:
                    rows = slice(r, r + sub)
                    gate = mm(normed_b[r], w_ref[t, :, c:c + chunk])
                    upper = mm(normed_b[r], w_ref[t, :, hid + c:hid + c + chunk])
                    sigma = 1.0 / (1.0 + jnp.exp(-gate))
                    silu = gate * sigma
                    hid_b[r] = (silu * upper).astype(BF16)
                    keep_a[rows, cols] = silu
                    keep_b[rows, cols] = upper * (sigma + silu * (1.0 - sigma))
                    right_s[2, pl.ds(base + r, sub), cols] = hid_b[r]
                for r in subs:
                    total_s[r:r + sub, :] += rdot(hid_b[r], w_ref[t, :, 2 * hid + c:2 * hid + c + chunk])

        d_second, d_ffn = {}, {}
        for r in subs:
            rows = slice(r, r + sub)
            here = pl.ds(base + r, sub)
            second = normed[r] + total_s[rows, :]
            rms2 = lax.rsqrt(jnp.mean(second * second, axis=-1, keepdims=True) + EPS)
            unit2 = second * rms2
            slot = me * local + base + r + lax.broadcasted_iota(jnp.int32, (sub, 1), 0)
            valid = slot < sched[1]
            out_ref[rows, :] = jnp.where(valid, unit2 * gf_ref[...], 0.0).astype(BF16)
            dy = jnp.where(valid, dy_ref[rows, :].astype(F32), 0.0)
            gains_ref[1:2, :] += jnp.sum(dy * unit2, axis=0, keepdims=True)
            scaled = dy * gf_ref[...]
            d_second[r] = rms2 * (scaled - unit2 * jnp.mean(scaled * unit2, axis=-1, keepdims=True))
            d_ffn[r] = d_second[r].astype(BF16)
            left_s[1, here, :] = d_ffn[r]
            total_s[rows, :] = d_second[r]

        @pl.loop(0, 2)
        def _(t):
            for c in range(0, hid, chunk):
                cols = pl.ds(pl.multiple_of(t * hid + c, chunk), chunk)
                dg, du = {}, {}
                for r in subs:
                    rows, here = slice(r, r + sub), pl.ds(base + r, sub)
                    d_hidden = mm(d_ffn[r], w_ref[t, :, 2 * hid + c:2 * hid + c + chunk])
                    dg[r] = (d_hidden * keep_b[rows, cols]).astype(BF16)
                    du[r] = (d_hidden * keep_a[rows, cols]).astype(BF16)
                    right_s[0, here, cols] = dg[r]
                    right_s[1, here, cols] = du[r]
                for r in subs:
                    total_s[r:r + sub, :] += rdot(dg[r], w_ref[t, :, c:c + chunk]) + rdot(
                        du[r], w_ref[t, :, hid + c:hid + c + chunk])

        for r in subs:
            rows = slice(r, r + sub)
            here = pl.ds(base + r, sub)
            d_normed = total_s[rows, :]
            gains_ref[0:1, :] += jnp.sum(d_normed * unit1[r], axis=0, keepdims=True)
            scaled = d_normed * ga_ref[...]
            d_first = rms1[r] * (scaled - unit1[r] * jnp.mean(scaled * unit1[r], axis=-1, keepdims=True))
            dfirst_ref[rows, :] = d_first
            d_attn = d_first.astype(BF16)
            dattn_s[here, :] = d_attn
            gown_ref[rows, :] = mm(d_attn, w_ref[me, :, outs]).astype(BF16)
            goth_ref[rows, :] = mm(d_attn, w_ref[1 - me, :, outs]).astype(BF16)

    @pl.when(step >= steps)
    def _():
        tile = step - steps
        t, part = lax.div(tile, parts), lax.rem(tile, parts)
        size = dattn_s.shape[1] // parts
        rows = pl.ds(pl.multiple_of(part * size, size), size)
        cols = pl.ds(pl.multiple_of(t * hid, hid), hid)

        def store(value, there):
            if share is None:
                grads_ref[0, :, there] = value
            else:
                near = grads_ref.shape[1]
                for n in range(size // share):
                    grads_ref[0, n % near, n // near, :, there] = value[n * share:(n + 1) * share]

        for n in range(3):
            left = left_s[n // 2, :, rows]
            store(tdot(left, right_s[n, :, cols]).astype(BF16), slice(n * hid, (n + 1) * hid))

        mixed = jnp.where(t == me, mixed_s[:, :head_cols], mixed_s[:, head_cols:])
        store(tdot(dattn_s[:, rows], mixed).astype(BF16), slice(3 * hid, 3 * hid + head_cols))


def feed(sched, x, own, oth, dy, weights, gain_attn, gain_ffn, hid, share, near,
         block=512, sub=256, chunk=512, parts=2):
    local, width = x.shape
    head_cols = own.shape[1]
    total = weights.shape[2]
    steps = local // block
    packed = share % 16 == 0

    def at(s):
        return jnp.minimum(s, steps - 1)

    rows = pl.BlockSpec((block, width), lambda s, sched: (at(s), 0))
    heads = pl.BlockSpec((block, head_cols), lambda s, sched: (at(s), 0))
    gain = pl.BlockSpec((1, width), lambda s, sched: (0, 0))

    def tile(s, sched):
        n = jnp.maximum(s - steps, 0)
        if packed:
            return (lax.div(n, parts), 0, lax.rem(n, parts), 0, 0)
        return (lax.div(n, parts), lax.rem(n, parts), 0)

    if packed:
        grads_shape = (2, near, width // (near * share), share, total)
        grads_block = (1, near, width // (near * share * parts), share, total)
    else:
        grads_shape, grads_block = (2, width, total), (1, width // parts, total)

    def shape(cols, dtype):
        return jax.ShapeDtypeStruct((local, cols), dtype)

    results = pl.pallas_call(
        partial(feed_kernel, block=block, sub=sub, chunk=chunk, local=local, hid=hid,
                head_cols=head_cols, parts=parts, share=share if packed else None),
        grid_spec=pltpu.PrefetchScalarGridSpec(
            num_scalar_prefetch=1,
            grid=(steps + 2 * parts,),
            in_specs=[rows, heads, heads, rows, pl.BlockSpec(memory_space=pl.ANY), gain, gain],
            out_specs=[rows, rows, heads, heads,
                       pl.BlockSpec(grads_block, tile),
                       pl.BlockSpec((16, width), lambda s, sched: (0, 0))],
            scratch_shapes=[pltpu.VMEM(weights.shape, BF16)]
            + [pltpu.VMEM((block, 2 * hid), F32)] * 2
            + [pltpu.VMEM((block, width), F32)]
            + [pltpu.VMEM((3, local, 2 * hid), BF16), pltpu.VMEM((2, local, width), BF16)]
            + [pltpu.VMEM((local, width), BF16)]
            + [pltpu.VMEM((local, 2 * head_cols), BF16), pltpu.SemaphoreType.DMA((4,))],
        ),
        out_shape=[
            shape(width, BF16), shape(width, F32), shape(head_cols, BF16), shape(head_cols, BF16),
            jax.ShapeDtypeStruct(grads_shape, BF16),
            jax.ShapeDtypeStruct((16, width), F32),
        ],
        compiler_params=params(60 * 1024 * 1024),
        cost_estimate=cost(12 * local * width * total, 30 * local * width),
        name="feed",
    )(sched, x, own, oth, dy, weights, gain_attn, gain_ffn)
    grads = results[4]
    if not packed:
        grads = grads.reshape(2, -1, near, share, total).swapaxes(1, 2)
    return (*results[:4], grads.reshape(-1, total), results[5])


def input_grad_kernel(sched, d_ref, w_ref, dfirst_ref, oth_ref, own_ref, *, half):
    step = pl.program_id(0)
    cols = d_ref.shape[1]
    order = [at + n * PAIR for n in range(3) for at in range(0, cols, 3 * PAIR)]
    part = rdot(jnp.concatenate([d_ref[:, at:at + PAIR] for at in order], axis=1), w_ref[...])

    @pl.when(step < half)
    def _():
        oth_ref[...] = part.astype(BF16)

    @pl.when(step >= half)
    def _():
        own_ref[...] = dfirst_ref[...] + part


def input_grads(sched, d_qkv, weights, d_first, block):
    local, width = d_first.shape
    cols = d_qkv.shape[1]
    half = local // block
    place, _ = placing(2 * half)
    own = pl.BlockSpec((block, width), lambda n, s: (jnp.maximum(n - half, 0), 0))
    return pl.pallas_call(
        partial(input_grad_kernel, half=half),
        grid_spec=pltpu.PrefetchScalarGridSpec(
            num_scalar_prefetch=1,
            grid=(2 * half,),
            in_specs=[pl.BlockSpec((block, cols), lambda n, s: (place(n, s), 0)),
                      pl.BlockSpec((width, cols), lambda n, s: (0, 0)), own],
            out_specs=[pl.BlockSpec((block, width), lambda n, s: (jnp.minimum(n, half - 1), 0)), own],
        ),
        out_shape=[jax.ShapeDtypeStruct((local, width), BF16),
                   jax.ShapeDtypeStruct((local, width), F32)],
        compiler_params=params(),
        cost_estimate=cost(4 * local * width * cols, 4 * local * (width + cols)),
        name="input_grads",
    )(sched, d_qkv, weights, d_first)


def finish_kernel(total_ref, gate_ref, up_ref, down_ref, out_ref):
    hid = gate_ref.shape[1]
    gate_ref[...] = total_ref[:, 0:hid].astype(F32)
    up_ref[...] = total_ref[:, hid:2 * hid].astype(F32)
    down_ref[...] = total_ref[:, 2 * hid:3 * hid].astype(F32)
    out_ref[...] = total_ref[:, 3 * hid:].astype(F32)


def finish(total, hid):
    share, cols = total.shape
    gate, up, down, out = pl.pallas_call(
        finish_kernel,
        out_shape=[jax.ShapeDtypeStruct((share, width), F32)
                   for width in (hid, hid, hid, cols - 3 * hid)],
        cost_estimate=cost(0, 6 * share * cols),
        name="finish",
    )(total)
    return gate, up, down.T, out.T


def whole_call(kernel, name, sched, values, shapes):
    whole = pl.BlockSpec(memory_space=pltpu.VMEM)
    size = 4 * sum(value.size for value in values)
    return pl.pallas_call(
        kernel,
        in_specs=[pl.BlockSpec(memory_space=pltpu.SMEM)] + [whole] * len(values),
        out_specs=[whole] * len(shapes),
        out_shape=[jax.ShapeDtypeStruct(shape, dtype) for shape, dtype in shapes],
        compiler_params=pltpu.CompilerParams(vmem_limit_bytes=32 * 1024 * 1024),
        cost_estimate=cost(0, size),
        name=name,
    )(sched, *values)


def add(left, right):
    return left.astype(F32) + right.astype(F32)


def near_kernel(sched, keep_a, got_a, keep_b, got_b, gains, next_a, send_a, next_b, send_b, total,
                *, share):
    size = next_a.shape[0]
    for held, got, bit, stay, go in ((keep_a, got_a, sched[BIT_Y], next_a, send_a),
                                     (keep_b, got_b, sched[BIT_X], next_b, send_b)):
        for n in range(size // share):
            here = slice(n * share, (n + 1) * share)
            mine = pl.ds(pl.multiple_of((2 * n + bit) * share, share), share)
            other = pl.ds(pl.multiple_of((2 * n + 1 - bit) * share, share), share)
            stay[here] = add(held[mine], got[mine]).astype(BF16)
            go[here] = add(held[other], got[other]).astype(BF16)
    total[...] = gains[...] + decode(got_a[2 * size:])
    send_a[size:] = encode(total[...])


def far_kernel(sched, keep_a, got_a, keep_b, got_b, gains, own, total, *sends):
    far, share = 1 + len(sends), own.shape[0]
    sums = []
    for n in range(far // 2):
        here = slice(n * share, (n + 1) * share)
        sums += [add(keep_a[here], got_a[here]), add(keep_b[here], got_b[here])]
    total[...] = gains[...] + decode(got_a[keep_a.shape[0]:])
    for shift in range(far):
        at = lax.rem(sched[FAR] + shift, far)
        value = sums[0]
        for n in range(1, far):
            value = jnp.where(at == n, sums[n], value)
        if shift == 0:
            own[...] = value
        else:
            sends[shift - 1][:share] = value.astype(BF16)
            sends[shift - 1][share:] = encode(total[...])


def last_kernel(sched, own, gains, *rest):
    got, outs, total = rest[:-4], rest[-4:-1], rest[-1]
    value, share, far = own[...], own.shape[0], 1 + len(rest[:-4])
    arrived = [gains[...]]
    for piece in got:
        value = value + piece[:share].astype(F32)
        arrived.append(decode(piece[share:]))
    for at in range(0, value.shape[1], PAIR):
        pair, part = at // PAIR // 3, at // PAIR % 3
        outs[part][:, pair * PAIR:(pair + 1) * PAIR] = value[:, at:at + PAIR]
    summed = None
    for n in range(far):
        shift = lax.rem(sched[FAR] - n + far, far)
        term = arrived[0]
        for k in range(1, far):
            term = jnp.where(shift == k, arrived[k], term)
        summed = term if summed is None else summed + term
    total[...] = summed


def shifted(value, shift):
    far = lax.axis_size("far")
    return lax.ppermute(value, "far", [(at, (at + shift) % far) for at in range(far)])


def sum_parts(sched, share, keep_a, send_a, keep_b, send_b, gains, beside, late):
    size, width = keep_a.shape
    far = lax.axis_size("far")
    send_a, send_b, beside, late = lax.optimization_barrier((send_a, send_b, beside, late))
    got_a, got_b = flip(send_a, 0), flip(send_b, 1)
    sizes = [size // 2, size // 2 + EXTRA, size // 2, size // 2]
    keep_a, send_a, keep_b, send_b, gains = whole_call(
        partial(near_kernel, share=share), "near_sums", sched,
        (keep_a, got_a, keep_b, got_b, gains),
        [((rows, width), BF16) for rows in sizes] + [(gains.shape, F32)])
    got_a, got_b = flip(send_a, 1), flip(send_b, 0)
    own, gains, *sends = whole_call(
        far_kernel, "far_sums", sched, (keep_a, got_a, keep_b, got_b, gains),
        [((share, width), F32), (gains.shape, F32)] + [((share + EXTRA, width), BF16)] * (far - 1))
    got = [shifted(value, shift + 1) for shift, value in enumerate(sends)]
    *dw, gains = whole_call(last_kernel, "last_sums", sched, (own, gains, *got),
                            [((share, width // 3), F32)] * 3 + [(gains.shape, F32)])
    return dw, gains, beside, late


def exchange(value):
    return lax.ppermute(value, "tensor", [(0, 1), (1, 0)])


def flip(value, bit):
    count = lax.axis_size(DP)
    return lax.ppermute(value, DP, [(at, at ^ (1 << bit)) for at in range(count)])


def bit_orders(count):
    bits = count.bit_length() - 1
    low = list(range(min(2, bits)))
    high = list(range(min(2, bits), bits))
    return high[::-1] + low, high[::-1] + low[::-1]


def join(held, bit):
    other = flip(held, bit)
    mine = ((lax.axis_index(DP) >> bit) & 1) == 0
    return jnp.stack([jnp.where(mine, held, other), jnp.where(mine, other, held)])


def in_order(held, order):
    bits = len(order)
    rows, cols = held.shape[-2:]
    held = held.reshape((2,) * bits + (rows, cols))
    axes = [bits - 1 - order.index(bit) for bit in range(bits - 1, -1, -1)]
    return held.transpose(*axes, bits, bits + 1).reshape(-1, cols)


def gather_rows(piece, edge):
    fore, back = bit_orders(lax.axis_size(DP))
    high = len(fore) - min(2, len(fore))
    held = piece[None]
    for bit in fore[:high]:
        held = join(held, bit)
    parts = [held[..., :edge], held[..., edge:]]
    for one, two in zip(fore[high:], back[high:]):
        parts = [join(parts[0], one), join(parts[1], two)]
    return jnp.concatenate([in_order(parts[0], fore), in_order(parts[1], back)], axis=1)


def scatter_rows(total, order):
    me = lax.axis_index(DP)
    bits = len(order)
    rows, cols = total.shape[0] >> bits, total.shape[1]
    held = total.reshape((2,) * bits + (rows, cols))
    left = list(range(bits - 1, -1, -1))
    for bit in order:
        axis = left.index(bit)
        left.pop(axis)
        low = lax.index_in_dim(held, 0, axis, keepdims=False)
        high = lax.index_in_dim(held, 1, axis, keepdims=False)
        mine = ((me >> bit) & 1) == 0
        got = flip(jnp.where(mine, high, low), bit)
        held = (jnp.where(mine, low, high).astype(F32) + got.astype(F32)).astype(BF16)
    return held.reshape(rows, cols)


def local(tokens, w_query, w_key, w_value, w_out, w_gate, w_up, w_down, gain_attn, gain_ffn,
          lengths, cotangent):
    rows, width = tokens.shape
    slots = 2 * rows
    me = lax.axis_index("tensor")
    count = lax.axis_size(DP)
    cols, hid = w_query.shape[1], w_gate.shape[1]
    share = width // count
    edge = 5 * cols // 3
    bq, bk = rows, rows // 2
    blocks = slots // bq

    packed = jnp.concatenate([w_gate, w_up, w_down.T, w_out.T], axis=1)
    feed_w = lax.all_gather(packed, ("tensor",) + DP, axis=0, tiled=True)
    feed_w = feed_w.reshape(2, width, packed.shape[1])
    full_qkv = gather_rows(jnp.concatenate([w_query, w_key, w_value], axis=1), edge)
    other_x = exchange(tokens)

    near_at = lax.axis_index("near")
    index = jnp.arange(slots, dtype=jnp.int32)
    row = lengths[0]
    ends = jnp.cumsum(row)
    begins = jnp.sum(jnp.where(index[:, None] >= ends[None, :], row[None, :], 0), axis=1)
    position = (index - begins).astype(F32)
    lane = jnp.arange(PAIR, dtype=jnp.int32) % HEAD
    inverse = ROPE_BASE ** (-((lane % (HEAD // 2)).astype(F32) * 2.0 / HEAD))
    angle = position[:, None] * inverse[None, :]
    cosine = jnp.cos(angle)
    sine = jnp.where(lane[None, :] < HEAD // 2, -jnp.sin(angle), jnp.sin(angle))
    sched = jnp.concatenate([
        jnp.stack([me, ends[-1], near_at % 2, near_at // 2, lax.axis_index("far")]).astype(jnp.int32),
        begins[::bq] // bk,
        begins[::bq] // (bk // 2),
    ])
    start = begins.reshape(1, slots)

    qkv, mixed_send, mixed_own, lse = attend_forward(
        sched, tokens, other_x, full_qkv, cosine, sine, start, bq, bk)
    mixed_oth = exchange(mixed_send)
    output, d_first, g_own, g_send, grads, gains = feed(
        sched, tokens, mixed_own, mixed_oth, cotangent, feed_w, gain_attn.reshape(1, width),
        gain_ffn.reshape(1, width), hid, share, lax.axis_size("near"))
    g_oth = exchange(g_send)
    reduced = lax.psum_scatter(grads, ("tensor", "near"), scatter_dimension=0, tiled=True)
    gains = gains[:2] + exchange(gains[:2])
    parted = share % 16 == 0 and lax.axis_size("near") == 4 and lax.axis_size("far") % 2 == 0
    gains = jnp.pad(gains, ((0, 0), (0, 3 * cols - width)))
    d_qkv, *dw = attend_backward(sched, qkv, cosine, sine, start, lse, mixed_send, mixed_own,
                                 g_oth, g_own, tokens, other_x, gains, bq, bk // 2,
                                 share if parted else None)
    x_send, x_own = input_grads(sched, d_qkv, full_qkv, d_first, 512)
    if parted:
        dw, gains, x_own, reduced = sum_parts(sched, share, *dw, gains, x_own, reduced)
    else:
        fore, back = bit_orders(count)
        dw = jnp.concatenate([scatter_rows(dw[0][:, :edge], fore[::-1]),
                              scatter_rows(dw[0][:, edge:], back[::-1])], axis=1).astype(F32)
        dw = dw.reshape(share, cols // PAIR, 3, PAIR).transpose(2, 0, 1, 3).reshape(3, share, cols)
        for bit in range(count.bit_length() - 1):
            gains = gains + flip(gains, bit)
    reduced = lax.psum_scatter(reduced, "far", scatter_dimension=0, tiled=True)
    input_grad = (x_own + exchange(x_send).astype(F32)).astype(BF16)
    grad_gate, grad_up, grad_down, grad_out = finish(reduced, hid)
    return (
        output,
        input_grad,
        dw[0],
        dw[1],
        dw[2],
        grad_out,
        grad_gate,
        grad_up,
        grad_down,
        gains[0, :width],
        gains[1, :width],
    )


def solution(mesh):
    count, pair = mesh.shape["dp"], mesh.shape["tensor"]
    near = min(4, count)
    mesh = Mesh(mesh.devices.reshape(count // near, near, pair), DP + ("tensor",))
    split = P(DP, "tensor")
    turned = P("tensor", DP)
    slots = P(DP + ("tensor",), None)
    return jax.shard_map(
        local,
        mesh=mesh,
        in_specs=(slots, split, split, split, turned, split, split, turned, P(), P(),
                  P(DP, None), slots),
        out_specs=(slots, slots, split, split, split, turned, split, split, turned, P(), P()),
        check_vma=False,
    )
```

```python
from functools import partial

import jax
import jax.numpy as jnp
from jax import lax
from jax.experimental import pallas as pl
from jax.experimental.pallas import tpu as pltpu
from jax.sharding import Mesh
from jax.sharding import PartitionSpec as P

HEAD = 64
PAIR = 2 * HEAD
EPS = 1e-05
ROPE_BASE = 10000.0
NEGATIVE = -1e30
F32 = jnp.float32
BF16 = jnp.bfloat16
VMEM_LIMIT = 56 * 1024 * 1024
DP = ("far", "near")
EXTRA = 16
SIDE, TOTAL, BIT_X, BIT_Y, FAR, LOWS = range(6)


def mm(left, right):
    return jnp.dot(left, right, preferred_element_type=F32)


def rdot(left, right):
    return lax.dot_general(left, right, (((1,), (1,)), ((), ())), preferred_element_type=F32)


def tdot(left, right):
    return lax.dot_general(left, right, (((0,), (0,)), ((), ())), preferred_element_type=F32)


def params(limit=VMEM_LIMIT, dims=1):
    return pltpu.CompilerParams(
        vmem_limit_bytes=limit, dimension_semantics=("arbitrary",) * dims
    )


def cost(flops, nbytes, trans=0):
    return pl.CostEstimate(flops=int(flops), bytes_accessed=int(nbytes), transcendentals=int(trans))


def swap_halves(values):
    lane = lax.broadcasted_iota(jnp.int32, values.shape, 1) % HEAD
    half = HEAD // 2
    width = values.shape[1]
    return jnp.where(
        lane < half, pltpu.roll(values, width - half, 1), pltpu.roll(values, half, 1)
    )


def head_masks(values):
    return one_head(values, 0), one_head(values, 1)


def one_head(values, h):
    lane = lax.broadcasted_iota(jnp.int32, (1, PAIR), 1)
    return values * (lane // HEAD == h).astype(values.dtype)


def forward_kernel(sched, own_x_ref, oth_x_ref, wq_ref, wk_ref, wv_ref, cos_ref, sin_ref, start_ref,
                   qkv_ref, oth_ref, own_ref, lse_ref, acc_ref, vt_ref, *, bq, bk, sub, chunk, blocks):
    step = pl.program_id(1)
    half = blocks // 2
    i = lax.rem(step + (1 - sched[0]) * half, blocks)

    @pl.when(step == 0)
    def _():
        local = own_x_ref.shape[0]
        weights = jnp.concatenate([wq_ref[...], wk_ref[...], wv_ref[...]], axis=1)
        for x_ref, side in ((own_x_ref, sched[0]), (oth_x_ref, 1 - sched[0])):
            for r in range(0, local, chunk):
                here = pl.ds(pl.multiple_of(side * local + r, chunk), chunk)
                u = mm(x_ref[r:r + chunk, :], weights)
                cosine, sine = cos_ref[here, :], sin_ref[here, :]
                for n, scale in ((0, HEAD ** -0.5), (1, 1.0)):
                    piece = u[:, n * PAIR:(n + 1) * PAIR]
                    turned = piece * cosine + swap_halves(piece) * sine
                    qkv_ref[here, n * PAIR:(n + 1) * PAIR] = (turned * scale).astype(BF16)
                v = u[:, 2 * PAIR:]
                qkv_ref[here, 2 * PAIR:] = v.astype(BF16)
                vt_ref[:, here] = v.T.astype(BF16)

    start = start_ref[...]
    acc_ref[...] = jnp.zeros_like(acc_ref)
    streams = list(range(0, bq, sub))

    @pl.loop(0, 2)
    def _(h):
        queries = one_head(qkv_ref[pl.ds(pl.multiple_of(i * bq, bq), bq), 0:PAIR], h)
        rows = pl.ds(pl.multiple_of(h * HEAD, HEAD), HEAD)

        def visit(j, carry, last):
            at = pl.multiple_of(i * bq if last else j * bk, bk)
            scores, out = [], []
            for c in streams:
                size = c + sub if last else bk
                s = rdot(qkv_ref[pl.ds(at, size), PAIR:2 * PAIR], queries[c:c + sub])
                key_index = lax.broadcasted_iota(jnp.int32, (size, sub), 0)
                allowed = key_index >= start[:, c:c + sub] - at
                if last:
                    query_index = c + lax.broadcasted_iota(jnp.int32, (size, sub), 1)
                    allowed = allowed & (key_index <= query_index)
                scores.append(jnp.where(allowed, s, NEGATIVE))
            for n, c in enumerate(streams):
                size = c + sub if last else bk
                peak, total = carry[2 * n], carry[2 * n + 1]
                new_peak = jnp.maximum(peak, jnp.max(scores[n], axis=0, keepdims=True))
                fade = jnp.exp(peak - new_peak)
                expo = jnp.exp(scores[n] - new_peak)
                total = total * fade + jnp.sum(expo, axis=0, keepdims=True)
                cols = slice(c, c + sub)
                acc_ref[rows, cols] = acc_ref[rows, cols] * fade + mm(
                    vt_ref[rows, pl.ds(at, size)], expo.astype(BF16)
                )
                out += [new_peak, total]
            return tuple(out)

        carry = (jnp.full((1, sub), NEGATIVE, F32), jnp.zeros((1, sub), F32)) * len(streams)
        carry = lax.fori_loop(sched[LOWS + i], i * (bq // bk), lambda j, c: visit(j, c, False), carry)
        carry = visit(None, carry, True)
        for n, c in enumerate(streams):
            peak, total = carry[2 * n], carry[2 * n + 1]
            cols = slice(c, c + sub)
            acc_ref[rows, cols] = acc_ref[rows, cols] / total
            lse_ref[pl.ds(h, 1), cols] = peak + jnp.log(total)

    mixed = acc_ref[...].T.astype(BF16)

    @pl.when(step < half)
    def _():
        oth_ref[...] = mixed

    @pl.when(step >= half)
    def _():
        own_ref[...] = mixed


def placing(blocks):
    half = blocks // 2

    def place(n, sched):
        return lax.rem(n + (1 - sched[0]) * half, blocks)

    return place, half


def attend_forward(sched, own_x, oth_x, weights, cosine, sine, start, bq, bk, sub=256, chunk=512):
    local, width = own_x.shape
    slots, cols = 2 * local, weights.shape[1] // 3
    pairs, blocks = cols // PAIR, slots // bq
    place, half = placing(blocks)
    rows = pl.BlockSpec((local, width), lambda p, n, s: (0, 0), pipeline_mode=pl.Buffered(1))
    table = pl.BlockSpec((slots, PAIR), lambda p, n, s: (0, 0), pipeline_mode=pl.Buffered(1))
    return pl.pallas_call(
        partial(forward_kernel, bq=bq, bk=bk, sub=sub, chunk=chunk, blocks=blocks),
        grid_spec=pltpu.PrefetchScalarGridSpec(
            num_scalar_prefetch=1,
            grid=(pairs, blocks),
            in_specs=[
                rows, rows,
                *[pl.BlockSpec((width, PAIR), lambda p, n, s, at=at: (0, at + p))
                  for at in (0, pairs, 2 * pairs)],
                table, table,
                pl.BlockSpec((1, bq), lambda p, n, s: (0, place(n, s))),
            ],
            out_specs=[
                pl.BlockSpec((slots, 3 * PAIR), lambda p, n, s: (0, p)),
                pl.BlockSpec((bq, PAIR), lambda p, n, s: (jnp.minimum(n, half - 1), p)),
                pl.BlockSpec((bq, PAIR), lambda p, n, s: (jnp.maximum(n - half, 0), p)),
                pl.BlockSpec((None, 2, bq), lambda p, n, s: (p, 0, place(n, s))),
            ],
            scratch_shapes=[pltpu.VMEM((PAIR, bq), F32), pltpu.VMEM((PAIR, slots), BF16)],
        ),
        out_shape=[
            jax.ShapeDtypeStruct((slots, 3 * cols), BF16),
            jax.ShapeDtypeStruct((local, cols), BF16),
            jax.ShapeDtypeStruct((local, cols), BF16),
            jax.ShapeDtypeStruct((pairs, 2, slots), F32),
        ],
        compiler_params=params(dims=2),
        cost_estimate=cost(4 * slots * slots * cols + 6 * slots * width * cols,
                           16 * slots * cols, slots * slots * 6),
        name="attend_forward",
    )(sched, own_x, oth_x, weights, weights, weights, cosine, sine, start)


def backward_kernel(sched, q_ref, k_ref, v_ref, cos_ref, sin_ref, start_ref, lse_ref,
                    o_oth_ref, o_own_ref, g_oth_ref, g_own_ref, x_own_ref, x_oth_ref,
                    gains_ref, all_ref, *rest, bq, bk, sub, blocks, share):
    step = pl.program_id(1)
    half = blocks // 2
    i = lax.rem(step + (1 - sched[0]) * half, blocks)

    dw_refs, (dq_acc, dkt_acc, dvt_acc) = rest[:-3], rest[-3:]

    @pl.when(step == 0)
    def _():
        dkt_acc[...] = jnp.zeros_like(dkt_acc)
        dvt_acc[...] = jnp.zeros_like(dvt_acc)

    first = step < half
    grads = jnp.where(first, g_oth_ref[...], g_own_ref[...])
    mixed = jnp.where(first, o_oth_ref[...], o_own_ref[...])
    queries = head_masks(q_ref[...])
    couts = head_masks(grads)
    query_t = q_ref[...].astype(F32).T.astype(BF16)
    cout_t = grads.astype(F32).T.astype(BF16)
    begin = jnp.broadcast_to(start_ref[...], (PAIR, bq)).T
    product = grads.astype(F32) * mixed.astype(F32)
    big = product.astype(BF16)
    small = (product - big.astype(F32)).astype(BF16)
    row = lax.broadcasted_iota(jnp.int32, (PAIR, 2 * PAIR), 0)
    lane = lax.broadcasted_iota(jnp.int32, (PAIR, 2 * PAIR), 1)
    pick = jnp.where(row // HEAD == lane // PAIR, 1.0, 0.0).astype(BF16)
    inner = mm(big, pick) + mm(small, pick)
    lse = [jnp.broadcast_to(lse_ref[h:h + 1, :], (PAIR, bq)).T for h in range(2)]
    dq_acc[...] = jnp.zeros_like(dq_acc)

    def wide(value, size):
        return jnp.concatenate([value] * (size // PAIR), axis=1)

    def visit(j, last):
        at = pl.multiple_of(i * bq if last else j * bk, bk)
        streams = [(c, h) for c in range(0, bq, sub) for h in range(2)]

        def scores(n):
            c, h = streams[n]
            size = c + sub if last else bk
            where = pl.ds(at, size)
            rows = slice(c, c + sub)
            return rdot(queries[h][rows], k_ref[where, :]), rdot(couts[h][rows], v_ref[where, :])

        def absorb(n, pair):
            c, h = streams[n]
            raw, d_probs = pair
            size = c + sub if last else bk
            where = pl.ds(at, size)
            rows = slice(c, c + sub)
            lanes = slice(h * HEAD, (h + 1) * HEAD)
            probs = jnp.exp(raw - wide(lse[h][rows], size))
            key_index = lax.broadcasted_iota(jnp.int32, (sub, size), 1)
            allowed = key_index >= wide(begin[rows], size) - at
            if last:
                query_index = c + lax.broadcasted_iota(jnp.int32, (sub, size), 0)
                allowed = allowed & (key_index <= query_index)
            probs = jnp.where(allowed, probs, 0.0)
            d_scores = (probs * (d_probs - wide(inner[rows, h * PAIR:(h + 1) * PAIR], size))).astype(BF16)
            dvt_acc[lanes, where] += mm(cout_t[lanes, rows], probs.astype(BF16))
            dkt_acc[lanes, where] += mm(query_t[lanes, rows], d_scores)
            dq_acc[rows, :] += mm(d_scores, head_masks(k_ref[where, :])[h])

        ready = scores(0)
        for n in range(len(streams)):
            held = ready
            if n + 1 < len(streams):
                ready = scores(n + 1)
            absorb(n, held)

    @pl.loop(sched[LOWS + blocks + i], i * (bq // bk))
    def _(j):
        visit(j, False)

    visit(None, True)

    def unrotate(g, cosine, sine):
        return g * cosine - swap_halves(g) * sine

    here = pl.ds(pl.multiple_of(i * bq, bq), bq)
    dq = unrotate(dq_acc[...] * (HEAD ** -0.5), cos_ref[here, :], sin_ref[here, :])
    all_ref[here, 0:PAIR] = dq.astype(BF16)

    @pl.when(step == blocks - 1)
    def _():
        dk = unrotate(dkt_acc[...].T, cos_ref[...], sin_ref[...])
        all_ref[:, PAIR:2 * PAIR] = dk.astype(BF16)
        all_ref[:, 2 * PAIR:] = dvt_acc[...].T.astype(BF16)
        local = x_own_ref.shape[0]
        mine = pl.ds(pl.multiple_of(sched[0] * local, local), local)
        other = pl.ds(pl.multiple_of((1 - sched[0]) * local, local), local)
        total = (tdot(x_own_ref[...], all_ref[mine, :])
                 + tdot(x_oth_ref[...], all_ref[other, :])).astype(BF16)
        if share is None:
            dw_refs[0][...] = total
        else:
            part_rows(total, gains_ref[0:2, :], sched[BIT_X], sched[BIT_Y], *dw_refs, share)


def encode(value):
    high = value.astype(BF16)
    rest = value - high.astype(F32)
    middle = rest.astype(BF16)
    low = (rest - middle.astype(F32)).astype(BF16)
    rows, cols = value.shape
    pieces = [piece.astype(F32) for piece in (high, middle, low)]
    return jnp.concatenate(pieces + [jnp.zeros((EXTRA - 3 * rows, cols), F32)], axis=0).astype(BF16)


def decode(rows, count=2):
    wide = rows.astype(F32)
    return wide[0:count] + wide[count:2 * count] + wide[2 * count:3 * count]


def part_rows(total, gains, bit_x, bit_y, keep_a, send_a, keep_b, send_b, share):
    def block(z, y, x):
        at = (4 * z + 2 * y + x) * share
        return total[at:at + share]

    pieces = keep_a.shape[0] // share
    for n in range(pieces):
        z, side, here = 2 * (n // 2), n % 2, slice(n * share, (n + 1) * share)
        zero, one = block(z, side, 0), block(z, side, 1)
        keep_a[here] = jnp.where(bit_x == 0, zero, one)
        send_a[here] = jnp.where(bit_x == 0, one, zero)
        zero, one = block(z + 1, 0, side), block(z + 1, 1, side)
        keep_b[here] = jnp.where(bit_y == 0, zero, one)
        send_b[here] = jnp.where(bit_y == 0, one, zero)
    send_a[pieces * share:] = encode(gains)


def attend_backward(sched, qkv, cosine, sine, start, lse, o_oth, o_own, g_oth, g_own, x_own, x_oth,
                    gains, bq, bk, share, sub=256):
    slots, cols = qkv.shape[0], qkv.shape[1] // 3
    pairs, blocks = cols // PAIR, slots // bq
    local, width = x_own.shape
    place, half = placing(blocks)
    table = pl.BlockSpec((slots, PAIR), lambda p, n, s: (0, 0), pipeline_mode=pl.Buffered(1))
    rows = pl.BlockSpec((local, width), lambda p, n, s: (0, 0), pipeline_mode=pl.Buffered(1))
    oth = pl.BlockSpec((bq, PAIR), lambda p, n, s: (jnp.minimum(n, half - 1), p))
    own = pl.BlockSpec((bq, PAIR), lambda p, n, s: (jnp.maximum(n - half, 0), p))
    if share is None:
        dw_specs = [pl.BlockSpec((width, 3 * PAIR), lambda p, n, s: (0, p))]
        dw_shapes = [(width, 3 * cols)]
    else:
        rows_out = [width // 4, width // 4 + EXTRA, width // 4, width // 4]
        dw_specs = [pl.BlockSpec((size, 3 * PAIR), lambda p, n, s: (0, p)) for size in rows_out]
        dw_shapes = [(size, 3 * cols) for size in rows_out]
    return pl.pallas_call(
        partial(backward_kernel, bq=bq, bk=bk, sub=sub, blocks=blocks, share=share),
        grid_spec=pltpu.PrefetchScalarGridSpec(
            num_scalar_prefetch=1,
            grid=(pairs, blocks),
            in_specs=[
                pl.BlockSpec((bq, PAIR), lambda p, n, s: (place(n, s), 3 * p)),
                pl.BlockSpec((slots, PAIR), lambda p, n, s: (0, 3 * p + 1)),
                pl.BlockSpec((slots, PAIR), lambda p, n, s: (0, 3 * p + 2)),
                table, table,
                pl.BlockSpec((1, bq), lambda p, n, s: (0, place(n, s))),
                pl.BlockSpec((None, 2, bq), lambda p, n, s: (p, 0, place(n, s))),
                oth, own, oth, own, rows, rows,
                pl.BlockSpec((8, 3 * PAIR), lambda p, n, s: (0, p)),
            ],
            out_specs=[pl.BlockSpec((slots, 3 * PAIR), lambda p, n, s: (0, p)), *dw_specs],
            scratch_shapes=[
                pltpu.VMEM((bq, PAIR), F32),
                pltpu.VMEM((PAIR, slots), F32),
                pltpu.VMEM((PAIR, slots), F32),
            ],
        ),
        out_shape=[jax.ShapeDtypeStruct(shape, BF16) for shape in [(slots, 3 * cols), *dw_shapes]],
        compiler_params=params(dims=2),
        cost_estimate=cost(10 * slots * slots * cols + 6 * slots * width * cols,
                           20 * slots * cols, slots * slots * 6),
        name="attend_backward",
    )(sched, qkv, qkv, qkv, cosine, sine, start, lse, o_oth, o_own, g_oth, g_own, x_own, x_oth, gains)


def feed_kernel(sched, x_ref, own_ref, oth_ref, dy_ref, w_hbm, ga_ref, gf_ref,
                out_ref, dfirst_ref, gown_ref, goth_ref, grads_ref, gains_ref,
                right_hbm, left_hbm, dattn_hbm,
                w_ref, keep_a, keep_b, total_s, right_s, left_s, dattn_s, mixed_s,
                sems, *, block, sub, chunk, local, hid, head_cols, parts, share):
    step = pl.program_id(0)
    me = sched[0]
    steps = local // block
    outs = slice(3 * hid, 3 * hid + head_cols)
    pieces = [(slice(3 * hid, w_ref.shape[2]), None), (slice(0, 2 * hid), 0), (slice(0, 2 * hid), 1),
              (slice(2 * hid, 3 * hid), None)]

    def piece(n):
        cols, t = pieces[n]
        at = (slice(None), slice(None), cols) if t is None else (t, slice(None), cols)
        return pltpu.make_async_copy(w_hbm.at[at], w_ref.at[at], sems.at[n])

    @pl.when(step == 0)
    def _():
        for n in range(len(pieces)):
            piece(n).start()
        gains_ref[...] = jnp.zeros_like(gains_ref)

    def arrive(n):
        @pl.when(step == 0)
        def _():
            piece(n).wait()

    @pl.when(step < steps)
    def _():
        subs = list(range(0, block, sub))
        base = pl.multiple_of(step * block, block)
        arrive(0)
        attn, rms1, unit1, normed, normed_b = {}, {}, {}, {}, {}
        for r in subs:
            rows = slice(r, r + sub)
            attn[r] = rdot(own_ref[rows, :], w_ref[me, :, outs]) + rdot(oth_ref[rows, :], w_ref[1 - me, :, outs])
        for r in subs:
            rows = slice(r, r + sub)
            here = pl.ds(base + r, sub)
            first = x_ref[rows, :].astype(F32) + attn[r]
            rms1[r] = lax.rsqrt(jnp.mean(first * first, axis=-1, keepdims=True) + EPS)
            unit1[r] = first * rms1[r]
            normed[r] = unit1[r] * ga_ref[...]
            normed_b[r] = normed[r].astype(BF16)
            left_s[0, here, :] = normed_b[r]
            mixed_s[here, :] = oth_ref[rows, :]
        total_s[...] = jnp.zeros_like(total_s)

        @pl.loop(0, 2)
        def _(t):
            for at, count in ((0, 1), (0, 3), (1, 2)):
                @pl.when((step == 0) & (t == at))
                def _():
                    piece(count).wait()

            for c in range(0, hid, chunk):
                cols = pl.ds(pl.multiple_of(t * hid + c, chunk), chunk)
                hid_b = {}
                for r in subs:
                    rows = slice(r, r + sub)
                    gate = mm(normed_b[r], w_ref[t, :, c:c + chunk])
                    upper = mm(normed_b[r], w_ref[t, :, hid + c:hid + c + chunk])
                    sigma = 1.0 / (1.0 + jnp.exp(-gate))
                    silu = gate * sigma
                    hid_b[r] = (silu * upper).astype(BF16)
                    keep_a[rows, cols] = silu
                    keep_b[rows, cols] = upper * (sigma + silu * (1.0 - sigma))
                    right_s[2, pl.ds(base + r, sub), cols] = hid_b[r]
                for r in subs:
                    total_s[r:r + sub, :] += rdot(hid_b[r], w_ref[t, :, 2 * hid + c:2 * hid + c + chunk])

        d_second, d_ffn = {}, {}
        for r in subs:
            rows = slice(r, r + sub)
            here = pl.ds(base + r, sub)
            second = normed[r] + total_s[rows, :]
            rms2 = lax.rsqrt(jnp.mean(second * second, axis=-1, keepdims=True) + EPS)
            unit2 = second * rms2
            slot = me * local + base + r + lax.broadcasted_iota(jnp.int32, (sub, 1), 0)
            valid = slot < sched[1]
            out_ref[rows, :] = jnp.where(valid, unit2 * gf_ref[...], 0.0).astype(BF16)
            dy = jnp.where(valid, dy_ref[rows, :].astype(F32), 0.0)
            gains_ref[1:2, 0:dy.shape[1]] += jnp.sum(dy * unit2, axis=0, keepdims=True)
            scaled = dy * gf_ref[...]
            d_second[r] = rms2 * (scaled - unit2 * jnp.mean(scaled * unit2, axis=-1, keepdims=True))
            d_ffn[r] = d_second[r].astype(BF16)
            left_s[1, here, :] = d_ffn[r]
            total_s[rows, :] = d_second[r]

        @pl.loop(0, 2)
        def _(t):
            for c in range(0, hid, chunk):
                cols = pl.ds(pl.multiple_of(t * hid + c, chunk), chunk)
                dg, du = {}, {}
                for r in subs:
                    rows, here = slice(r, r + sub), pl.ds(base + r, sub)
                    d_hidden = mm(d_ffn[r], w_ref[t, :, 2 * hid + c:2 * hid + c + chunk])
                    dg[r] = (d_hidden * keep_b[rows, cols]).astype(BF16)
                    du[r] = (d_hidden * keep_a[rows, cols]).astype(BF16)
                    right_s[0, here, cols] = dg[r]
                    right_s[1, here, cols] = du[r]
                for r in subs:
                    total_s[r:r + sub, :] += rdot(dg[r], w_ref[t, :, c:c + chunk]) + rdot(
                        du[r], w_ref[t, :, hid + c:hid + c + chunk])

        for r in subs:
            rows = slice(r, r + sub)
            here = pl.ds(base + r, sub)
            d_normed = total_s[rows, :]
            gains_ref[0:1, 0:d_normed.shape[1]] += jnp.sum(d_normed * unit1[r], axis=0, keepdims=True)
            scaled = d_normed * ga_ref[...]
            d_first = rms1[r] * (scaled - unit1[r] * jnp.mean(scaled * unit1[r], axis=-1, keepdims=True))
            dfirst_ref[rows, :] = d_first
            d_attn = d_first.astype(BF16)
            dattn_s[here, :] = d_attn
            gown_ref[rows, :] = mm(d_attn, w_ref[me, :, outs]).astype(BF16)
            goth_ref[rows, :] = mm(d_attn, w_ref[1 - me, :, outs]).astype(BF16)

    mine = pl.ds(pl.multiple_of(me * hid, hid), hid)
    outgoing = [
        pltpu.make_async_copy(right_s.at[:, :, mine], right_hbm, sems.at[len(pieces)]),
        pltpu.make_async_copy(left_s, left_hbm, sems.at[len(pieces) + 1]),
        pltpu.make_async_copy(dattn_s, dattn_hbm, sems.at[len(pieces) + 2]),
    ]

    @pl.when(step == steps)
    def _():
        for copy in outgoing:
            copy.start()

    @pl.when(step >= steps)
    def _():
        size = dattn_s.shape[1] // parts
        rows = pl.ds(pl.multiple_of((step - steps) * size, size), size)
        cols = pl.ds(pl.multiple_of((1 - me) * hid, hid), hid)
        for n in range(3):
            left = left_s[n // 2, :, rows]
            store_rows(grads_ref, tdot(left, right_s[n, :, cols]), slice(n * hid, (n + 1) * hid), share)
        store_rows(grads_ref, tdot(dattn_s[:, rows], mixed_s[...]),
                   slice(3 * hid, 3 * hid + head_cols), share)

    @pl.when(step == steps + parts - 1)
    def _():
        for copy in outgoing:
            copy.wait()


def store_rows(ref, value, cols, share, part=0):
    value = value.astype(BF16)
    rows = value.shape[0]
    if share is None:
        ref[pl.ds(pl.multiple_of(part * rows, rows), rows), cols] = value
    else:
        near = ref.shape[0]
        for n in range(rows // share):
            far = part * (rows // (share * near)) + n // near
            ref[n % near, far, :, cols] = value[n * share:(n + 1) * share]


def own_grads_kernel(left_ref, right_ref, dattn_ref, mixed_ref, out_ref, *, tiles, share):
    step = pl.program_id(0)

    size = left_ref.shape[1] // 2

    @pl.loop(0, 2)
    def _(part):
        rows = pl.ds(pl.multiple_of(part * size, size), size)

        @pl.when(step < tiles)
        def _():
            store_rows(out_ref, tdot(left_ref[:, rows], right_ref[...]), slice(None), share, part)

        @pl.when(step == tiles)
        def _():
            store_rows(out_ref, tdot(dattn_ref[:, rows], mixed_ref[...]),
                       slice(0, mixed_ref.shape[1]), share, part)


def own_grads(left, right, d_attn, mixed, share, near, tile=512):
    _, local, width = left.shape
    hid, head_cols = right.shape[2], mixed.shape[1]
    each = hid // tile
    tiles = 3 * each
    total = 3 * hid + head_cols
    packed = share % 16 == 0
    if packed:
        shape = (near, width // (near * share), share)
        out_spec = pl.BlockSpec((*shape, tile), lambda n: (0, 0, 0, n))
    else:
        shape = (width,)
        out_spec = pl.BlockSpec((width, tile), lambda n: (0, n))

    def kind(n):
        return jnp.minimum(lax.div(n, each), 2)

    grads = pl.pallas_call(
        partial(own_grads_kernel, tiles=tiles, share=share if packed else None),
        grid=(tiles + 1,),
        in_specs=[
            pl.BlockSpec((None, local, width), lambda n: (lax.div(kind(n), 2), 0, 0)),
            pl.BlockSpec((None, local, tile), lambda n: (kind(n), 0, lax.rem(jnp.minimum(n, tiles - 1), each))),
            pl.BlockSpec((local, width), lambda n: (0, 0)),
            pl.BlockSpec((local, head_cols), lambda n: (0, 0)),
        ],
        out_specs=out_spec,
        out_shape=jax.ShapeDtypeStruct((*shape, total), BF16),
        compiler_params=params(),
        cost_estimate=cost(2 * local * width * total, 2 * local * (4 * width + 3 * hid)),
        name="own_grads",
    )(left, right, d_attn, mixed)
    return by_near(grads, share, near)


def by_near(grads, share, near):
    total = grads.shape[-1]
    if share % 16:
        grads = grads.reshape(-1, near, share, total).swapaxes(0, 1)
    return grads.reshape(-1, total)


def feed(sched, x, own, oth, dy, weights, gain_attn, gain_ffn, hid, share, near,
         block=512, sub=256, chunk=512, parts=2):
    local, width = x.shape
    head_cols = own.shape[1]
    total = weights.shape[2]
    steps = local // block
    packed = share % 16 == 0

    def at(s):
        return jnp.minimum(s, steps - 1)

    rows = pl.BlockSpec((block, width), lambda s, sched: (at(s), 0))
    heads = pl.BlockSpec((block, head_cols), lambda s, sched: (at(s), 0))
    gain = pl.BlockSpec((1, width), lambda s, sched: (0, 0))

    def tile(s, sched):
        n = jnp.maximum(s - steps, 0)
        return (0, n, 0, 0) if packed else (n, 0)

    if packed:
        grads_shape = (near, width // (near * share), share, total)
        grads_block = (near, width // (near * share * parts), share, total)
    else:
        grads_shape, grads_block = (width, total), (width // parts, total)

    def shape(cols, dtype):
        return jax.ShapeDtypeStruct((local, cols), dtype)

    results = pl.pallas_call(
        partial(feed_kernel, block=block, sub=sub, chunk=chunk, local=local, hid=hid,
                head_cols=head_cols, parts=parts, share=share if packed else None),
        grid_spec=pltpu.PrefetchScalarGridSpec(
            num_scalar_prefetch=1,
            grid=(steps + parts,),
            in_specs=[rows, heads, heads, rows, pl.BlockSpec(memory_space=pl.ANY), gain, gain],
            out_specs=[rows, rows, heads, heads,
                       pl.BlockSpec(grads_block, tile),
                       pl.BlockSpec((8, 3 * head_cols), lambda s, sched: (0, 0))]
            + [pl.BlockSpec(memory_space=pl.ANY)] * 3,
            scratch_shapes=[pltpu.VMEM(weights.shape, BF16)]
            + [pltpu.VMEM((block, 2 * hid), F32)] * 2
            + [pltpu.VMEM((block, width), F32)]
            + [pltpu.VMEM((3, local, 2 * hid), BF16), pltpu.VMEM((2, local, width), BF16)]
            + [pltpu.VMEM((local, width), BF16)]
            + [pltpu.VMEM((local, head_cols), BF16), pltpu.SemaphoreType.DMA((7,))],
        ),
        out_shape=[
            shape(width, BF16), shape(width, F32), shape(head_cols, BF16), shape(head_cols, BF16),
            jax.ShapeDtypeStruct(grads_shape, BF16),
            jax.ShapeDtypeStruct((8, 3 * head_cols), F32),
            jax.ShapeDtypeStruct((3, local, hid), BF16),
            jax.ShapeDtypeStruct((2, local, width), BF16),
            shape(width, BF16),
        ],
        compiler_params=params(60 * 1024 * 1024),
        cost_estimate=cost(12 * local * width * total, 30 * local * width),
        name="feed",
    )(sched, x, own, oth, dy, weights, gain_attn, gain_ffn)
    return (*results[:4], by_near(results[4], share, near), *results[5:])


def input_grad_kernel(sched, d_ref, w_ref, dfirst_ref, oth_ref, own_ref, *, half):
    step = pl.program_id(0)
    cols = d_ref.shape[1]
    order = [at + n * PAIR for n in range(3) for at in range(0, cols, 3 * PAIR)]
    part = rdot(jnp.concatenate([d_ref[:, at:at + PAIR] for at in order], axis=1), w_ref[...])

    @pl.when(step < half)
    def _():
        oth_ref[...] = part.astype(BF16)

    @pl.when(step >= half)
    def _():
        own_ref[...] = dfirst_ref[...] + part


def input_grads(sched, d_qkv, weights, d_first, block):
    local, width = d_first.shape
    cols = d_qkv.shape[1]
    half = local // block
    place, _ = placing(2 * half)
    own = pl.BlockSpec((block, width), lambda n, s: (jnp.maximum(n - half, 0), 0))
    return pl.pallas_call(
        partial(input_grad_kernel, half=half),
        grid_spec=pltpu.PrefetchScalarGridSpec(
            num_scalar_prefetch=1,
            grid=(2 * half,),
            in_specs=[pl.BlockSpec((block, cols), lambda n, s: (place(n, s), 0)),
                      pl.BlockSpec((width, cols), lambda n, s: (0, 0)), own],
            out_specs=[pl.BlockSpec((block, width), lambda n, s: (jnp.minimum(n, half - 1), 0)), own],
        ),
        out_shape=[jax.ShapeDtypeStruct((local, width), BF16),
                   jax.ShapeDtypeStruct((local, width), F32)],
        compiler_params=params(),
        cost_estimate=cost(4 * local * width * cols, 4 * local * (width + cols)),
        name="input_grads",
    )(sched, d_qkv, weights, d_first)


def finish_kernel(total_ref, gate_ref, up_ref, down_ref, out_ref):
    hid = gate_ref.shape[1]
    gate_ref[...] = total_ref[:, 0:hid].astype(F32)
    up_ref[...] = total_ref[:, hid:2 * hid].astype(F32)
    down_ref[...] = total_ref[:, 2 * hid:3 * hid].astype(F32)
    out_ref[...] = total_ref[:, 3 * hid:].astype(F32)


def finish(total, hid):
    share, cols = total.shape
    gate, up, down, out = pl.pallas_call(
        finish_kernel,
        out_shape=[jax.ShapeDtypeStruct((share, width), F32)
                   for width in (hid, hid, hid, cols - 3 * hid)],
        cost_estimate=cost(0, 6 * share * cols),
        name="finish",
    )(total)
    return gate, up, down.T, out.T


def whole_call(kernel, name, sched, values, shapes):
    whole = pl.BlockSpec(memory_space=pltpu.VMEM)
    size = 4 * sum(value.size for value in values)
    return pl.pallas_call(
        kernel,
        in_specs=[pl.BlockSpec(memory_space=pltpu.SMEM)] + [whole] * len(values),
        out_specs=[whole] * len(shapes),
        out_shape=[jax.ShapeDtypeStruct(shape, dtype) for shape, dtype in shapes],
        compiler_params=pltpu.CompilerParams(vmem_limit_bytes=32 * 1024 * 1024),
        cost_estimate=cost(0, size),
        name=name,
    )(sched, *values)


def add(left, right):
    return left.astype(F32) + right.astype(F32)


def near_kernel(sched, keep_a, got_a, keep_b, got_b, gains, next_a, send_a, next_b, send_b, total,
                *, share):
    size = next_a.shape[0]
    for held, got, bit, stay, go in ((keep_a, got_a, sched[BIT_Y], next_a, send_a),
                                     (keep_b, got_b, sched[BIT_X], next_b, send_b)):
        for n in range(size // share):
            here = slice(n * share, (n + 1) * share)
            mine = pl.ds(pl.multiple_of((2 * n + bit) * share, share), share)
            other = pl.ds(pl.multiple_of((2 * n + 1 - bit) * share, share), share)
            stay[here] = add(held[mine], got[mine]).astype(BF16)
            go[here] = add(held[other], got[other]).astype(BF16)
    total[...] = gains[0:2, :] + decode(got_a[2 * size:])
    send_a[size:] = encode(total[...])


def far_kernel(sched, keep_a, got_a, keep_b, got_b, gains, own, total, *sends):
    far, share = 1 + len(sends), own.shape[0]
    sums = []
    for n in range(far // 2):
        here = slice(n * share, (n + 1) * share)
        sums += [add(keep_a[here], got_a[here]), add(keep_b[here], got_b[here])]
    total[...] = gains[...] + decode(got_a[keep_a.shape[0]:])
    for shift in range(far):
        at = lax.rem(sched[FAR] + shift, far)
        value = sums[0]
        for n in range(1, far):
            value = jnp.where(at == n, sums[n], value)
        if shift == 0:
            own[...] = value
        else:
            sends[shift - 1][:share] = value.astype(BF16)
            sends[shift - 1][share:] = encode(total[...])


def last_kernel(sched, own, gains, *rest):
    got, outs, total = rest[:-4], rest[-4:-1], rest[-1]
    value, share, far = own[...], own.shape[0], 1 + len(rest[:-4])
    arrived = [gains[...]]
    for piece in got:
        value = value + piece[:share].astype(F32)
        arrived.append(decode(piece[share:]))
    for at in range(0, value.shape[1], PAIR):
        pair, part = at // PAIR // 3, at // PAIR % 3
        outs[part][:, pair * PAIR:(pair + 1) * PAIR] = value[:, at:at + PAIR]
    summed = None
    for n in range(far):
        shift = lax.rem(sched[FAR] - n + far, far)
        term = arrived[0]
        for k in range(1, far):
            term = jnp.where(shift == k, arrived[k], term)
        summed = term if summed is None else summed + term
    total[...] = summed


def shifted(value, shift):
    far = lax.axis_size("far")
    return lax.ppermute(value, "far", [(at, (at + shift) % far) for at in range(far)])


def sum_parts(sched, share, keep_a, send_a, keep_b, send_b, gains, meanwhile):
    size, width = keep_a.shape
    far = lax.axis_size("far")
    got_a, got_b = flip(send_a, 0), flip(send_b, 1)
    beside = meanwhile()
    got_a, got_b, beside = lax.optimization_barrier((got_a, got_b, beside))
    sizes = [size // 2, size // 2 + EXTRA, size // 2, size // 2]
    keep_a, send_a, keep_b, send_b, gains = whole_call(
        partial(near_kernel, share=share), "near_sums", sched,
        (keep_a, got_a, keep_b, got_b, gains),
        [((rows, width), BF16) for rows in sizes] + [((2, width), F32)])
    got_a, got_b = flip(send_a, 1), flip(send_b, 0)
    own, gains, *sends = whole_call(
        far_kernel, "far_sums", sched, (keep_a, got_a, keep_b, got_b, gains),
        [((share, width), F32), (gains.shape, F32)] + [((share + EXTRA, width), BF16)] * (far - 1))
    got = [shifted(value, shift + 1) for shift, value in enumerate(sends)]
    return (own, gains, *got), beside


def last_sums(sched, own, gains, *got):
    share, width = own.shape
    *dw, gains = whole_call(last_kernel, "last_sums", sched, (own, gains, *got),
                            [((share, width // 3), F32)] * 3 + [(gains.shape, F32)])
    return dw, gains


def exchange(value):
    return lax.ppermute(value, "tensor", [(0, 1), (1, 0)])


def flip(value, bit):
    count = lax.axis_size(DP)
    return lax.ppermute(value, DP, [(at, at ^ (1 << bit)) for at in range(count)])


def bit_orders(count):
    bits = count.bit_length() - 1
    low = list(range(min(2, bits)))
    high = list(range(min(2, bits), bits))
    return high[::-1] + low, high[::-1] + low[::-1]


def join(held, bit):
    other = flip(held, bit)
    mine = ((lax.axis_index(DP) >> bit) & 1) == 0
    return jnp.stack([jnp.where(mine, held, other), jnp.where(mine, other, held)])


def in_order(held, order):
    bits = len(order)
    rows, cols = held.shape[-2:]
    held = held.reshape((2,) * bits + (rows, cols))
    axes = [bits - 1 - order.index(bit) for bit in range(bits - 1, -1, -1)]
    return held.transpose(*axes, bits, bits + 1).reshape(-1, cols)


def gather_rows(piece, edge):
    fore, back = bit_orders(lax.axis_size(DP))
    high = len(fore) - min(2, len(fore))
    held = piece[None]
    for bit in fore[:high]:
        held = join(held, bit)
    parts = [held[..., :edge], held[..., edge:]]
    for one, two in zip(fore[high:], back[high:]):
        parts = [join(parts[0], one), join(parts[1], two)]
    return jnp.concatenate([in_order(parts[0], fore), in_order(parts[1], back)], axis=1)


def scatter_rows(total, order):
    me = lax.axis_index(DP)
    bits = len(order)
    rows, cols = total.shape[0] >> bits, total.shape[1]
    held = total.reshape((2,) * bits + (rows, cols))
    left = list(range(bits - 1, -1, -1))
    for bit in order:
        axis = left.index(bit)
        left.pop(axis)
        low = lax.index_in_dim(held, 0, axis, keepdims=False)
        high = lax.index_in_dim(held, 1, axis, keepdims=False)
        mine = ((me >> bit) & 1) == 0
        got = flip(jnp.where(mine, high, low), bit)
        held = (jnp.where(mine, low, high).astype(F32) + got.astype(F32)).astype(BF16)
    return held.reshape(rows, cols)


def local(tokens, w_query, w_key, w_value, w_out, w_gate, w_up, w_down, gain_attn, gain_ffn,
          lengths, cotangent):
    rows, width = tokens.shape
    slots = 2 * rows
    me = lax.axis_index("tensor")
    count = lax.axis_size(DP)
    cols, hid = w_query.shape[1], w_gate.shape[1]
    share = width // count
    edge = 5 * cols // 3
    bq, bk = rows, rows // 2
    blocks = slots // bq

    packed = jnp.concatenate([w_gate, w_up, w_down.T, w_out.T], axis=1)
    feed_w = lax.all_gather(packed, ("tensor",) + DP, axis=0, tiled=True)
    feed_w = feed_w.reshape(2, width, packed.shape[1])
    full_qkv = gather_rows(jnp.concatenate([w_query, w_key, w_value], axis=1), edge)
    other_x = exchange(tokens)

    near_at = lax.axis_index("near")
    index = jnp.arange(slots, dtype=jnp.int32)
    row = lengths[0]
    ends = jnp.cumsum(row)
    begins = jnp.sum(jnp.where(index[:, None] >= ends[None, :], row[None, :], 0), axis=1)
    position = (index - begins).astype(F32)
    lane = jnp.arange(PAIR, dtype=jnp.int32) % HEAD
    inverse = ROPE_BASE ** (-((lane % (HEAD // 2)).astype(F32) * 2.0 / HEAD))
    angle = position[:, None] * inverse[None, :]
    cosine = jnp.cos(angle)
    sine = jnp.where(lane[None, :] < HEAD // 2, -jnp.sin(angle), jnp.sin(angle))
    sched = jnp.concatenate([
        jnp.stack([me, ends[-1], near_at % 2, near_at // 2, lax.axis_index("far")]).astype(jnp.int32),
        begins[::bq] // bk,
        begins[::bq] // (bk // 2),
    ])
    start = begins.reshape(1, slots)

    qkv, mixed_send, mixed_own, lse = attend_forward(
        sched, tokens, other_x, full_qkv, cosine, sine, start, bq, bk)
    mixed_oth = exchange(mixed_send)
    output, d_first, g_own, g_send, grads, gains, right, left, d_attn = feed(
        sched, tokens, mixed_own, mixed_oth, cotangent, feed_w, gain_attn.reshape(1, width),
        gain_ffn.reshape(1, width), hid, share, lax.axis_size("near"))
    g_oth = exchange(g_send)
    other_grads = exchange(grads)
    grads = own_grads(left, right, d_attn, mixed_own, share, lax.axis_size("near"))
    grads = (grads.astype(F32) + other_grads.astype(F32)).astype(BF16)
    grads, g_oth = lax.optimization_barrier((grads, g_oth))
    reduced = lax.psum_scatter(grads, "near", scatter_dimension=0, tiled=True)
    gains = gains + exchange(gains)
    parted = share % 16 == 0 and lax.axis_size("near") == 4 and lax.axis_size("far") % 2 == 0
    d_qkv, *dw = attend_backward(sched, qkv, cosine, sine, start, lse, mixed_send, mixed_own,
                                 g_oth, g_own, tokens, other_x, gains, bq, bk // 2,
                                 share if parted else None)
    d_qkv, reduced, *dw = lax.optimization_barrier((d_qkv, reduced, *dw))
    into_input = partial(input_grads, sched, d_qkv, full_qkv, d_first, 512)
    if parted:
        last, (x_send, x_own) = sum_parts(sched, share, *dw, gains, into_input)
    else:
        x_send, x_own = into_input()
        fore, back = bit_orders(count)
        dw = jnp.concatenate([scatter_rows(dw[0][:, :edge], fore[::-1]),
                              scatter_rows(dw[0][:, edge:], back[::-1])], axis=1).astype(F32)
        dw = dw.reshape(share, cols // PAIR, 3, PAIR).transpose(2, 0, 1, 3).reshape(3, share, cols)
        for bit in range(count.bit_length() - 1):
            gains = gains + flip(gains, bit)
    reduced = lax.psum_scatter(reduced, "far", scatter_dimension=0, tiled=True)
    input_grad = (x_own + exchange(x_send).astype(F32)).astype(BF16)
    ready = (input_grad, *finish(reduced, hid))
    if parted:
        ready, last = lax.optimization_barrier((ready, last))
        dw, gains = last_sums(sched, *last)
    input_grad, grad_gate, grad_up, grad_down, grad_out = ready
    return (
        output,
        input_grad,
        dw[0],
        dw[1],
        dw[2],
        grad_out,
        grad_gate,
        grad_up,
        grad_down,
        gains[0, :width],
        gains[1, :width],
    )


def solution(mesh):
    count, pair = mesh.shape["dp"], mesh.shape["tensor"]
    near = min(4, count)
    mesh = Mesh(mesh.devices.reshape(count // near, near, pair), DP + ("tensor",))
    split = P(DP, "tensor")
    turned = P("tensor", DP)
    slots = P(DP + ("tensor",), None)
    return jax.shard_map(
        local,
        mesh=mesh,
        in_specs=(slots, split, split, split, turned, split, split, turned, P(), P(),
                  P(DP, None), slots),
        out_specs=(slots, slots, split, split, split, turned, split, split, turned, P(), P()),
        check_vma=False,
    )
```

```python
from functools import partial

import jax
import jax.numpy as jnp
from jax import lax
from jax.experimental import pallas as pl
from jax.experimental.pallas import tpu as pltpu
from jax.sharding import Mesh
from jax.sharding import PartitionSpec as P

HEAD = 64
PAIR = 2 * HEAD
EPS = 1e-05
ROPE_BASE = 10000.0
NEGATIVE = -1e30
F32 = jnp.float32
BF16 = jnp.bfloat16
VMEM_LIMIT = 56 * 1024 * 1024
DP = ("far", "near")
EXTRA = 16
SIDE, TOTAL, BIT_X, BIT_Y, FAR, LOWS = range(6)


def mm(left, right):
    return jnp.dot(left, right, preferred_element_type=F32)


def rdot(left, right):
    return lax.dot_general(left, right, (((1,), (1,)), ((), ())), preferred_element_type=F32)


def tdot(left, right):
    return lax.dot_general(left, right, (((0,), (0,)), ((), ())), preferred_element_type=F32)


def params(limit=VMEM_LIMIT, dims=1):
    return pltpu.CompilerParams(
        vmem_limit_bytes=limit, dimension_semantics=("arbitrary",) * dims
    )


def cost(flops, nbytes, trans=0):
    return pl.CostEstimate(flops=int(flops), bytes_accessed=int(nbytes), transcendentals=int(trans))


def swap_halves(values):
    lane = lax.broadcasted_iota(jnp.int32, values.shape, 1) % HEAD
    half = HEAD // 2
    width = values.shape[1]
    return jnp.where(
        lane < half, pltpu.roll(values, width - half, 1), pltpu.roll(values, half, 1)
    )


def head_masks(values):
    return one_head(values, 0), one_head(values, 1)


def one_head(values, h):
    lane = lax.broadcasted_iota(jnp.int32, (1, PAIR), 1)
    return values * (lane // HEAD == h).astype(values.dtype)


def forward_kernel(sched, own_x_ref, oth_x_ref, wq_ref, wk_ref, wv_ref, cos_ref, sin_ref, start_ref,
                   qkv_ref, oth_ref, own_ref, lse_ref, acc_ref, vt_ref, *, bq, bk, sub, chunk, blocks):
    step = pl.program_id(1)
    half = blocks // 2
    i = lax.rem(step + (1 - sched[0]) * half, blocks)

    @pl.when(step == 0)
    def _():
        local = own_x_ref.shape[0]
        weights = jnp.concatenate([wq_ref[...], wk_ref[...], wv_ref[...]], axis=1)
        for x_ref, side in ((own_x_ref, sched[0]), (oth_x_ref, 1 - sched[0])):
            for r in range(0, local, chunk):
                here = pl.ds(pl.multiple_of(side * local + r, chunk), chunk)
                u = mm(x_ref[r:r + chunk, :], weights)
                cosine, sine = cos_ref[here, :], sin_ref[here, :]
                for n, scale in ((0, HEAD ** -0.5), (1, 1.0)):
                    piece = u[:, n * PAIR:(n + 1) * PAIR]
                    turned = piece * cosine + swap_halves(piece) * sine
                    qkv_ref[here, n * PAIR:(n + 1) * PAIR] = (turned * scale).astype(BF16)
                v = u[:, 2 * PAIR:]
                qkv_ref[here, 2 * PAIR:] = v.astype(BF16)
                vt_ref[:, here] = v.T.astype(BF16)

    start = start_ref[...]
    acc_ref[...] = jnp.zeros_like(acc_ref)
    streams = list(range(0, bq, sub))

    @pl.loop(0, 2)
    def _(h):
        queries = one_head(qkv_ref[pl.ds(pl.multiple_of(i * bq, bq), bq), 0:PAIR], h)
        rows = pl.ds(pl.multiple_of(h * HEAD, HEAD), HEAD)

        def visit(j, carry, last):
            at = pl.multiple_of(i * bq if last else j * bk, bk)
            scores, out = [], []
            for c in streams:
                size = c + sub if last else bk
                s = rdot(qkv_ref[pl.ds(at, size), PAIR:2 * PAIR], queries[c:c + sub])
                key_index = lax.broadcasted_iota(jnp.int32, (size, sub), 0)
                allowed = key_index >= start[:, c:c + sub] - at
                if last:
                    query_index = c + lax.broadcasted_iota(jnp.int32, (size, sub), 1)
                    allowed = allowed & (key_index <= query_index)
                scores.append(jnp.where(allowed, s, NEGATIVE))
            for n, c in enumerate(streams):
                size = c + sub if last else bk
                peak, total = carry[2 * n], carry[2 * n + 1]
                new_peak = jnp.maximum(peak, jnp.max(scores[n], axis=0, keepdims=True))
                fade = jnp.exp(peak - new_peak)
                expo = jnp.exp(scores[n] - new_peak)
                total = total * fade + jnp.sum(expo, axis=0, keepdims=True)
                cols = slice(c, c + sub)
                acc_ref[rows, cols] = acc_ref[rows, cols] * fade + mm(
                    vt_ref[rows, pl.ds(at, size)], expo.astype(BF16)
                )
                out += [new_peak, total]
            return tuple(out)

        carry = (jnp.full((1, sub), NEGATIVE, F32), jnp.zeros((1, sub), F32)) * len(streams)
        carry = lax.fori_loop(sched[LOWS + i], i * (bq // bk), lambda j, c: visit(j, c, False), carry)
        carry = visit(None, carry, True)
        for n, c in enumerate(streams):
            peak, total = carry[2 * n], carry[2 * n + 1]
            cols = slice(c, c + sub)
            acc_ref[rows, cols] = acc_ref[rows, cols] / total
            lse_ref[pl.ds(h, 1), cols] = peak + jnp.log(total)

    mixed = acc_ref[...].T.astype(BF16)

    @pl.when(step < half)
    def _():
        oth_ref[...] = mixed

    @pl.when(step >= half)
    def _():
        own_ref[...] = mixed


def placing(blocks):
    half = blocks // 2

    def place(n, sched):
        return lax.rem(n + (1 - sched[0]) * half, blocks)

    return place, half


def attend_forward(sched, own_x, oth_x, weights, cosine, sine, start, bq, bk, sub=256, chunk=512):
    local, width = own_x.shape
    slots, cols = 2 * local, weights.shape[1] // 3
    pairs, blocks = cols // PAIR, slots // bq
    place, half = placing(blocks)
    rows = pl.BlockSpec((local, width), lambda p, n, s: (0, 0), pipeline_mode=pl.Buffered(1))
    table = pl.BlockSpec((slots, PAIR), lambda p, n, s: (0, 0), pipeline_mode=pl.Buffered(1))
    return pl.pallas_call(
        partial(forward_kernel, bq=bq, bk=bk, sub=sub, chunk=chunk, blocks=blocks),
        grid_spec=pltpu.PrefetchScalarGridSpec(
            num_scalar_prefetch=1,
            grid=(pairs, blocks),
            in_specs=[
                rows, rows,
                *[pl.BlockSpec((width, PAIR), lambda p, n, s, at=at: (0, at + p))
                  for at in (0, pairs, 2 * pairs)],
                table, table,
                pl.BlockSpec((1, bq), lambda p, n, s: (0, place(n, s))),
            ],
            out_specs=[
                pl.BlockSpec((slots, 3 * PAIR), lambda p, n, s: (0, p)),
                pl.BlockSpec((bq, PAIR), lambda p, n, s: (jnp.minimum(n, half - 1), p)),
                pl.BlockSpec((bq, PAIR), lambda p, n, s: (jnp.maximum(n - half, 0), p)),
                pl.BlockSpec((None, 2, bq), lambda p, n, s: (p, 0, place(n, s))),
            ],
            scratch_shapes=[pltpu.VMEM((PAIR, bq), F32), pltpu.VMEM((PAIR, slots), BF16)],
        ),
        out_shape=[
            jax.ShapeDtypeStruct((slots, 3 * cols), BF16),
            jax.ShapeDtypeStruct((local, cols), BF16),
            jax.ShapeDtypeStruct((local, cols), BF16),
            jax.ShapeDtypeStruct((pairs, 2, slots), F32),
        ],
        compiler_params=params(dims=2),
        cost_estimate=cost(4 * slots * slots * cols + 6 * slots * width * cols,
                           16 * slots * cols, slots * slots * 6),
        name="attend_forward",
    )(sched, own_x, oth_x, weights, weights, weights, cosine, sine, start)


def backward_kernel(sched, q_ref, k_ref, v_ref, cos_ref, sin_ref, start_ref, lse_ref,
                    o_oth_ref, o_own_ref, g_oth_ref, g_own_ref, x_own_ref, x_oth_ref,
                    gains_ref, gains_oth_ref, all_ref, *rest, bq, bk, sub, blocks, share):
    step = pl.program_id(1)
    half = blocks // 2
    i = lax.rem(step + (1 - sched[0]) * half, blocks)

    dw_refs, (dq_acc, dkt_acc, dvt_acc) = rest[:-3], rest[-3:]

    @pl.when(step == 0)
    def _():
        dkt_acc[...] = jnp.zeros_like(dkt_acc)
        dvt_acc[...] = jnp.zeros_like(dvt_acc)

    first = step < half
    grads = jnp.where(first, g_oth_ref[...], g_own_ref[...])
    mixed = jnp.where(first, o_oth_ref[...], o_own_ref[...])
    queries = head_masks(q_ref[...])
    couts = head_masks(grads)
    query_t = q_ref[...].astype(F32).T.astype(BF16)
    cout_t = grads.astype(F32).T.astype(BF16)
    begin = jnp.broadcast_to(start_ref[...], (PAIR, bq)).T
    product = grads.astype(F32) * mixed.astype(F32)
    big = product.astype(BF16)
    small = (product - big.astype(F32)).astype(BF16)
    row = lax.broadcasted_iota(jnp.int32, (PAIR, 2 * PAIR), 0)
    lane = lax.broadcasted_iota(jnp.int32, (PAIR, 2 * PAIR), 1)
    pick = jnp.where(row // HEAD == lane // PAIR, 1.0, 0.0).astype(BF16)
    inner = mm(big, pick) + mm(small, pick)
    lse = [jnp.broadcast_to(lse_ref[h:h + 1, :], (PAIR, bq)).T for h in range(2)]
    dq_acc[...] = jnp.zeros_like(dq_acc)

    def wide(value, size):
        return jnp.concatenate([value] * (size // PAIR), axis=1)

    def visit(j, last):
        at = pl.multiple_of(i * bq if last else j * bk, bk)
        streams = [(c, h) for c in range(0, bq, sub) for h in range(2)]

        def scores(n):
            c, h = streams[n]
            size = c + sub if last else bk
            where = pl.ds(at, size)
            rows = slice(c, c + sub)
            return rdot(queries[h][rows], k_ref[where, :]), rdot(couts[h][rows], v_ref[where, :])

        def absorb(n, pair):
            c, h = streams[n]
            raw, d_probs = pair
            size = c + sub if last else bk
            where = pl.ds(at, size)
            rows = slice(c, c + sub)
            lanes = slice(h * HEAD, (h + 1) * HEAD)
            probs = jnp.exp(raw - wide(lse[h][rows], size))
            key_index = lax.broadcasted_iota(jnp.int32, (sub, size), 1)
            allowed = key_index >= wide(begin[rows], size) - at
            if last:
                query_index = c + lax.broadcasted_iota(jnp.int32, (sub, size), 0)
                allowed = allowed & (key_index <= query_index)
            probs = jnp.where(allowed, probs, 0.0)
            d_scores = (probs * (d_probs - wide(inner[rows, h * PAIR:(h + 1) * PAIR], size))).astype(BF16)
            dvt_acc[lanes, where] += mm(cout_t[lanes, rows], probs.astype(BF16))
            dkt_acc[lanes, where] += mm(query_t[lanes, rows], d_scores)
            dq_acc[rows, :] += mm(d_scores, head_masks(k_ref[where, :])[h])

        ready = scores(0)
        for n in range(len(streams)):
            held = ready
            if n + 1 < len(streams):
                ready = scores(n + 1)
            absorb(n, held)

    @pl.loop(sched[LOWS + blocks + i], i * (bq // bk))
    def _(j):
        visit(j, False)

    visit(None, True)

    def unrotate(g, cosine, sine):
        return g * cosine - swap_halves(g) * sine

    here = pl.ds(pl.multiple_of(i * bq, bq), bq)
    dq = unrotate(dq_acc[...] * (HEAD ** -0.5), cos_ref[here, :], sin_ref[here, :])
    all_ref[here, 0:PAIR] = dq.astype(BF16)

    @pl.when(step == blocks - 1)
    def _():
        dk = unrotate(dkt_acc[...].T, cos_ref[...], sin_ref[...])
        all_ref[:, PAIR:2 * PAIR] = dk.astype(BF16)
        all_ref[:, 2 * PAIR:] = dvt_acc[...].T.astype(BF16)
        local = x_own_ref.shape[0]
        mine = pl.ds(pl.multiple_of(sched[0] * local, local), local)
        other = pl.ds(pl.multiple_of((1 - sched[0]) * local, local), local)
        total = (tdot(x_own_ref[...], all_ref[mine, :])
                 + tdot(x_oth_ref[...], all_ref[other, :])).astype(BF16)
        if share is None:
            dw_refs[0][...] = total
        else:
            gains = gains_ref[0:2, :] + gains_oth_ref[0:2, :]
            part_rows(total, gains, sched[BIT_X], sched[BIT_Y], *dw_refs, share)


def encode(value):
    high = value.astype(BF16)
    rest = value - high.astype(F32)
    middle = rest.astype(BF16)
    low = (rest - middle.astype(F32)).astype(BF16)
    rows, cols = value.shape
    pieces = [piece.astype(F32) for piece in (high, middle, low)]
    return jnp.concatenate(pieces + [jnp.zeros((EXTRA - 3 * rows, cols), F32)], axis=0).astype(BF16)


def decode(rows, count=2):
    wide = rows.astype(F32)
    return wide[0:count] + wide[count:2 * count] + wide[2 * count:3 * count]


def part_rows(total, gains, bit_x, bit_y, keep_a, send_a, keep_b, send_b, share):
    def block(z, y, x):
        at = (4 * z + 2 * y + x) * share
        return total[at:at + share]

    pieces = keep_a.shape[0] // share
    for n in range(pieces):
        z, side, here = 2 * (n // 2), n % 2, slice(n * share, (n + 1) * share)
        zero, one = block(z, side, 0), block(z, side, 1)
        keep_a[here] = jnp.where(bit_x == 0, zero, one)
        send_a[here] = jnp.where(bit_x == 0, one, zero)
        zero, one = block(z + 1, 0, side), block(z + 1, 1, side)
        keep_b[here] = jnp.where(bit_y == 0, zero, one)
        send_b[here] = jnp.where(bit_y == 0, one, zero)
    send_a[pieces * share:] = encode(gains)


def attend_backward(sched, qkv, cosine, sine, start, lse, o_oth, o_own, g_oth, g_own, x_own, x_oth,
                    gains, gains_oth, bq, bk, share, sub=256):
    slots, cols = qkv.shape[0], qkv.shape[1] // 3
    pairs, blocks = cols // PAIR, slots // bq
    local, width = x_own.shape
    place, half = placing(blocks)
    table = pl.BlockSpec((slots, PAIR), lambda p, n, s: (0, 0), pipeline_mode=pl.Buffered(1))
    rows = pl.BlockSpec((local, width), lambda p, n, s: (0, 0), pipeline_mode=pl.Buffered(1))
    oth = pl.BlockSpec((bq, PAIR), lambda p, n, s: (jnp.minimum(n, half - 1), p))
    own = pl.BlockSpec((bq, PAIR), lambda p, n, s: (jnp.maximum(n - half, 0), p))
    if share is None:
        dw_specs = [pl.BlockSpec((width, 3 * PAIR), lambda p, n, s: (0, p))]
        dw_shapes = [(width, 3 * cols)]
    else:
        rows_out = [width // 4, width // 4 + EXTRA, width // 4, width // 4]
        dw_specs = [pl.BlockSpec((size, 3 * PAIR), lambda p, n, s: (0, p)) for size in rows_out]
        dw_shapes = [(size, 3 * cols) for size in rows_out]
    return pl.pallas_call(
        partial(backward_kernel, bq=bq, bk=bk, sub=sub, blocks=blocks, share=share),
        grid_spec=pltpu.PrefetchScalarGridSpec(
            num_scalar_prefetch=1,
            grid=(pairs, blocks),
            in_specs=[
                pl.BlockSpec((bq, PAIR), lambda p, n, s: (place(n, s), 3 * p)),
                pl.BlockSpec((slots, PAIR), lambda p, n, s: (0, 3 * p + 1)),
                pl.BlockSpec((slots, PAIR), lambda p, n, s: (0, 3 * p + 2)),
                table, table,
                pl.BlockSpec((1, bq), lambda p, n, s: (0, place(n, s))),
                pl.BlockSpec((None, 2, bq), lambda p, n, s: (p, 0, place(n, s))),
                oth, own, oth, own, rows, rows,
                pl.BlockSpec((8, 3 * PAIR), lambda p, n, s: (0, p)),
                pl.BlockSpec((8, 3 * PAIR), lambda p, n, s: (0, p)),
            ],
            out_specs=[pl.BlockSpec((slots, 3 * PAIR), lambda p, n, s: (0, p)), *dw_specs],
            scratch_shapes=[
                pltpu.VMEM((bq, PAIR), F32),
                pltpu.VMEM((PAIR, slots), F32),
                pltpu.VMEM((PAIR, slots), F32),
            ],
        ),
        out_shape=[jax.ShapeDtypeStruct(shape, BF16) for shape in [(slots, 3 * cols), *dw_shapes]],
        compiler_params=params(dims=2),
        cost_estimate=cost(10 * slots * slots * cols + 6 * slots * width * cols,
                           20 * slots * cols, slots * slots * 6),
        name="attend_backward",
    )(sched, qkv, qkv, qkv, cosine, sine, start, lse, o_oth, o_own, g_oth, g_own, x_own, x_oth,
      gains, gains_oth)


def feed_kernel(sched, x_ref, own_ref, oth_ref, dy_ref, w_hbm, ga_ref, gf_ref,
                out_ref, dfirst_ref, gown_ref, goth_ref, grads_ref, gains_ref,
                right_hbm, left_hbm, dattn_hbm,
                w_ref, keep_a, keep_b, total_s, right_s, left_s, dattn_s, mixed_s,
                sems, *, block, sub, chunk, local, hid, head_cols, parts, share):
    step = pl.program_id(0)
    me = sched[0]
    steps = local // block
    outs = slice(3 * hid, 3 * hid + head_cols)
    pieces = [(slice(3 * hid, w_ref.shape[2]), None), (slice(0, 2 * hid), 0), (slice(0, 2 * hid), 1),
              (slice(2 * hid, 3 * hid), None)]

    def piece(n):
        cols, t = pieces[n]
        at = (slice(None), slice(None), cols) if t is None else (t, slice(None), cols)
        return pltpu.make_async_copy(w_hbm.at[at], w_ref.at[at], sems.at[n])

    @pl.when(step == 0)
    def _():
        for n in range(len(pieces)):
            piece(n).start()
        gains_ref[...] = jnp.zeros_like(gains_ref)

    def arrive(n):
        @pl.when(step == 0)
        def _():
            piece(n).wait()

    @pl.when(step < steps)
    def _():
        subs = list(range(0, block, sub))
        base = pl.multiple_of(step * block, block)
        arrive(0)
        attn, rms1, unit1, normed, normed_b = {}, {}, {}, {}, {}
        for r in subs:
            rows = slice(r, r + sub)
            attn[r] = rdot(own_ref[rows, :], w_ref[me, :, outs]) + rdot(oth_ref[rows, :], w_ref[1 - me, :, outs])
        for r in subs:
            rows = slice(r, r + sub)
            here = pl.ds(base + r, sub)
            first = x_ref[rows, :].astype(F32) + attn[r]
            rms1[r] = lax.rsqrt(jnp.mean(first * first, axis=-1, keepdims=True) + EPS)
            unit1[r] = first * rms1[r]
            normed[r] = unit1[r] * ga_ref[...]
            normed_b[r] = normed[r].astype(BF16)
            left_s[0, here, :] = normed_b[r]
            mixed_s[here, :] = oth_ref[rows, :]
        total_s[...] = jnp.zeros_like(total_s)

        @pl.loop(0, 2)
        def _(t):
            for at, count in ((0, 1), (0, 3), (1, 2)):
                @pl.when((step == 0) & (t == at))
                def _():
                    piece(count).wait()

            for c in range(0, hid, chunk):
                cols = pl.ds(pl.multiple_of(t * hid + c, chunk), chunk)
                hid_b = {}
                for r in subs:
                    rows = slice(r, r + sub)
                    gate = mm(normed_b[r], w_ref[t, :, c:c + chunk])
                    upper = mm(normed_b[r], w_ref[t, :, hid + c:hid + c + chunk])
                    sigma = 1.0 / (1.0 + jnp.exp(-gate))
                    silu = gate * sigma
                    hid_b[r] = (silu * upper).astype(BF16)
                    keep_a[rows, cols] = silu
                    keep_b[rows, cols] = upper * (sigma + silu * (1.0 - sigma))
                    right_s[2, pl.ds(base + r, sub), cols] = hid_b[r]
                for r in subs:
                    total_s[r:r + sub, :] += rdot(hid_b[r], w_ref[t, :, 2 * hid + c:2 * hid + c + chunk])

        d_second, d_ffn = {}, {}
        for r in subs:
            rows = slice(r, r + sub)
            here = pl.ds(base + r, sub)
            second = normed[r] + total_s[rows, :]
            rms2 = lax.rsqrt(jnp.mean(second * second, axis=-1, keepdims=True) + EPS)
            unit2 = second * rms2
            slot = me * local + base + r + lax.broadcasted_iota(jnp.int32, (sub, 1), 0)
            valid = slot < sched[1]
            out_ref[rows, :] = jnp.where(valid, unit2 * gf_ref[...], 0.0).astype(BF16)
            dy = jnp.where(valid, dy_ref[rows, :].astype(F32), 0.0)
            gains_ref[1:2, 0:dy.shape[1]] += jnp.sum(dy * unit2, axis=0, keepdims=True)
            scaled = dy * gf_ref[...]
            d_second[r] = rms2 * (scaled - unit2 * jnp.mean(scaled * unit2, axis=-1, keepdims=True))
            d_ffn[r] = d_second[r].astype(BF16)
            left_s[1, here, :] = d_ffn[r]
            total_s[rows, :] = d_second[r]

        @pl.loop(0, 2)
        def _(t):
            for c in range(0, hid, chunk):
                cols = pl.ds(pl.multiple_of(t * hid + c, chunk), chunk)
                dg, du = {}, {}
                for r in subs:
                    rows, here = slice(r, r + sub), pl.ds(base + r, sub)
                    d_hidden = mm(d_ffn[r], w_ref[t, :, 2 * hid + c:2 * hid + c + chunk])
                    dg[r] = (d_hidden * keep_b[rows, cols]).astype(BF16)
                    du[r] = (d_hidden * keep_a[rows, cols]).astype(BF16)
                    right_s[0, here, cols] = dg[r]
                    right_s[1, here, cols] = du[r]
                for r in subs:
                    total_s[r:r + sub, :] += rdot(dg[r], w_ref[t, :, c:c + chunk]) + rdot(
                        du[r], w_ref[t, :, hid + c:hid + c + chunk])

        for r in subs:
            rows = slice(r, r + sub)
            here = pl.ds(base + r, sub)
            d_normed = total_s[rows, :]
            gains_ref[0:1, 0:d_normed.shape[1]] += jnp.sum(d_normed * unit1[r], axis=0, keepdims=True)
            scaled = d_normed * ga_ref[...]
            d_first = rms1[r] * (scaled - unit1[r] * jnp.mean(scaled * unit1[r], axis=-1, keepdims=True))
            dfirst_ref[rows, :] = d_first
            d_attn = d_first.astype(BF16)
            dattn_s[here, :] = d_attn
            gown_ref[rows, :] = mm(d_attn, w_ref[me, :, outs]).astype(BF16)
            goth_ref[rows, :] = mm(d_attn, w_ref[1 - me, :, outs]).astype(BF16)

    mine = pl.ds(pl.multiple_of(me * hid, hid), hid)
    outgoing = [
        pltpu.make_async_copy(right_s.at[:, :, mine], right_hbm, sems.at[len(pieces)]),
        pltpu.make_async_copy(left_s, left_hbm, sems.at[len(pieces) + 1]),
        pltpu.make_async_copy(dattn_s, dattn_hbm, sems.at[len(pieces) + 2]),
    ]

    @pl.when(step == steps)
    def _():
        for copy in outgoing:
            copy.start()

    @pl.when(step >= steps)
    def _():
        size = dattn_s.shape[1] // parts
        rows = pl.ds(pl.multiple_of((step - steps) * size, size), size)
        cols = pl.ds(pl.multiple_of((1 - me) * hid, hid), hid)
        for n in range(3):
            left = left_s[n // 2, :, rows]
            store_rows(grads_ref, tdot(left, right_s[n, :, cols]), slice(n * hid, (n + 1) * hid), share)
        store_rows(grads_ref, tdot(dattn_s[:, rows], mixed_s[...]),
                   slice(3 * hid, 3 * hid + head_cols), share)

    @pl.when(step == steps + parts - 1)
    def _():
        for copy in outgoing:
            copy.wait()


def store_rows(ref, value, cols, share, part=0):
    value = value.astype(BF16)
    rows = value.shape[0]
    if share is None:
        ref[pl.ds(pl.multiple_of(part * rows, rows), rows), cols] = value
    else:
        near = ref.shape[0]
        for n in range(rows // share):
            far = part * (rows // (share * near)) + n // near
            ref[n % near, far, :, cols] = value[n * share:(n + 1) * share]


def own_grads_kernel(left_ref, right_ref, dattn_ref, mixed_ref, out_ref, *, tiles, share):
    step = pl.program_id(0)

    size = left_ref.shape[1] // 2

    @pl.loop(0, 2)
    def _(part):
        rows = pl.ds(pl.multiple_of(part * size, size), size)

        @pl.when(step < tiles)
        def _():
            store_rows(out_ref, tdot(left_ref[:, rows], right_ref[...]), slice(None), share, part)

        @pl.when(step == tiles)
        def _():
            store_rows(out_ref, tdot(dattn_ref[:, rows], mixed_ref[...]),
                       slice(0, mixed_ref.shape[1]), share, part)


def own_grads(left, right, d_attn, mixed, share, near, tile=512):
    _, local, width = left.shape
    hid, head_cols = right.shape[2], mixed.shape[1]
    each = hid // tile
    tiles = 3 * each
    total = 3 * hid + head_cols
    packed = share % 16 == 0
    if packed:
        shape = (near, width // (near * share), share)
        out_spec = pl.BlockSpec((*shape, tile), lambda n: (0, 0, 0, n))
    else:
        shape = (width,)
        out_spec = pl.BlockSpec((width, tile), lambda n: (0, n))

    def kind(n):
        return jnp.minimum(lax.div(n, each), 2)

    grads = pl.pallas_call(
        partial(own_grads_kernel, tiles=tiles, share=share if packed else None),
        grid=(tiles + 1,),
        in_specs=[
            pl.BlockSpec((None, local, width), lambda n: (lax.div(kind(n), 2), 0, 0)),
            pl.BlockSpec((None, local, tile), lambda n: (kind(n), 0, lax.rem(jnp.minimum(n, tiles - 1), each))),
            pl.BlockSpec((local, width), lambda n: (0, 0)),
            pl.BlockSpec((local, head_cols), lambda n: (0, 0)),
        ],
        out_specs=out_spec,
        out_shape=jax.ShapeDtypeStruct((*shape, total), BF16),
        compiler_params=params(48 * 1024 * 1024),
        cost_estimate=cost(2 * local * width * total, 2 * local * (4 * width + 3 * hid)),
        name="own_grads",
    )(*[pltpu.with_memory_space_constraint(value, pltpu.HBM) for value in (left, right, d_attn, mixed)])
    return by_near(grads, share, near)


def by_near(grads, share, near):
    total = grads.shape[-1]
    if share % 16:
        grads = grads.reshape(-1, near, share, total).swapaxes(0, 1)
    return grads.reshape(-1, total)


def feed(sched, x, own, oth, dy, weights, gain_attn, gain_ffn, hid, share, near,
         block=512, sub=256, chunk=512, parts=2):
    local, width = x.shape
    head_cols = own.shape[1]
    total = weights.shape[2]
    steps = local // block
    packed = share % 16 == 0

    def at(s):
        return jnp.minimum(s, steps - 1)

    rows = pl.BlockSpec((block, width), lambda s, sched: (at(s), 0))
    heads = pl.BlockSpec((block, head_cols), lambda s, sched: (at(s), 0))
    gain = pl.BlockSpec((1, width), lambda s, sched: (0, 0))

    def tile(s, sched):
        n = jnp.maximum(s - steps, 0)
        return (0, n, 0, 0) if packed else (n, 0)

    if packed:
        grads_shape = (near, width // (near * share), share, total)
        grads_block = (near, width // (near * share * parts), share, total)
    else:
        grads_shape, grads_block = (width, total), (width // parts, total)

    def shape(cols, dtype):
        return jax.ShapeDtypeStruct((local, cols), dtype)

    results = pl.pallas_call(
        partial(feed_kernel, block=block, sub=sub, chunk=chunk, local=local, hid=hid,
                head_cols=head_cols, parts=parts, share=share if packed else None),
        grid_spec=pltpu.PrefetchScalarGridSpec(
            num_scalar_prefetch=1,
            grid=(steps + parts,),
            in_specs=[rows, heads, heads, rows, pl.BlockSpec(memory_space=pl.ANY), gain, gain],
            out_specs=[rows, rows, heads, heads,
                       pl.BlockSpec(grads_block, tile),
                       pl.BlockSpec((8, 3 * head_cols), lambda s, sched: (0, 0))]
            + [pl.BlockSpec(memory_space=pl.ANY)] * 3,
            scratch_shapes=[pltpu.VMEM(weights.shape, BF16)]
            + [pltpu.VMEM((block, 2 * hid), F32)] * 2
            + [pltpu.VMEM((block, width), F32)]
            + [pltpu.VMEM((3, local, 2 * hid), BF16), pltpu.VMEM((2, local, width), BF16)]
            + [pltpu.VMEM((local, width), BF16)]
            + [pltpu.VMEM((local, head_cols), BF16), pltpu.SemaphoreType.DMA((7,))],
        ),
        out_shape=[
            shape(width, BF16), shape(width, F32), shape(head_cols, BF16), shape(head_cols, BF16),
            jax.ShapeDtypeStruct(grads_shape, BF16),
            jax.ShapeDtypeStruct((8, 3 * head_cols), F32),
            jax.ShapeDtypeStruct((3, local, hid), BF16),
            jax.ShapeDtypeStruct((2, local, width), BF16),
            shape(width, BF16),
        ],
        compiler_params=params(60 * 1024 * 1024),
        cost_estimate=cost(12 * local * width * total, 30 * local * width),
        name="feed",
    )(sched, x, own, oth, dy, weights, gain_attn, gain_ffn)
    return (*results[:4], by_near(results[4], share, near), *results[5:])


def input_grad_kernel(sched, d_ref, w_ref, dfirst_ref, oth_ref, own_ref, *, half):
    step = pl.program_id(0)
    cols = d_ref.shape[1]
    order = [at + n * PAIR for n in range(3) for at in range(0, cols, 3 * PAIR)]
    part = rdot(jnp.concatenate([d_ref[:, at:at + PAIR] for at in order], axis=1), w_ref[...])

    @pl.when(step < half)
    def _():
        oth_ref[...] = part.astype(BF16)

    @pl.when(step >= half)
    def _():
        own_ref[...] = dfirst_ref[...] + part


def input_grads(sched, d_qkv, weights, d_first, block):
    local, width = d_first.shape
    cols = d_qkv.shape[1]
    half = local // block
    place, _ = placing(2 * half)
    own = pl.BlockSpec((block, width), lambda n, s: (jnp.maximum(n - half, 0), 0))
    return pl.pallas_call(
        partial(input_grad_kernel, half=half),
        grid_spec=pltpu.PrefetchScalarGridSpec(
            num_scalar_prefetch=1,
            grid=(2 * half,),
            in_specs=[pl.BlockSpec((block, cols), lambda n, s: (place(n, s), 0)),
                      pl.BlockSpec((width, cols), lambda n, s: (0, 0)), own],
            out_specs=[pl.BlockSpec((block, width), lambda n, s: (jnp.minimum(n, half - 1), 0)), own],
        ),
        out_shape=[jax.ShapeDtypeStruct((local, width), BF16),
                   jax.ShapeDtypeStruct((local, width), F32)],
        compiler_params=params(),
        cost_estimate=cost(4 * local * width * cols, 4 * local * (width + cols)),
        name="input_grads",
    )(sched, d_qkv, weights, d_first)


def add_kernel(left_ref, right_ref, out_ref):
    out_ref[...] = add(left_ref[...], right_ref[...]).astype(BF16)


def add_rows(left, right, parts=4):
    rows, cols = left.shape
    spec = pl.BlockSpec((rows // parts, cols), lambda n: (n, 0))
    return pl.pallas_call(
        add_kernel,
        grid=(parts,),
        in_specs=[spec, spec],
        out_specs=spec,
        out_shape=jax.ShapeDtypeStruct(left.shape, BF16),
        compiler_params=params(),
        cost_estimate=cost(rows * cols, 8 * rows * cols),
        name="add_rows",
    )(left, right)


def finish_kernel(total_ref, gate_ref, up_ref, down_ref, out_ref):
    hid = gate_ref.shape[1]
    gate_ref[...] = total_ref[:, 0:hid].astype(F32)
    up_ref[...] = total_ref[:, hid:2 * hid].astype(F32)
    down_ref[...] = total_ref[:, 2 * hid:3 * hid].astype(F32)
    out_ref[...] = total_ref[:, 3 * hid:].astype(F32)


def finish(total, hid):
    share, cols = total.shape
    gate, up, down, out = pl.pallas_call(
        finish_kernel,
        out_shape=[jax.ShapeDtypeStruct((share, width), F32)
                   for width in (hid, hid, hid, cols - 3 * hid)],
        cost_estimate=cost(0, 6 * share * cols),
        name="finish",
    )(total)
    return gate, up, down.T, out.T


def whole_call(kernel, name, sched, values, shapes):
    whole = pl.BlockSpec(memory_space=pltpu.VMEM)
    size = 4 * sum(value.size for value in values)
    return pl.pallas_call(
        kernel,
        in_specs=[pl.BlockSpec(memory_space=pltpu.SMEM)] + [whole] * len(values),
        out_specs=[whole] * len(shapes),
        out_shape=[jax.ShapeDtypeStruct(shape, dtype) for shape, dtype in shapes],
        compiler_params=pltpu.CompilerParams(vmem_limit_bytes=32 * 1024 * 1024),
        cost_estimate=cost(0, size),
        name=name,
    )(sched, *values)


def add(left, right):
    return left.astype(F32) + right.astype(F32)


def near_kernel(sched, keep_a, got_a, keep_b, got_b, gains, gains_oth, next_a, send_a, next_b, send_b, total,
                *, share):
    size = next_a.shape[0]
    for held, got, bit, stay, go in ((keep_a, got_a, sched[BIT_Y], next_a, send_a),
                                     (keep_b, got_b, sched[BIT_X], next_b, send_b)):
        for n in range(size // share):
            here = slice(n * share, (n + 1) * share)
            mine = pl.ds(pl.multiple_of((2 * n + bit) * share, share), share)
            other = pl.ds(pl.multiple_of((2 * n + 1 - bit) * share, share), share)
            stay[here] = add(held[mine], got[mine]).astype(BF16)
            go[here] = add(held[other], got[other]).astype(BF16)
    total[...] = gains[0:2, :] + gains_oth[0:2, :] + decode(got_a[2 * size:])
    send_a[size:] = encode(total[...])


def far_kernel(sched, keep_a, got_a, keep_b, got_b, gains, own, total, *sends):
    far, share = 1 + len(sends), own.shape[0]
    sums = []
    for n in range(far // 2):
        here = slice(n * share, (n + 1) * share)
        sums += [add(keep_a[here], got_a[here]), add(keep_b[here], got_b[here])]
    total[...] = gains[...] + decode(got_a[keep_a.shape[0]:])
    for shift in range(far):
        at = lax.rem(sched[FAR] + shift, far)
        value = sums[0]
        for n in range(1, far):
            value = jnp.where(at == n, sums[n], value)
        if shift == 0:
            own[...] = value
        else:
            sends[shift - 1][:share] = value.astype(BF16)
            sends[shift - 1][share:] = encode(total[...])


def last_kernel(sched, own, gains, *rest):
    got, outs, totals = rest[:-5], rest[-5:-2], rest[-2:]
    value, share, far = own[...], own.shape[0], 1 + len(got)
    arrived = [gains[...]]
    for piece in got:
        value = value + piece[:share].astype(F32)
        arrived.append(decode(piece[share:]))
    for at in range(0, value.shape[1], PAIR):
        pair, part = at // PAIR // 3, at // PAIR % 3
        outs[part][:, pair * PAIR:(pair + 1) * PAIR] = value[:, at:at + PAIR]
    summed = None
    for n in range(far):
        shift = lax.rem(sched[FAR] - n + far, far)
        term = arrived[0]
        for k in range(1, far):
            term = jnp.where(shift == k, arrived[k], term)
        summed = term if summed is None else summed + term
    for row, total in enumerate(totals):
        total[...] = summed[row, :total.shape[0]]


def shifted(value, shift):
    far = lax.axis_size("far")
    return lax.ppermute(value, "far", [(at, (at + shift) % far) for at in range(far)])


def sum_parts(sched, share, keep_a, send_a, keep_b, send_b, gains, gains_oth, meanwhile):
    size, width = keep_a.shape
    far = lax.axis_size("far")
    got_a, got_b = flip(send_a, 0), flip(send_b, 1)
    beside = meanwhile()
    got_a, got_b, beside = lax.optimization_barrier((got_a, got_b, beside))
    sizes = [size // 2, size // 2 + EXTRA, size // 2, size // 2]
    keep_a, send_a, keep_b, send_b, gains = whole_call(
        partial(near_kernel, share=share), "near_sums", sched,
        (keep_a, got_a, keep_b, got_b, gains, gains_oth),
        [((rows, width), BF16) for rows in sizes] + [((2, width), F32)])
    got_a, got_b = flip(send_a, 1), flip(send_b, 0)
    own, gains, *sends = whole_call(
        far_kernel, "far_sums", sched, (keep_a, got_a, keep_b, got_b, gains),
        [((share, width), F32), (gains.shape, F32)] + [((share + EXTRA, width), BF16)] * (far - 1))
    got = [shifted(value, shift + 1) for shift, value in enumerate(sends)]
    return (own, gains, *got), beside


def last_sums(sched, own, gains, *got, features):
    share, width = own.shape
    *dw, gain_attn, gain_ffn = whole_call(
        last_kernel, "last_sums", sched, (own, gains, *got),
        [((share, width // 3), F32)] * 3 + [((features,), F32)] * 2)
    return dw, (gain_attn, gain_ffn)


def exchange(value):
    return lax.ppermute(value, "tensor", [(0, 1), (1, 0)])


def flip(value, bit):
    count = lax.axis_size(DP)
    return lax.ppermute(value, DP, [(at, at ^ (1 << bit)) for at in range(count)])


def bit_orders(count):
    bits = count.bit_length() - 1
    low = list(range(min(2, bits)))
    high = list(range(min(2, bits), bits))
    return high[::-1] + low, high[::-1] + low[::-1]


def join(held, bit):
    other = flip(held, bit)
    mine = ((lax.axis_index(DP) >> bit) & 1) == 0
    return jnp.stack([jnp.where(mine, held, other), jnp.where(mine, other, held)])


def in_order(held, order):
    bits = len(order)
    rows, cols = held.shape[-2:]
    held = held.reshape((2,) * bits + (rows, cols))
    axes = [bits - 1 - order.index(bit) for bit in range(bits - 1, -1, -1)]
    return held.transpose(*axes, bits, bits + 1).reshape(-1, cols)


def gather_rows(piece, edge):
    fore, back = bit_orders(lax.axis_size(DP))
    high = len(fore) - min(2, len(fore))
    held = piece[None]
    for bit in fore[:high]:
        held = join(held, bit)
    parts = [held[..., :edge], held[..., edge:]]
    for one, two in zip(fore[high:], back[high:]):
        parts = [join(parts[0], one), join(parts[1], two)]
    return jnp.concatenate([in_order(parts[0], fore), in_order(parts[1], back)], axis=1)


def scatter_rows(total, order):
    me = lax.axis_index(DP)
    bits = len(order)
    rows, cols = total.shape[0] >> bits, total.shape[1]
    held = total.reshape((2,) * bits + (rows, cols))
    left = list(range(bits - 1, -1, -1))
    for bit in order:
        axis = left.index(bit)
        left.pop(axis)
        low = lax.index_in_dim(held, 0, axis, keepdims=False)
        high = lax.index_in_dim(held, 1, axis, keepdims=False)
        mine = ((me >> bit) & 1) == 0
        got = flip(jnp.where(mine, high, low), bit)
        held = (jnp.where(mine, low, high).astype(F32) + got.astype(F32)).astype(BF16)
    return held.reshape(rows, cols)


def local(tokens, w_query, w_key, w_value, w_out, w_gate, w_up, w_down, gain_attn, gain_ffn,
          lengths, cotangent):
    rows, width = tokens.shape
    slots = 2 * rows
    me = lax.axis_index("tensor")
    count = lax.axis_size(DP)
    cols, hid = w_query.shape[1], w_gate.shape[1]
    share = width // count
    edge = 5 * cols // 3
    bq, bk = rows, rows // 2
    blocks = slots // bq

    packed = jnp.concatenate([w_gate, w_up, w_down.T, w_out.T], axis=1)
    feed_w = lax.all_gather(packed, ("tensor",) + DP, axis=0, tiled=True)
    feed_w = feed_w.reshape(2, width, packed.shape[1])
    full_qkv = gather_rows(jnp.concatenate([w_query, w_key, w_value], axis=1), edge)
    other_x = exchange(tokens)

    near_at = lax.axis_index("near")
    index = jnp.arange(slots, dtype=jnp.int32)
    row = lengths[0]
    ends = jnp.cumsum(row)
    begins = jnp.sum(jnp.where(index[:, None] >= ends[None, :], row[None, :], 0), axis=1)
    position = (index - begins).astype(F32)
    lane = jnp.arange(PAIR, dtype=jnp.int32) % HEAD
    inverse = ROPE_BASE ** (-((lane % (HEAD // 2)).astype(F32) * 2.0 / HEAD))
    angle = position[:, None] * inverse[None, :]
    cosine = jnp.cos(angle)
    sine = jnp.where(lane[None, :] < HEAD // 2, -jnp.sin(angle), jnp.sin(angle))
    sched = jnp.concatenate([
        jnp.stack([me, ends[-1], near_at % 2, near_at // 2, lax.axis_index("far")]).astype(jnp.int32),
        begins[::bq] // bk,
        begins[::bq] // (bk // 2),
    ])
    start = begins.reshape(1, slots)

    qkv, mixed_send, mixed_own, lse = attend_forward(
        sched, tokens, other_x, full_qkv, cosine, sine, start, bq, bk)
    mixed_oth = exchange(mixed_send)
    output, d_first, g_own, g_send, grads, gains, right, left, d_attn = feed(
        sched, tokens, mixed_own, mixed_oth, cotangent, feed_w, gain_attn.reshape(1, width),
        gain_ffn.reshape(1, width), hid, share, lax.axis_size("near"))
    g_oth = exchange(g_send)
    other_grads = exchange(grads)
    grads = own_grads(left, right, d_attn, mixed_own, share, lax.axis_size("near"))
    grads = (grads.astype(F32) + other_grads.astype(F32)).astype(BF16)
    gains_oth = exchange(gains)
    grads, g_oth, gains_oth = lax.optimization_barrier((grads, g_oth, gains_oth))
    reduced = lax.psum_scatter(grads, "near", scatter_dimension=0, tiled=True)
    parted = share % 16 == 0 and lax.axis_size("near") == 4 and lax.axis_size("far") % 2 == 0
    d_qkv, *dw = attend_backward(sched, qkv, cosine, sine, start, lse, mixed_send, mixed_own,
                                 g_oth, g_own, tokens, other_x, gains, gains_oth, bq, bk // 2,
                                 share if parted else None)
    d_qkv, reduced, *dw = lax.optimization_barrier((d_qkv, reduced, *dw))
    into_input = partial(input_grads, sched, d_qkv, full_qkv, d_first, 512)
    if parted:
        last, (x_send, x_own) = sum_parts(sched, share, *dw, gains, gains_oth, into_input)
    else:
        x_send, x_own = into_input()
        fore, back = bit_orders(count)
        dw = jnp.concatenate([scatter_rows(dw[0][:, :edge], fore[::-1]),
                              scatter_rows(dw[0][:, edge:], back[::-1])], axis=1).astype(F32)
        dw = dw.reshape(share, cols // PAIR, 3, PAIR).transpose(2, 0, 1, 3).reshape(3, share, cols)
        gains = gains + gains_oth
        for bit in range(count.bit_length() - 1):
            gains = gains + flip(gains, bit)
        gains = gains[0, :width], gains[1, :width]
    reduced = lax.psum_scatter(reduced, "far", scatter_dimension=0, tiled=True)
    input_grad = add_rows(x_own, exchange(x_send))
    ready = (input_grad, *finish(reduced, hid))
    if parted:
        ready, last = lax.optimization_barrier((ready, last))
        dw, gains = last_sums(sched, *last, features=width)
    input_grad, grad_gate, grad_up, grad_down, grad_out = ready
    return (
        output,
        input_grad,
        dw[0],
        dw[1],
        dw[2],
        grad_out,
        grad_gate,
        grad_up,
        grad_down,
        *gains,
    )


def solution(mesh):
    count, pair = mesh.shape["dp"], mesh.shape["tensor"]
    near = min(4, count)
    mesh = Mesh(mesh.devices.reshape(count // near, near, pair), DP + ("tensor",))
    split = P(DP, "tensor")
    turned = P("tensor", DP)
    slots = P(DP + ("tensor",), None)
    return jax.shard_map(
        local,
        mesh=mesh,
        in_specs=(slots, split, split, split, turned, split, split, turned, P(), P(),
                  P(DP, None), slots),
        out_specs=(slots, slots, split, split, split, turned, split, split, turned, P(), P()),
        check_vma=False,
    )
```
